32 devices in a mesh: tm: 16 (over z, x, core), space: 2 (over y).
Axes of the slice: x: 2, y: 2, z: 4, core: 2. Of those that a mesh axis runs over, the one named last changes fastest.
Arguments:
- conv_input: bfloat16 [16, 12, 40, 256], P('tm', None, 'space'), may hold values from -6 to 6
- conv_out: bfloat16 [16, 12, 40, 256], P('tm', None, 'space'), may hold values from -20 to 20
- kernel: bfloat16 [3, 3, 3, 256, 256], replicated, may hold values from -0.078125 to 0.078125
- gain: float32 [256], replicated, may hold values from 0.25 to 1.75
- bias: float32 [256], replicated, may hold values from -4 to 4
- cotangent: bfloat16 [16, 12, 40, 256], P('tm', None, 'space'), may hold values from -7 to 7
Outputs:
- grad_input: bfloat16 [16, 12, 40, 256], P('tm', None, 'space')
- grad_kernel: float32 [3, 3, 3, 256, 256], P(None, None, None, None, 'space')
- grad_gain: float32 [256], replicated
- grad_bias: float32 [256], replicated
The draws below stay inside these ranges and needn't reach their ends.
All inputs are finite; a program needn't handle non-finite values.
Results may differ from the reference program's by a relative error of at most 0.0075.
Values may be sent and summed in bfloat16 or wider, within the bound.
A program may use at most 64 MiB of HBM per device.

```python
import jax
import jax.numpy as jnp
from jax import lax

CH = 256
GROUPS = 32
ROWS = 12
COLS = 20
FRAMES = 16
WIDTH = 40


def ordered_levels(key, count, low, high):
    order = jax.random.permutation(key, count).astype(jnp.float32)
    return low + (high - low) * order / max(count - 1, 1)


def draw_conv_out(key, part):
    keys = jax.random.split(jax.random.fold_in(key, 7), 6)
    shape = (FRAMES, ROWS, WIDTH, CH)
    base = jnp.clip(jax.random.normal(keys[0], shape, jnp.float32), -3.5, 3.5)
    frame_scale = ordered_levels(keys[1], FRAMES, 0.6, 1.8)
    frame_offset = jax.random.uniform(keys[2], (FRAMES,), jnp.float32, -0.5, 0.5)
    strips = WIDTH // COLS
    strip_scale = jnp.exp(ordered_levels(keys[3], strips, -0.35, 0.35))
    column_scale = strip_scale[jnp.arange(WIDTH) // COLS]
    scales = jnp.exp(jax.random.uniform(keys[4], (CH,), jnp.float32, -0.6, 0.6))
    offsets = jnp.clip(0.5 * jax.random.normal(keys[5], (CH,), jnp.float32), -1.5, 1.5)
    values = base * frame_scale[:, None, None, None] * column_scale[None, None, :, None] * scales
    values = values + offsets + frame_offset[:, None, None, None]
    return jnp.clip(values, -20.0, 20.0).astype(jnp.bfloat16)


def draw_cotangent(key, part):
    keys = jax.random.split(jax.random.fold_in(key, 11), 3)
    shape = (FRAMES, ROWS, WIDTH, CH)
    base = jnp.clip(jax.random.normal(keys[0], shape, jnp.float32), -4.0, 4.0)
    channel_offset = jnp.clip(1.5 * jax.random.normal(keys[1], (CH,), jnp.float32), -2.0, 2.0)
    frame_factor = ordered_levels(keys[2], FRAMES, 0.4, 1.2)
    values = base + channel_offset * frame_factor[:, None, None, None]
    return jnp.clip(values, -7.0, 7.0).astype(jnp.bfloat16)


def block_levels(rng, extent, shards, least, top_value):
    def one(dim, blocks):
        draws = jax.random.uniform(jax.random.fold_in(jax.random.fold_in(rng, 6), dim), (blocks,), jnp.float32, least / len(shards), top_value / len(shards))
        return jnp.repeat(jnp.exp(draws), extent[dim] // blocks).reshape((-1,) + (1,) * (len(extent) - dim - 1))

    loudness = one(*shards[0])
    for cut in shards[1:]:
        loudness = loudness * one(*cut)
    return loudness


def noise(key, extent, deviation, reach, cuts=(), dtype=jnp.bfloat16):
    drawn = deviation * jax.random.normal(key, extent, jnp.float32)
    if cuts:
        drawn = drawn * block_levels(key, extent, cuts, -0.22, 0.18)
    return jnp.clip(drawn, -reach, reach).astype(dtype)


def setup_inputs(seed: int = 0) -> dict:
    key_of = jax.random.split(jax.random.key(seed), 7)
    conv_input = noise(key_of[0], (FRAMES, ROWS, WIDTH, CH), 1.0, 6.0, ((0, 16), (2, 2)))
    conv_out = draw_conv_out(jax.random.fold_in(key_of[6], 71), 0)
    kernel = noise(key_of[2], (3, 3, 3, CH, CH), (27 * CH) ** -0.5, 0.078125)
    gain = jnp.clip(1.0 + 0.15 * jax.random.normal(key_of[3], (CH,), jnp.float32), 0.25, 1.75)
    bias = noise(key_of[4], (CH,), 0.8, 4.0, (), jnp.float32)
    cotangent = draw_cotangent(jax.random.fold_in(key_of[6], 71), 0)
    return {"conv_input": conv_input, "conv_out": conv_out, "kernel": kernel, "gain": gain, "bias": bias, "cotangent": cotangent}


epsilon = 1e-06

def reference(conv_input, conv_out, kernel, gain, bias, cotangent):
    frames, rows, cols, chans = conv_out.shape
    width = chans // GROUPS
    grouped = conv_out.astype(jnp.float32).reshape(frames, rows, cols, GROUPS, width)
    count = frames * rows * cols * width
    mean = lax.optimization_barrier(jnp.sum(grouped, axis=(0, 1, 2, 4))) / count
    square = lax.optimization_barrier(jnp.sum(grouped * grouped, axis=(0, 1, 2, 4))) / count
    inv_std = lax.rsqrt(square - mean * mean + epsilon)
    normed_grouped = (grouped - mean[:, None]) * inv_std[:, None]
    normed = normed_grouped.reshape(frames, rows, cols, chans)
    shifted = normed * gain + bias
    sigma = jax.nn.sigmoid(shifted)
    grad_shift = cotangent.astype(jnp.float32) * sigma * (1.0 + shifted * (1.0 - sigma))
    grad_bias = lax.optimization_barrier(jnp.sum(grad_shift, axis=(0, 1, 2)))
    grad_gain = lax.optimization_barrier(jnp.sum(grad_shift * normed, axis=(0, 1, 2)))
    grad_grouped = (grad_shift * gain).reshape(frames, rows, cols, GROUPS, width)
    plain = lax.optimization_barrier(jnp.sum(grad_grouped, axis=(0, 1, 2, 4)))
    product = lax.optimization_barrier(jnp.sum(grad_grouped * normed_grouped, axis=(0, 1, 2, 4)))
    grad_conv = inv_std[:, None] * (grad_grouped - plain[:, None] / count - normed_grouped * product[:, None] / count)
    grad_conv = grad_conv.reshape(frames, rows, cols, chans).astype(jnp.bfloat16)
    padded_input = jnp.pad(conv_input, ((2, 0), (1, 1), (1, 1), (0, 0)))
    padded_grad = jnp.pad(grad_conv, ((0, 2), (1, 1), (1, 1), (0, 0)))
    flat_grad = grad_conv.reshape(-1, chans)
    taps = []
    accum = jnp.zeros((frames * rows * cols, chans), jnp.float32)
    for tap_t in range(3):
        for tap_h in range(3):
            for tap_w in range(3):
                source = padded_input[tap_t:tap_t + frames, tap_h:tap_h + rows, tap_w:tap_w + cols].reshape(-1, chans)
                taps.append(jnp.dot(source.T, flat_grad, preferred_element_type=jnp.float32))
                window = padded_grad[2 - tap_t:2 - tap_t + frames, 2 - tap_h:2 - tap_h + rows, 2 - tap_w:2 - tap_w + cols].reshape(-1, chans)
                accum = accum + jnp.dot(window, kernel[tap_t, tap_h, tap_w].T, preferred_element_type=jnp.float32)
    grad_kernel = jnp.stack(taps).reshape(3, 3, 3, chans, chans)
    grad_input = accum.reshape(frames, rows, cols, chans).astype(jnp.bfloat16)
    return (grad_input, grad_kernel, grad_gain, grad_bias)
```

```python
import functools
import heapq

import jax
import jax.numpy as jnp
from jax import lax
from jax.experimental import pallas as pl
from jax.experimental.pallas import tpu as pltpu
from jax.sharding import PartitionSpec as P

GROUPS = 32
STREAMS = 9
PARTS = 4
EPSILON = 1e-06
MESH = pl.DeviceIdType.MESH
F32 = jnp.float32
BF16 = jnp.bfloat16


def round_up(value, unit):
    return (value + unit - 1) // unit * unit


def group_sum(x, width):
    lanes = x.shape[1]
    lane = lax.broadcasted_iota(jnp.int32, x.shape, 1)
    step = 1
    while step < width:
        up = pltpu.roll(x, lanes - step, 1)
        down = pltpu.roll(x, step, 1)
        x = x + jnp.where((lane // step) % 2 == 0, up, down)
        step *= 2
    return x


def hand_out(gi_in, gk_in, gg_in, gb_in, gi_out, gk_out, gg_out, gb_out):
    gk_out[...] = gk_in[...].astype(F32)

    @pl.when(pl.program_id(0) == 0)
    def _():
        gi_out[...] = gi_in[...]
        gg_out[...] = gg_in[...]
        gb_out[...] = gb_in[...]


TAPS_A = (2, 1, 0)
MATMUL = 0.36
FILLER = 0.36
ON_CHIP = (1.0, 250e3)
ON_LINK = (1.7, 42e3)
FAR = 0.75


def stage_orders(bits, streams):
    straight = list(range(bits))
    swapped = list(range(bits))
    if bits > 2:
        swapped[1], swapped[2] = swapped[2], swapped[1]
    return [swapped if p % 4 == 2 else straight for p in range(streams)]


def stream_starts(sizes, chans):
    done, begun, starts = set(), set(), []
    edges = [sum(sizes[:p]) for p in range(len(sizes) + 1)]
    for a in TAPS_A:
        for b in range(3):
            done.add(a * 3 + b)
            ready = []
            for p in range(len(sizes)):
                first, last = edges[p] // (3 * chans), (min(edges[p + 1], 27 * chans) - 1) // (3 * chans)
                if p not in begun and all(g in done for g in range(first, last + 1)):
                    begun.add(p)
                    ready.append(p)
            starts.append(((a, b), ready))
    return starts


def plan(bits, sizes, orders, starts, row_bytes):
    free = {}
    heap = []
    steps = 2 * bits

    def send(now, p, step):
        level = step if step < bits else steps - 1 - step
        rows = sizes[p] >> (level + 1)
        bit = orders[p][level]
        latency, rate = ON_CHIP if bit == 0 else ON_LINK
        time = rows * row_bytes / rate
        if bit > 2:
            latency, time = latency + FAR, 2 * time
        link = min(bit, 2)
        begin = max(now, free.get(link, 0.0))
        free[link] = begin + time
        heapq.heappush(heap, (begin + time + latency, step, p))

    matmuls = list(starts)
    fillers = [(0.0, ("gown", 0)), (4.5, ("gown", 1)), (7.5, ("gown", 2))]
    fillers += [(0.0, ("input", a, b)) for a in TAPS_A for b in range(3)]
    tasks, now = [], 0.0
    while heap or matmuls or fillers:
        if heap and heap[0][0] <= now:
            _, step, p = heapq.heappop(heap)
            tasks.append(("arrive", p, step))
            now += 0.03 + 1.5e-4 * (sizes[p] >> (step + 1) if step < bits else 0)
            if step + 1 < steps:
                send(now, p, step + 1)
        elif matmuls:
            (a, b), ready = matmuls.pop(0)
            tasks.append(("taps", a, b, ready))
            now += MATMUL
            for p in ready:
                send(now, p, 0)
        elif fillers and fillers[0][0] <= now:
            tasks.append(fillers.pop(0)[1])
            now += FILLER
        else:
            times = [heap[0][0]] if heap else []
            times += [fillers[0][0]] if fillers else []
            now = min(times)
    return tasks


def body(
    T, S, sizes,
    x_hbm, co_hbm, k_hbm, gain_ref, bias_ref, ct_hbm,
    gi_ref, gk_ref, gg_ref, gb_ref,
    xw, co_ref, ct_ref, slice_out, cw, st_out, st_in, own, pre, fx, fg, fbuf,
    gs, gh, ge_out, ge_in, gown, gw, xt, wbuf, tot, acc, sbuf, rbuf,
    in_sem, w_sem, st_send, st_recv, bulk_send, bulk_recv, rs_send, rs_recv,
):
    N = T * S
    total_rows = sum(sizes)
    _, rows, cols, chans = co_ref.shape
    width = cols * S
    ce = chans // S
    depth = xt.shape[2]
    pitch = fbuf.shape[1]
    flat = rows * pitch
    flat_all = (rows + 2) * pitch
    halves = chans // 128
    t = lax.axis_index("tm")
    s = lax.axis_index("space")
    me = t * S + s

    loads = [
        pltpu.make_async_copy(src, dst, in_sem.at[i])
        for i, (src, dst) in enumerate(((co_hbm, co_ref), (ct_hbm, ct_ref), (x_hbm.at[0], xw.at[0, s])))
    ]
    for copy in loads:
        copy.start()
    load = pltpu.make_async_copy(k_hbm, wbuf, w_sem)
    load.start()

    barrier = pltpu.get_barrier_semaphore()

    def greet(r, carry):
        d = lax.rem(me + r, N)
        pl.semaphore_signal(barrier, inc=1, device_id=(d // S, lax.rem(d, S)), device_id_type=MESH)
        return carry

    lax.fori_loop(1, N, greet, 0)

    loads[0].wait()
    conv = co_ref[0].astype(F32)
    first = jnp.sum(jnp.sum(conv, axis=0), axis=0, keepdims=True)
    second = jnp.sum(jnp.sum(conv * conv, axis=0), axis=0, keepdims=True)

    def put_stats(which, one, two):
        for i in range(halves):
            st_out[which, i : i + 1, :] = one[:, i * 128 : (i + 1) * 128]
            st_out[which, halves + i : halves + i + 1, :] = two[:, i * 128 : (i + 1) * 128]

    def send_stats(which):
        def send(r, carry):
            r = 1 + lax.rem(r + N // 2 - 1, N - 1)
            d = lax.rem(me + r, N)
            pltpu.make_async_remote_copy(
                src_ref=st_out.at[which], dst_ref=st_in.at[which, r - 1],
                send_sem=st_send.at[which], recv_sem=st_recv.at[which],
                device_id=(d // S, lax.rem(d, S)), device_id_type=MESH,
            ).start()
            return carry

        lax.fori_loop(1, N, send, 0)

    def take_stats(which):
        pltpu.make_async_copy(st_in.at[which], st_in.at[which], st_recv.at[which]).wait()
        return jnp.sum(st_in[which], axis=0) + st_out[which]

    put_stats(0, first, second)
    loads[1].wait()
    loads[2].wait()
    for arr, ref in ((0, co_ref), (1, ct_ref)):
        whole = ref[0]
        for j in range(S):
            slice_out[j, arr] = whole[:, :, j * ce : (j + 1) * ce]
    keep = pltpu.make_async_copy(slice_out.at[s], cw.at[s], in_sem.at[3])
    keep.start()
    pl.semaphore_wait(barrier, N - 1)
    send_stats(0)

    sent = []

    def push(src, dst, device, ok=None):
        i = len(sent)
        copy = pltpu.make_async_remote_copy(
            src_ref=src, dst_ref=dst, send_sem=bulk_send.at[i], recv_sem=bulk_recv.at[i],
            device_id=device, device_id_type=MESH,
        )
        if ok is None:
            copy.start()
        else:
            pl.when(ok)(copy.start)
        sent.append((copy, ok))
        return i

    def take(i, dst, ok=None):
        copy = pltpu.make_async_copy(dst, dst, bulk_recv.at[i])
        if ok is None:
            copy.wait()
        else:
            pl.when(ok)(copy.wait)

    def frame(n):
        return lax.rem(t + T + n, T)

    def strip(n):
        return lax.rem(s + S + n, S)

    ahead = (frame(1), s)
    behind = (frame(-1), s)
    has_next, has_before = t + 1 < T, t > 0
    cut, mate, past = [], [], [[], []]
    for r in range(1, S):
        cut.append(push(slice_out.at[strip(-r)], cw.at[s], (t, strip(-r))))
    past[0].append(push(xw.at[0, s], xw.at[1, s], ahead, has_next))
    for r in range(1, S):
        mate.append(push(xw.at[0, s], xw.at[0, s], (t, strip(-r))))

    def relay(k, r):
        j = strip(r)
        if k == 0:
            take(mate[r - 1], xw.at[0, j])
            ok = has_next
        else:
            take(past[k - 1][r], xw.at[k, j], has_before)
            ok = has_next & has_before
        if k < 2:
            past[k].append(push(xw.at[k, j], xw.at[k + 1, j], ahead, ok))

    fx[...] = jnp.zeros_like(fx)
    fg[...] = jnp.zeros_like(fg)
    fbuf[...] = jnp.zeros_like(fbuf)
    if total_rows > 27 * chans:
        acc[27 * chans :, :] = jnp.zeros((total_rows - 27 * chans, ce), F32)

    gain = gain_ref[...]
    bias = bias_ref[...]
    group = chans // GROUPS
    count = rows * width * T * group
    relay(1, 0)
    for r in range(1, S):
        relay(0, r)
    sums = take_stats(0)
    grouped = group_sum(sums, group)
    mean2 = grouped[:halves] / count
    inv2 = lax.rsqrt(grouped[halves:] / count - mean2 * mean2 + EPSILON)

    def wide(two):
        return jnp.concatenate([two[i : i + 1] for i in range(halves)], axis=1)

    mean, inv = wide(mean2), wide(inv2)

    def shift_grad(conv, cot, mean, inv, gain, bias):
        normed = (conv.astype(F32) - mean) * inv
        shifted = normed * gain + bias
        sigma = jax.nn.sigmoid(shifted)
        return normed, cot.astype(F32) * sigma * (1.0 + shifted * (1.0 - sigma))

    normed, grad = shift_grad(co_ref[0], ct_ref[0], mean, inv, gain, bias)
    own[0] = normed
    own[1] = grad
    put_stats(
        1,
        jnp.sum(jnp.sum(grad, axis=0), axis=0, keepdims=True),
        jnp.sum(jnp.sum(grad * normed, axis=0), axis=0, keepdims=True),
    )
    send_stats(1)

    def part(v):
        out = v[..., 0:ce]
        for j in range(1, S):
            out = jnp.where(s == j, v[..., j * ce : (j + 1) * ce], out)
        return out

    for r in range(1, S):
        relay(1, r)
        take(cut[r - 1], cw.at[strip(r)])
    keep.wait()
    firsts = tuple(part(p) for p in (mean, inv, gain, bias))
    for j in range(S):
        normed, grad = shift_grad(cw[j, 0], cw[j, 1], *firsts)
        pre[j, 0] = normed
        pre[j, 1] = grad

    def put_input(k):
        for j in range(S):
            value = xw[k, j].astype(F32)
            if k > 0:
                value = jnp.where(t >= k, value, 0.0)
            fx[0:rows, j * cols : (j + 1) * cols, :] = value
        placed = fx[...].reshape(fx.shape[0] * fx.shape[1], chans)[0:depth]
        xt[k] = jnp.transpose(placed).astype(BF16)

    put_input(0)
    put_input(1)
    relay_second = t > 1
    for r in range(S):
        take(past[1][r], xw.at[2, strip(r)], relay_second)
    put_input(2)
    sums = take_stats(1)
    chan_bias, chan_gain = wide(sums[:halves]), wide(sums[halves:])
    gb_ref[...] = chan_bias
    gg_ref[...] = chan_gain
    gain2 = jnp.concatenate([gain[:, i * 128 : (i + 1) * 128] for i in range(halves)], axis=0)
    plain = wide(group_sum(sums[:halves] * gain2, group)) / count
    product = wide(group_sum(sums[halves:] * gain2, group)) / count

    def conv_grad(normed, grad, inv, gain, plain, product):
        return inv * (grad * gain - plain - normed * product)

    g = conv_grad(own[0], own[1], inv, gain, plain, product)
    gs[...] = g.astype(BF16)
    for h in range(rows):
        ge_out[0, h : h + 1, :] = g[h, 0:1, :].astype(BF16)
        ge_out[1, h : h + 1, :] = g[h, cols - 1 : cols, :].astype(BF16)
    later = [push(gs, gh.at[0], behind, has_before)]
    rims = []
    for k in range(3):
        back = (frame(-k), strip(1)), (frame(-k), strip(-1))
        rims.append((
            push(ge_out.at[1], ge_in.at[k, 0], back[0], (t >= k) & (s + 1 < S)),
            push(ge_out.at[0], ge_in.at[k, 1], back[1], (t >= k) & (s > 0)),
        ))

    seconds = tuple(part(p) for p in (inv, gain, plain, product))
    for j in range(S):
        fg[1 : rows + 1, j * cols : (j + 1) * cols, :] = conv_grad(pre[j, 0], pre[j, 1], *seconds)
    tall = fg.shape[0] * width
    f = fg[...].reshape(tall, ce)
    column = lax.broadcasted_iota(jnp.int32, fg.shape, 1).reshape(tall, ce)
    moved = (
        jnp.where(column < width - 1, pltpu.roll(f, tall - 1, 0), 0.0),
        f,
        jnp.where(column > 0, pltpu.roll(f, 1, 0), 0.0),
    )
    for c, w in enumerate(moved):
        for b in range(3):
            gw[b, :, c * ce : (c + 1) * ce] = w[(2 - b) * width : (2 - b) * width + depth].astype(BF16)

    bits = T.bit_length() - 1
    streams = len(sizes)
    orders = stage_orders(bits, streams)
    starts = stream_starts(sizes, chans)
    bases = [sum(sizes[:p]) for p in range(streams)]
    offs = [0] * streams
    flying = [None] * streams
    copies = []

    def side(bit):
        return lax.rem(t // (2**bit), 2)

    def partner(bit):
        return (t + (1 - 2 * side(bit)) * 2**bit, s)

    def span(p, off, n):
        return pl.ds(pl.multiple_of(bases[p] + off, 16), n)

    def start_of(p, i):
        return bases[p] + sizes[p] - (sizes[p] >> i)

    def launch(i, p):
        half = sizes[p] >> (i + 1)
        start = start_of(p, i)
        copy = pltpu.make_async_remote_copy(
            src_ref=sbuf.at[start : start + half], dst_ref=rbuf.at[start : start + half],
            send_sem=rs_send.at[0, p, i], recv_sem=rs_recv.at[0, p, i],
            device_id=partner(orders[p][i]), device_id_type=MESH,
        )
        copy.start()
        copies.append(copy)
        flying[p] = copy

    def begin(p):
        half = sizes[p] >> 1
        mine = side(orders[p][0])
        start = start_of(p, 0)
        sbuf[start : start + half, :] = acc[span(p, (1 - mine) * half, half), :].astype(BF16)
        launch(0, p)
        offs[p] = mine * half

    def sum_at(p, i, off, n):
        at = span(p, offs[p] + off, n)
        seen = pl.ds(pl.multiple_of(start_of(p, i) + off, 16), n)
        return at, acc[at, :] + rbuf[seen, :].astype(F32)

    def spread(i, p):
        n = sizes[p] >> (i + 1)
        bit = orders[p][i]
        at = span(p, offs[p], n)
        copy = pltpu.make_async_remote_copy(
            src_ref=gk_ref.at[at], dst_ref=gk_ref.at[at],
            send_sem=rs_send.at[1, p, i], recv_sem=rs_recv.at[1, p, i],
            device_id=partner(bit), device_id_type=MESH,
        )
        copy.start()
        copies.append(copy)
        offs[p] = offs[p] - side(bit) * n
        flying[p] = copy

    def arrive(p, step):
        flying[p].wait_recv()
        if step < bits - 1:
            half = sizes[p] >> (step + 2)
            mine = side(orders[p][step + 1])
            start = start_of(p, step + 1)
            _, value = sum_at(p, step, (1 - mine) * half, half)
            sbuf[start : start + half, :] = value.astype(BF16)
            launch(step + 1, p)
            at, value = sum_at(p, step, mine * half, half)
            acc[at, :] = value
            offs[p] = offs[p] + mine * half
        elif step == bits - 1:
            at, value = sum_at(p, step, 0, sizes[p] >> bits)
            gk_ref[at, :] = value.astype(BF16)
            spread(bits - 1, p)
        elif step + 1 < 2 * bits:
            spread(2 * bits - 2 - step, p)

    def taps(a, b, ready):
        res = jnp.dot(xt[2 - a], gw[b], preferred_element_type=F32)
        for c in range(3):
            at = ((a * 3 + b) * 3 + c) * chans
            acc[at : at + chans, :] = res[:, c * ce : (c + 1) * ce]
        for p in ready:
            begin(p)

    def put_gown(k):
        live = t + k < T
        if k == 0:
            value = gs[...].astype(F32)
        else:
            take(later[k - 1], gh.at[k - 1], live)
            if k == 1:
                later.append(push(gh.at[0], gh.at[1], behind, live & has_before))
            value = jnp.where(live, gh[k - 1].astype(F32), 0.0)
        fbuf[1 : rows + 1, 0:cols, :] = value
        take(rims[k][0], ge_in.at[k, 0], live & (s > 0))
        take(rims[k][1], ge_in.at[k, 1], live & (s + 1 < S))
        left = jnp.where(live & (s > 0), ge_in[k, 0].astype(F32), 0.0)
        right = jnp.where(live & (s < S - 1), ge_in[k, 1].astype(F32), 0.0)
        for h in range(rows):
            fbuf[h, pitch - 1 : pitch, :] = left[h : h + 1]
            fbuf[h + 1, cols : cols + 1, :] = right[h : h + 1]
        f = fbuf[...].reshape(flat_all, chans)
        for c, w in enumerate((pltpu.roll(f, flat_all - 1, 0), f, pltpu.roll(f, 1, 0))):
            gown[k, :, c * chans : (c + 1) * chans] = w.astype(BF16)

    counted = [0]

    def input_grad(a, b):
        if counted[0] == 0:
            load.wait()
        total = None if counted[0] == 0 else tot[...]
        for c in range(3):
            term = lax.dot_general(
                gown[2 - a, (2 - b) * pitch : (2 - b) * pitch + flat, c * chans : (c + 1) * chans],
                wbuf[a, b, c], (((1,), (1,)), ((), ())), preferred_element_type=F32,
            )
            total = term if total is None else total + term
        counted[0] += 1
        if counted[0] < 9:
            tot[...] = total
        else:
            gi_ref[0] = total.reshape(rows, pitch, chans)[:, 0:cols, :].astype(BF16)

    for task in plan(bits, sizes, orders, starts, ce * 2):
        if task[0] == "taps":
            taps(*task[1:])
        elif task[0] == "arrive":
            arrive(*task[1:])
        elif task[0] == "gown":
            put_gown(task[1])
        else:
            input_grad(*task[1:])

    for copy in copies:
        copy.wait_send()
    for copy, ok in sent:
        if ok is None:
            copy.wait_send()
        else:
            pl.when(ok)(copy.wait_send)
    for which in range(2):
        pltpu.make_async_copy(st_in.at[which], st_in.at[which], st_send.at[which]).wait()


def solution(mesh):
    T, S = mesh.shape["tm"], mesh.shape["space"]

    def shards(conv_input, conv_out, kernel, gain, bias, cotangent):
        _, rows, cols, chans = conv_out.shape
        width = cols * S
        ce = chans // S
        bits = T.bit_length() - 1
        groups = round_up(27 * chans, T * 16) // (T * 16)
        streams = min(STREAMS, groups)
        sizes = [(groups // streams + (p < groups % streams)) * T * 16 for p in range(streams)]
        total_rows = sum(sizes)
        pitch = round_up(cols + 2, 16)
        depth = round_up(rows * width, 128)
        fx_rows = (depth + width - 1) // width
        fg_rows = max(rows + 2, (2 * width + depth + width - 1) // width)
        n_bulk = (S - 1) * 2 + 2 * S + 2 + 6
        vmem = pl.BlockSpec(memory_space=pltpu.VMEM)
        whole = pl.BlockSpec(memory_space=pl.ANY)
        gi, gk, gg, gb = pl.pallas_call(
            functools.partial(body, T, S, sizes),
            out_shape=(
                jax.ShapeDtypeStruct(conv_input.shape, BF16),
                jax.ShapeDtypeStruct((total_rows, ce), BF16),
                jax.ShapeDtypeStruct((1, chans), F32),
                jax.ShapeDtypeStruct((1, chans), F32),
            ),
            in_specs=[whole, whole, whole, vmem, vmem, whole],
            out_specs=(vmem, vmem, vmem, vmem),
            scratch_shapes=[
                pltpu.VMEM((3, S, rows, cols, chans), BF16),
                pltpu.VMEM(conv_out.shape, BF16),
                pltpu.VMEM(cotangent.shape, BF16),
                pltpu.VMEM((S, 2, rows, cols, ce), BF16),
                pltpu.VMEM((S, 2, rows, cols, ce), BF16),
                pltpu.VMEM((2, 2 * chans // 128, 128), F32),
                pltpu.VMEM((2, T * S - 1, 2 * chans // 128, 128), F32),
                pltpu.VMEM((2, rows, cols, chans), F32),
                pltpu.VMEM((S, 2, rows, cols, ce), F32),
                pltpu.VMEM((fx_rows, width, chans), F32),
                pltpu.VMEM((fg_rows, width, ce), F32),
                pltpu.VMEM((rows + 2, pitch, chans), F32),
                pltpu.VMEM((rows, cols, chans), BF16),
                pltpu.VMEM((2, rows, cols, chans), BF16),
                pltpu.VMEM((2, rows, chans), BF16),
                pltpu.VMEM((3, 2, rows, chans), BF16),
                pltpu.VMEM((3, (rows + 2) * pitch, 3 * chans), BF16),
                pltpu.VMEM((3, depth, 3 * ce), BF16),
                pltpu.VMEM((3, chans, depth), BF16),
                pltpu.VMEM((3, 3, 3, chans, chans), BF16),
                pltpu.VMEM((rows * pitch, chans), F32),
                pltpu.VMEM((total_rows, ce), F32),
                pltpu.VMEM((total_rows, ce), BF16),
                pltpu.VMEM((total_rows, ce), BF16),
                pltpu.SemaphoreType.DMA((4,)),
                pltpu.SemaphoreType.DMA,
                pltpu.SemaphoreType.DMA((2,)),
                pltpu.SemaphoreType.DMA((2,)),
                pltpu.SemaphoreType.DMA((n_bulk,)),
                pltpu.SemaphoreType.DMA((n_bulk,)),
                pltpu.SemaphoreType.DMA((2, streams, bits)),
                pltpu.SemaphoreType.DMA((2, streams, bits)),
            ],
            compiler_params=pltpu.CompilerParams(
                collective_id=0, has_side_effects=True, vmem_limit_bytes=60 * 1024 * 1024
            ),
        )(conv_input, conv_out, kernel, gain.reshape(1, chans), bias.reshape(1, chans), cotangent)
        part_rows = 27 * chans // PARTS
        gi, gk, gg, gb = pl.pallas_call(
            hand_out,
            grid=(PARTS,),
            out_shape=(
                jax.ShapeDtypeStruct(gi.shape, BF16),
                jax.ShapeDtypeStruct((27 * chans, ce), F32),
                jax.ShapeDtypeStruct((1, chans), F32),
                jax.ShapeDtypeStruct((1, chans), F32),
            ),
            in_specs=[
                pl.BlockSpec(gi.shape, lambda i: (0, 0, 0, 0)),
                pl.BlockSpec((part_rows, ce), lambda i: (i, 0)),
                pl.BlockSpec((1, chans), lambda i: (0, 0)),
                pl.BlockSpec((1, chans), lambda i: (0, 0)),
            ],
            out_specs=(
                pl.BlockSpec(gi.shape, lambda i: (0, 0, 0, 0)),
                pl.BlockSpec((part_rows, ce), lambda i: (i, 0)),
                pl.BlockSpec((1, chans), lambda i: (0, 0)),
                pl.BlockSpec((1, chans), lambda i: (0, 0)),
            ),
        )(gi, gk, gg, gb)
        return gi, gk.reshape(3, 3, 3, chans, ce), gg.reshape(chans), gb.reshape(chans)

    strip = P("tm", None, "space", None)
    return jax.shard_map(
        shards,
        mesh=mesh,
        in_specs=(strip, strip, P(), P(), P(), strip),
        out_specs=(strip, P(None, None, None, None, "space"), P(), P()),
        check_vma=False,
    )
```

```python
import functools
import heapq

import jax
import jax.numpy as jnp
from jax import lax
from jax.experimental import pallas as pl
from jax.experimental.pallas import tpu as pltpu
from jax.sharding import PartitionSpec as P

GROUPS = 32
STREAMS = 13
PARTS = 2
EPSILON = 1e-06
MESH = pl.DeviceIdType.MESH
F32 = jnp.float32
BF16 = jnp.bfloat16


def round_up(value, unit):
    return (value + unit - 1) // unit * unit


def group_sum(x, width):
    lanes = x.shape[1]
    lane = lax.broadcasted_iota(jnp.int32, x.shape, 1)
    step = 1
    while step < width:
        up = pltpu.roll(x, lanes - step, 1)
        down = pltpu.roll(x, step, 1)
        x = x + jnp.where((lane // step) % 2 == 0, up, down)
        step *= 2
    return x


def hand_out(gi_in, gk_in, gg_in, gb_in, gi_out, gk_out, gg_out, gb_out):
    gk_out[...] = gk_in[...].astype(F32)

    @pl.when(pl.program_id(0) == 0)
    def _():
        gi_out[...] = gi_in[...]
        gg_out[...] = gg_in[...]
        gb_out[...] = gb_in[...]


TAPS_A = (2, 1, 0)
MATMUL = 0.36
FILLER = 0.36
ON_CHIP = (1.1, 200e3)
ON_LINK = (1.7, 46e3)
FAR = 0.75


def stage_orders(bits, streams):
    straight = list(range(bits))
    swapped = list(range(bits))
    if bits > 2:
        swapped[1], swapped[2] = swapped[2], swapped[1]
    return [swapped if p % 2 else straight for p in range(streams)]


def stream_starts(sizes, chans):
    done, begun, starts = set(), set(), []
    edges = [sum(sizes[:p]) for p in range(len(sizes) + 1)]
    for a in TAPS_A:
        for b in range(3):
            done.add(a * 3 + b)
            ready = []
            for p in range(len(sizes)):
                first, last = edges[p] // (3 * chans), (min(edges[p + 1], 27 * chans) - 1) // (3 * chans)
                if p not in begun and all(g in done for g in range(first, last + 1)):
                    begun.add(p)
                    ready.append(p)
            starts.append(((a, b), ready))
    return starts


def plan(bits, sizes, orders, starts, row_bytes):
    free = {}
    heap = []
    steps = 2 * bits

    def send(now, p, step):
        level = step if step < bits else steps - 1 - step
        rows = sizes[p] >> (level + 1)
        bit = orders[p][level]
        latency, rate = ON_CHIP if bit == 0 else ON_LINK
        time = rows * row_bytes / rate
        if bit > 2:
            latency, time = latency + FAR, 2 * time
        link = min(bit, 2)
        begin = max(now, free.get(link, 0.0))
        free[link] = begin + time
        heapq.heappush(heap, (begin + time + latency, step, p))

    matmuls = list(starts)
    fillers = [(0.0, ("gown", 0))] + [(0.0, ("input", 2, b)) for b in range(3)]
    fillers += [(7.0, ("gown", 1))] + [(0.0, ("input", 1, b)) for b in range(3)]
    fillers += [(11.0, ("gown", 2))] + [(0.0, ("input", 0, b)) for b in range(3)]
    tasks, now = [], 0.0
    while heap or matmuls or fillers:
        if heap and heap[0][0] <= now:
            _, step, p = heapq.heappop(heap)
            tasks.append(("arrive", p, step))
            now += 0.03 + 1.5e-4 * (sizes[p] >> (step + 1) if step < bits else 0)
            if step + 1 < steps:
                send(now, p, step + 1)
        elif matmuls:
            (a, b), ready = matmuls.pop(0)
            tasks.append(("taps", a, b, ready))
            now += MATMUL
            for p in ready:
                send(now, p, 0)
        elif fillers and fillers[0][0] <= now and (not heap or heap[0][0] - now >= 0.8 * FILLER):
            tasks.append(fillers.pop(0)[1])
            now += FILLER
        else:
            now = heap[0][0] if heap else fillers[0][0]
    return tasks


def body(
    T, S, sizes,
    x_hbm, co_hbm, k_hbm, gain_ref, bias_ref, ct_hbm,
    gi_ref, gk_ref, gg_ref, gb_ref,
    xw, co_ref, ct_ref, slice_out, cw, st_out, st_in, own, pre, fx, fg, fbuf,
    gs, gh, ge_out, ge_in, gown, gw, xt, wbuf, tot, acc, sbuf, rbuf,
    in_sem, w_sem, st_send, st_recv, bulk_send, bulk_recv, rs_send, rs_recv,
):
    N = T * S
    total_rows = sum(sizes)
    _, rows, cols, chans = co_ref.shape
    width = cols * S
    ce = chans // S
    depth = xt.shape[2]
    pitch = fbuf.shape[1]
    flat = rows * pitch
    flat_all = (rows + 2) * pitch
    halves = chans // 128
    t = lax.axis_index("tm")
    s = lax.axis_index("space")
    me = t * S + s

    loads = [
        pltpu.make_async_copy(src, dst, in_sem.at[i])
        for i, (src, dst) in enumerate(((co_hbm, co_ref), (ct_hbm, ct_ref), (x_hbm.at[0], xw.at[0, s])))
    ]
    for copy in loads:
        copy.start()
    load = pltpu.make_async_copy(k_hbm, wbuf, w_sem)
    load.start()

    barrier = pltpu.get_barrier_semaphore()

    def greet(r, carry):
        d = lax.rem(me + r, N)
        pl.semaphore_signal(barrier, inc=1, device_id=(d // S, lax.rem(d, S)), device_id_type=MESH)
        return carry

    lax.fori_loop(1, N, greet, 0)

    loads[0].wait()
    conv = co_ref[0].astype(F32)
    first = jnp.sum(jnp.sum(conv, axis=0), axis=0, keepdims=True)
    second = jnp.sum(jnp.sum(conv * conv, axis=0), axis=0, keepdims=True)

    def put_stats(which, one, two):
        for i in range(halves):
            st_out[which, i : i + 1, :] = one[:, i * 128 : (i + 1) * 128]
            st_out[which, halves + i : halves + i + 1, :] = two[:, i * 128 : (i + 1) * 128]

    def send_stats(which):
        def send(r, carry):
            r = 1 + lax.rem(r + N // 2 - 1, N - 1)
            d = lax.rem(me + r, N)
            pltpu.make_async_remote_copy(
                src_ref=st_out.at[which], dst_ref=st_in.at[which, r - 1],
                send_sem=st_send.at[which], recv_sem=st_recv.at[which],
                device_id=(d // S, lax.rem(d, S)), device_id_type=MESH,
            ).start()
            return carry

        lax.fori_loop(1, N, send, 0)

    def take_stats(which):
        pltpu.make_async_copy(st_in.at[which], st_in.at[which], st_recv.at[which]).wait()
        return jnp.sum(st_in[which], axis=0) + st_out[which]

    put_stats(0, first, second)
    loads[1].wait()
    loads[2].wait()
    for arr, ref in ((0, co_ref), (1, ct_ref)):
        whole = ref[0]
        for j in range(S):
            slice_out[j, arr] = whole[:, :, j * ce : (j + 1) * ce]
    keep = pltpu.make_async_copy(slice_out.at[s], cw.at[s], in_sem.at[3])
    keep.start()
    pl.semaphore_wait(barrier, N - 1)
    send_stats(0)

    sent = []

    def push(src, dst, device, ok=None):
        i = len(sent)
        copy = pltpu.make_async_remote_copy(
            src_ref=src, dst_ref=dst, send_sem=bulk_send.at[i], recv_sem=bulk_recv.at[i],
            device_id=device, device_id_type=MESH,
        )
        if ok is None:
            copy.start()
        else:
            pl.when(ok)(copy.start)
        sent.append((copy, ok))
        return i

    def take(i, dst, ok=None):
        copy = pltpu.make_async_copy(dst, dst, bulk_recv.at[i])
        if ok is None:
            copy.wait()
        else:
            pl.when(ok)(copy.wait)

    def frame(n):
        return lax.rem(t + T + n, T)

    def strip(n):
        return lax.rem(s + S + n, S)

    ahead = (frame(1), s)
    behind = (frame(-1), s)
    has_next, has_before = t + 1 < T, t > 0
    cut, mate, past = [], [], [[], []]
    past[0].append(push(xw.at[0, s], xw.at[1, s], ahead, has_next))
    for r in range(1, S):
        mate.append(push(xw.at[0, s], xw.at[0, s], (t, strip(-r))))
    for r in range(1, S):
        cut.append(push(slice_out.at[strip(-r)], cw.at[s], (t, strip(-r))))

    def relay(k, r):
        j = strip(r)
        if k == 0:
            take(mate[r - 1], xw.at[0, j])
            ok = has_next
        else:
            take(past[k - 1][r], xw.at[k, j], has_before)
            ok = has_next & has_before
        if k < 2:
            past[k].append(push(xw.at[k, j], xw.at[k + 1, j], ahead, ok))

    fx[...] = jnp.zeros_like(fx)
    fg[...] = jnp.zeros_like(fg)
    fbuf[...] = jnp.zeros_like(fbuf)
    if total_rows > 27 * chans:
        acc[27 * chans :, :] = jnp.zeros((total_rows - 27 * chans, ce), F32)

    gain = gain_ref[...]
    bias = bias_ref[...]
    group = chans // GROUPS
    count = rows * width * T * group
    relay(1, 0)
    sums = take_stats(0)
    grouped = group_sum(sums, group)
    mean2 = grouped[:halves] / count
    inv2 = lax.rsqrt(grouped[halves:] / count - mean2 * mean2 + EPSILON)

    def wide(two):
        return jnp.concatenate([two[i : i + 1] for i in range(halves)], axis=1)

    mean, inv = wide(mean2), wide(inv2)

    def shift_grad(conv, cot, mean, inv, gain, bias):
        normed = (conv.astype(F32) - mean) * inv
        shifted = normed * gain + bias
        sigma = jax.nn.sigmoid(shifted)
        return normed, cot.astype(F32) * sigma * (1.0 + shifted * (1.0 - sigma))

    normed, grad = shift_grad(co_ref[0], ct_ref[0], mean, inv, gain, bias)
    own[0] = normed
    own[1] = grad
    put_stats(
        1,
        jnp.sum(jnp.sum(grad, axis=0), axis=0, keepdims=True),
        jnp.sum(jnp.sum(grad * normed, axis=0), axis=0, keepdims=True),
    )
    send_stats(1)

    def part(v):
        out = v[..., 0:ce]
        for j in range(1, S):
            out = jnp.where(s == j, v[..., j * ce : (j + 1) * ce], out)
        return out

    for r in range(1, S):
        relay(0, r)
    for r in range(1, S):
        take(cut[r - 1], cw.at[strip(r)])
    keep.wait()
    firsts = tuple(part(p) for p in (mean, inv, gain, bias))
    for j in range(S):
        normed, grad = shift_grad(cw[j, 0], cw[j, 1], *firsts)
        pre[j, 0] = normed
        pre[j, 1] = grad

    def put_input(k):
        for j in range(S):
            value = xw[k, j].astype(F32)
            if k > 0:
                value = jnp.where(t >= k, value, 0.0)
            fx[0:rows, j * cols : (j + 1) * cols, :] = value
        placed = fx[...].reshape(fx.shape[0] * fx.shape[1], chans)[0:depth]
        xt[k] = jnp.transpose(placed).astype(BF16)

    put_input(0)
    for r in range(1, S):
        relay(1, r)
    put_input(1)
    sums = take_stats(1)
    chan_bias, chan_gain = wide(sums[:halves]), wide(sums[halves:])
    gb_ref[...] = chan_bias
    gg_ref[...] = chan_gain
    gain2 = jnp.concatenate([gain[:, i * 128 : (i + 1) * 128] for i in range(halves)], axis=0)
    plain = wide(group_sum(sums[:halves] * gain2, group)) / count
    product = wide(group_sum(sums[halves:] * gain2, group)) / count

    def conv_grad(normed, grad, inv, gain, plain, product):
        return inv * (grad * gain - plain - normed * product)

    g = conv_grad(own[0], own[1], inv, gain, plain, product)
    gs[...] = g.astype(BF16)
    for h in range(rows):
        ge_out[0, h : h + 1, :] = g[h, 0:1, :].astype(BF16)
        ge_out[1, h : h + 1, :] = g[h, cols - 1 : cols, :].astype(BF16)
    odd = lax.rem(t, 2) == 1
    later = [
        push(gs, gh.at[0], behind, has_before),
        push(gs, gh.at[1], (frame(-2), s), odd & (t > 1)),
    ]
    rims = []
    for k in range(3):
        back = (frame(-k), strip(1)), (frame(-k), strip(-1))
        rims.append((
            push(ge_out.at[1], ge_in.at[k, 0], back[0], (t >= k) & (s + 1 < S)),
            push(ge_out.at[0], ge_in.at[k, 1], back[1], (t >= k) & (s > 0)),
        ))

    seconds = tuple(part(p) for p in (inv, gain, plain, product))
    for j in range(S):
        fg[1 : rows + 1, j * cols : (j + 1) * cols, :] = conv_grad(pre[j, 0], pre[j, 1], *seconds)
    tall = fg.shape[0] * width
    f = fg[...].reshape(tall, ce)
    column = lax.broadcasted_iota(jnp.int32, fg.shape, 1).reshape(tall, ce)
    moved = (
        jnp.where(column < width - 1, pltpu.roll(f, tall - 1, 0), 0.0),
        f,
        jnp.where(column > 0, pltpu.roll(f, 1, 0), 0.0),
    )
    for c, w in enumerate(moved):
        for b in range(3):
            gw[b, :, c * ce : (c + 1) * ce] = w[(2 - b) * width : (2 - b) * width + depth].astype(BF16)

    bits = T.bit_length() - 1
    streams = len(sizes)
    orders = stage_orders(bits, streams)
    starts = stream_starts(sizes, chans)
    bases = [sum(sizes[:p]) for p in range(streams)]
    offs = [0] * streams
    flying = [None] * streams
    copies = []

    def side(bit):
        return lax.rem(t // (2**bit), 2)

    def partner(bit):
        return (t + (1 - 2 * side(bit)) * 2**bit, s)

    def span(p, off, n):
        return pl.ds(pl.multiple_of(bases[p] + off, 16), n)

    def start_of(p, i):
        return bases[p] + sizes[p] - (sizes[p] >> i)

    def launch(i, p):
        half = sizes[p] >> (i + 1)
        start = start_of(p, i)
        copy = pltpu.make_async_remote_copy(
            src_ref=sbuf.at[start : start + half], dst_ref=rbuf.at[start : start + half],
            send_sem=rs_send.at[0, p, i], recv_sem=rs_recv.at[0, p, i],
            device_id=partner(orders[p][i]), device_id_type=MESH,
        )
        copy.start()
        copies.append(copy)
        flying[p] = copy

    def begin(p):
        half = sizes[p] >> 1
        mine = side(orders[p][0])
        start = start_of(p, 0)
        sbuf[start : start + half, :] = acc[span(p, (1 - mine) * half, half), :].astype(BF16)
        launch(0, p)
        offs[p] = mine * half

    def sum_at(p, i, off, n):
        at = span(p, offs[p] + off, n)
        seen = pl.ds(pl.multiple_of(start_of(p, i) + off, 16), n)
        return at, acc[at, :] + rbuf[seen, :].astype(F32)

    def spread(i, p):
        n = sizes[p] >> (i + 1)
        bit = orders[p][i]
        at = span(p, offs[p], n)
        copy = pltpu.make_async_remote_copy(
            src_ref=gk_ref.at[at], dst_ref=gk_ref.at[at],
            send_sem=rs_send.at[1, p, i], recv_sem=rs_recv.at[1, p, i],
            device_id=partner(bit), device_id_type=MESH,
        )
        copy.start()
        copies.append(copy)
        offs[p] = offs[p] - side(bit) * n
        flying[p] = copy

    def arrive(p, step):
        flying[p].wait_recv()
        if step < bits - 1:
            half = sizes[p] >> (step + 2)
            mine = side(orders[p][step + 1])
            start = start_of(p, step + 1)
            _, value = sum_at(p, step, (1 - mine) * half, half)
            sbuf[start : start + half, :] = value.astype(BF16)
            launch(step + 1, p)
            at, value = sum_at(p, step, mine * half, half)
            acc[at, :] = value
            offs[p] = offs[p] + mine * half
        elif step == bits - 1:
            at, value = sum_at(p, step, 0, sizes[p] >> bits)
            gk_ref[at, :] = value.astype(BF16)
            spread(bits - 1, p)
        elif step + 1 < 2 * bits:
            spread(2 * bits - 2 - step, p)

    def taps(a, b, ready):
        if a == TAPS_A[-1] and b == 0:
            for r in range(S):
                take(past[1][r], xw.at[2, strip(r)], t > 1)
            put_input(2)
        res = jnp.dot(xt[2 - a], gw[b], preferred_element_type=F32)
        for c in range(3):
            at = ((a * 3 + b) * 3 + c) * chans
            acc[at : at + chans, :] = res[:, c * ce : (c + 1) * ce]
        for p in ready:
            begin(p)

    def put_gown(k):
        live = t + k < T
        if k == 0:
            value = gs[...].astype(F32)
        else:
            if k == 1:
                take(later[0], gh.at[0], live)
                later.append(push(gh.at[0], gh.at[1], behind, live & odd))
            else:
                take(later[1], gh.at[1], live & odd)
                take(later[2], gh.at[1], live & (lax.rem(t, 2) == 0))
            value = jnp.where(live, gh[k - 1].astype(F32), 0.0)
        fbuf[1 : rows + 1, 0:cols, :] = value
        take(rims[k][0], ge_in.at[k, 0], live & (s > 0))
        take(rims[k][1], ge_in.at[k, 1], live & (s + 1 < S))
        left = jnp.where(live & (s > 0), ge_in[k, 0].astype(F32), 0.0)
        right = jnp.where(live & (s < S - 1), ge_in[k, 1].astype(F32), 0.0)
        for h in range(rows):
            fbuf[h, pitch - 1 : pitch, :] = left[h : h + 1]
            fbuf[h + 1, cols : cols + 1, :] = right[h : h + 1]
        f = fbuf[...].reshape(flat_all, chans)
        for c, w in enumerate((pltpu.roll(f, flat_all - 1, 0), f, pltpu.roll(f, 1, 0))):
            gown[k, :, c * chans : (c + 1) * chans] = w.astype(BF16)

    counted = [0]

    def input_grad(a, b):
        if counted[0] == 0:
            load.wait()
        total = None if counted[0] == 0 else tot[...]
        for c in range(3):
            term = lax.dot_general(
                gown[2 - a, (2 - b) * pitch : (2 - b) * pitch + flat, c * chans : (c + 1) * chans],
                wbuf[a, b, c], (((1,), (1,)), ((), ())), preferred_element_type=F32,
            )
            total = term if total is None else total + term
        counted[0] += 1
        if counted[0] < 9:
            tot[...] = total
        else:
            gi_ref[0] = total.reshape(rows, pitch, chans)[:, 0:cols, :].astype(BF16)

    for task in plan(bits, sizes, orders, starts, ce * 2):
        if task[0] == "taps":
            taps(*task[1:])
        elif task[0] == "arrive":
            arrive(*task[1:])
        elif task[0] == "gown":
            put_gown(task[1])
        else:
            input_grad(*task[1:])

    for copy in copies:
        copy.wait_send()
    for copy, ok in sent:
        if ok is None:
            copy.wait_send()
        else:
            pl.when(ok)(copy.wait_send)
    for which in range(2):
        pltpu.make_async_copy(st_in.at[which], st_in.at[which], st_send.at[which]).wait()


def solution(mesh):
    T, S = mesh.shape["tm"], mesh.shape["space"]

    def shards(conv_input, conv_out, kernel, gain, bias, cotangent):
        _, rows, cols, chans = conv_out.shape
        width = cols * S
        ce = chans // S
        bits = T.bit_length() - 1
        groups = round_up(27 * chans, T * 16) // (T * 16)
        streams = min(STREAMS, groups)
        sizes = [(groups // streams + (p < groups % streams)) * T * 16 for p in range(streams)]
        total_rows = sum(sizes)
        pitch = round_up(cols + 2, 16)
        depth = round_up(rows * width, 128)
        fx_rows = (depth + width - 1) // width
        fg_rows = max(rows + 2, (2 * width + depth + width - 1) // width)
        n_bulk = (S - 1) * 2 + 2 * S + 3 + 6
        vmem = pl.BlockSpec(memory_space=pltpu.VMEM)
        whole = pl.BlockSpec(memory_space=pl.ANY)
        gi, gk, gg, gb = pl.pallas_call(
            functools.partial(body, T, S, sizes),
            out_shape=(
                jax.ShapeDtypeStruct(conv_input.shape, BF16),
                jax.ShapeDtypeStruct((total_rows, ce), BF16),
                jax.ShapeDtypeStruct((1, chans), F32),
                jax.ShapeDtypeStruct((1, chans), F32),
            ),
            in_specs=[whole, whole, whole, vmem, vmem, whole],
            out_specs=(vmem, vmem, vmem, vmem),
            scratch_shapes=[
                pltpu.VMEM((3, S, rows, cols, chans), BF16),
                pltpu.VMEM(conv_out.shape, BF16),
                pltpu.VMEM(cotangent.shape, BF16),
                pltpu.VMEM((S, 2, rows, cols, ce), BF16),
                pltpu.VMEM((S, 2, rows, cols, ce), BF16),
                pltpu.VMEM((2, 2 * chans // 128, 128), F32),
                pltpu.VMEM((2, T * S - 1, 2 * chans // 128, 128), F32),
                pltpu.VMEM((2, rows, cols, chans), F32),
                pltpu.VMEM((S, 2, rows, cols, ce), F32),
                pltpu.VMEM((fx_rows, width, chans), F32),
                pltpu.VMEM((fg_rows, width, ce), F32),
                pltpu.VMEM((rows + 2, pitch, chans), F32),
                pltpu.VMEM((rows, cols, chans), BF16),
                pltpu.VMEM((2, rows, cols, chans), BF16),
                pltpu.VMEM((2, rows, chans), BF16),
                pltpu.VMEM((3, 2, rows, chans), BF16),
                pltpu.VMEM((3, (rows + 2) * pitch, 3 * chans), BF16),
                pltpu.VMEM((3, depth, 3 * ce), BF16),
                pltpu.VMEM((3, chans, depth), BF16),
                pltpu.VMEM((3, 3, 3, chans, chans), BF16),
                pltpu.VMEM((rows * pitch, chans), F32),
                pltpu.VMEM((total_rows, ce), F32),
                pltpu.VMEM((total_rows, ce), BF16),
                pltpu.VMEM((total_rows, ce), BF16),
                pltpu.SemaphoreType.DMA((4,)),
                pltpu.SemaphoreType.DMA,
                pltpu.SemaphoreType.DMA((2,)),
                pltpu.SemaphoreType.DMA((2,)),
                pltpu.SemaphoreType.DMA((n_bulk,)),
                pltpu.SemaphoreType.DMA((n_bulk,)),
                pltpu.SemaphoreType.DMA((2, streams, bits)),
                pltpu.SemaphoreType.DMA((2, streams, bits)),
            ],
            compiler_params=pltpu.CompilerParams(
                collective_id=0, has_side_effects=True, vmem_limit_bytes=60 * 1024 * 1024
            ),
        )(conv_input, conv_out, kernel, gain.reshape(1, chans), bias.reshape(1, chans), cotangent)
        part_rows = 27 * chans // PARTS
        gi, gk, gg, gb = pl.pallas_call(
            hand_out,
            grid=(PARTS,),
            out_shape=(
                jax.ShapeDtypeStruct(gi.shape, BF16),
                jax.ShapeDtypeStruct((27 * chans, ce), F32),
                jax.ShapeDtypeStruct((1, chans), F32),
                jax.ShapeDtypeStruct((1, chans), F32),
            ),
            in_specs=[
                pl.BlockSpec(gi.shape, lambda i: (0, 0, 0, 0)),
                pl.BlockSpec((part_rows, ce), lambda i: (i, 0)),
                pl.BlockSpec((1, chans), lambda i: (0, 0)),
                pl.BlockSpec((1, chans), lambda i: (0, 0)),
            ],
            out_specs=(
                pl.BlockSpec(gi.shape, lambda i: (0, 0, 0, 0)),
                pl.BlockSpec((part_rows, ce), lambda i: (i, 0)),
                pl.BlockSpec((1, chans), lambda i: (0, 0)),
                pl.BlockSpec((1, chans), lambda i: (0, 0)),
            ),
        )(gi, gk, gg, gb)
        return gi, gk.reshape(3, 3, 3, chans, ce), gg.reshape(chans), gb.reshape(chans)

    strip = P("tm", None, "space", None)
    return jax.shard_map(
        shards,
        mesh=mesh,
        in_specs=(strip, strip, P(), P(), P(), strip),
        out_specs=(strip, P(None, None, None, None, "space"), P(), P()),
        check_vma=False,
    )
```

```python
import functools
import heapq

import jax
import jax.numpy as jnp
from jax import lax
from jax.experimental import pallas as pl
from jax.experimental.pallas import tpu as pltpu
from jax.sharding import PartitionSpec as P

GROUPS = 32
STREAMS = 13
PARTS = 2
EPSILON = 1e-06
MESH = pl.DeviceIdType.MESH
F32 = jnp.float32
BF16 = jnp.bfloat16


def round_up(value, unit):
    return (value + unit - 1) // unit * unit


def group_sum(x, width):
    lanes = x.shape[1]
    lane = lax.broadcasted_iota(jnp.int32, x.shape, 1)
    step = 1
    while step < width:
        up = pltpu.roll(x, lanes - step, 1)
        down = pltpu.roll(x, step, 1)
        x = x + jnp.where((lane // step) % 2 == 0, up, down)
        step *= 2
    return x


def hand_out(gi_in, gk_in, gg_in, gb_in, gi_out, gk_out, gg_out, gb_out):
    gk_out[...] = gk_in[...].astype(F32)

    @pl.when(pl.program_id(0) == 0)
    def _():
        gi_out[...] = gi_in[...]
        gg_out[...] = gg_in[...]
        gb_out[...] = gb_in[...]


TAPS_A = (2, 1, 0)
MATMUL = 0.36
FILLER = 0.36
ON_CHIP = (1.1, 200e3)
ON_LINK = (1.7, 46e3)
FAR = 0.75


def stage_orders(bits, streams):
    straight = list(range(bits))
    swapped = list(range(bits))
    if bits > 2:
        swapped[1], swapped[2] = swapped[2], swapped[1]
    return [swapped if p % 2 else straight for p in range(streams)]


def stream_starts(sizes, chans):
    done, begun, starts = set(), set(), []
    edges = [sum(sizes[:p]) for p in range(len(sizes) + 1)]
    for a in TAPS_A:
        for b in range(3):
            done.add(a * 3 + b)
            ready = []
            for p in range(len(sizes)):
                first, last = edges[p] // (3 * chans), (min(edges[p + 1], 27 * chans) - 1) // (3 * chans)
                if p not in begun and all(g in done for g in range(first, last + 1)):
                    begun.add(p)
                    ready.append(p)
            starts.append(((a, b), ready))
    return starts


def plan(bits, sizes, orders, starts, row_bytes):
    free = {}
    heap = []
    steps = 2 * bits

    def send(now, p, step):
        level = step if step < bits else steps - 1 - step
        rows = sizes[p] >> (level + 1)
        bit = orders[p][level]
        latency, rate = ON_CHIP if bit == 0 else ON_LINK
        time = rows * row_bytes / rate
        if bit > 2:
            latency, time = latency + FAR, 2 * time
        link = min(bit, 2)
        begin = max(now, free.get(link, 0.0))
        free[link] = begin + time
        heapq.heappush(heap, (begin + time + latency, step, p))

    matmuls = list(starts)
    fillers = [(0.0, ("gown", 0))] + [(0.0, ("input", 2, b)) for b in range(3)]
    fillers += [(7.0, ("gown", 1))] + [(0.0, ("input", 1, b)) for b in range(3)]
    fillers += [(11.0, ("gown", 2))] + [(0.0, ("input", 0, b)) for b in range(3)]
    tasks, now = [], 0.0
    while heap or matmuls or fillers:
        if heap and heap[0][0] <= now:
            _, step, p = heapq.heappop(heap)
            tasks.append(("arrive", p, step))
            now += 0.03 + 1.5e-4 * (sizes[p] >> (step + 1) if step < bits else 0)
            if step + 1 < steps:
                send(now, p, step + 1)
        elif matmuls:
            (a, b), ready = matmuls.pop(0)
            tasks.append(("taps", a, b, ready))
            now += MATMUL
            for p in ready:
                send(now, p, 0)
        elif fillers and fillers[0][0] <= now and (not heap or heap[0][0] - now >= 0.8 * FILLER):
            tasks.append(fillers.pop(0)[1])
            now += FILLER
        else:
            now = heap[0][0] if heap else fillers[0][0]
    return tasks


EVENTS = ((1.06, 0.31), (3.7, 0.72), (5.7, 0.73), (7.69, 0.73), (9.53, 0.71), (11.68, 0.76), (13.94, 1.05))
FILL_AT = (4.45, 12.45, 17.5)
FILL_STEP = 1.09
LINE = 4


def tree_plan(starts, streams):
    tasks, number = [], 0
    for i, ((a, b), ready) in enumerate(starts):
        tasks.append((i * MATMUL, ("taps", a, b, ready)))
        for p in ready:
            last = i * MATMUL
            for e, (first, step) in enumerate(EVENTS):
                last = max(last + 1e-3, first + step * number * 13 / streams)
                tasks.append((last, ("tree", p, e)))
            number += 1
    for k, a in enumerate(TAPS_A):
        tasks.append((FILL_AT[k], ("gown", k)))
        for b in range(3):
            tasks.append((FILL_AT[k] + (b + 1) * FILL_STEP, ("input", a, b)))
    return [task for _, task in sorted(tasks, key=lambda item: item[0])]


def body(
    T, S, sizes,
    x_hbm, co_hbm, k_hbm, gain_ref, bias_ref, ct_hbm,
    gi_ref, gk_ref, gg_ref, gb_ref,
    xw, co_ref, ct_ref, slice_out, cw, st_out, st_in, own, pre, fx, fg, fbuf,
    gs, gh, ge_out, ge_in, gown, gw, xt, wbuf, tot, acc, sbuf, rbuf, zbuf,
    in_sem, w_sem, st_send, st_recv, bulk_send, bulk_recv, rs_send, rs_recv, tree_send, tree_recv,
):
    N = T * S
    total_rows = sum(sizes)
    _, rows, cols, chans = co_ref.shape
    width = cols * S
    ce = chans // S
    depth = xt.shape[2]
    pitch = fbuf.shape[1]
    flat = rows * pitch
    flat_all = (rows + 2) * pitch
    halves = chans // 128
    t = lax.axis_index("tm")
    s = lax.axis_index("space")
    me = t * S + s

    loads = [
        pltpu.make_async_copy(src, dst, in_sem.at[i])
        for i, (src, dst) in enumerate(((co_hbm, co_ref), (ct_hbm, ct_ref), (x_hbm.at[0], xw.at[0, s])))
    ]
    for copy in loads:
        copy.start()
    load = pltpu.make_async_copy(k_hbm, wbuf, w_sem)
    load.start()

    barrier = pltpu.get_barrier_semaphore()

    def greet(r, carry):
        d = lax.rem(me + r, N)
        pl.semaphore_signal(barrier, inc=1, device_id=(d // S, lax.rem(d, S)), device_id_type=MESH)
        return carry

    lax.fori_loop(1, N, greet, 0)

    loads[0].wait()
    conv = co_ref[0].astype(F32)
    first = jnp.sum(jnp.sum(conv, axis=0), axis=0, keepdims=True)
    second = jnp.sum(jnp.sum(conv * conv, axis=0), axis=0, keepdims=True)

    def put_stats(which, one, two):
        for i in range(halves):
            st_out[which, i : i + 1, :] = one[:, i * 128 : (i + 1) * 128]
            st_out[which, halves + i : halves + i + 1, :] = two[:, i * 128 : (i + 1) * 128]

    def send_stats(which):
        def send(r, carry):
            r = 1 + lax.rem(r + N // 2 - 1, N - 1)
            d = lax.rem(me + r, N)
            pltpu.make_async_remote_copy(
                src_ref=st_out.at[which], dst_ref=st_in.at[which, r - 1],
                send_sem=st_send.at[which], recv_sem=st_recv.at[which],
                device_id=(d // S, lax.rem(d, S)), device_id_type=MESH,
            ).start()
            return carry

        lax.fori_loop(1, N, send, 0)

    def take_stats(which):
        pltpu.make_async_copy(st_in.at[which], st_in.at[which], st_recv.at[which]).wait()
        return jnp.sum(st_in[which], axis=0) + st_out[which]

    put_stats(0, first, second)
    loads[1].wait()
    loads[2].wait()
    for arr, ref in ((0, co_ref), (1, ct_ref)):
        whole = ref[0]
        for j in range(S):
            slice_out[j, arr] = whole[:, :, j * ce : (j + 1) * ce]
    keep = pltpu.make_async_copy(slice_out.at[s], cw.at[s], in_sem.at[3])
    keep.start()
    pl.semaphore_wait(barrier, N - 1)
    send_stats(0)

    sent = []

    def push(src, dst, device, ok=None, now=None):
        i = len(sent)
        copy = pltpu.make_async_remote_copy(
            src_ref=src, dst_ref=dst, send_sem=bulk_send.at[i], recv_sem=bulk_recv.at[i],
            device_id=device, device_id_type=MESH,
        )
        if ok is None:
            copy.start()
        else:
            pl.when(ok if now is None else now)(copy.start)
        sent.append((copy, ok))
        return i

    def take(i, dst, ok=None):
        copy = pltpu.make_async_copy(dst, dst, bulk_recv.at[i])
        if ok is None:
            copy.wait()
        else:
            pl.when(ok)(copy.wait)

    def frame(n):
        return lax.rem(t + T + n, T)

    def strip(n):
        return lax.rem(s + S + n, S)

    ahead = (frame(1), s)
    behind = (frame(-1), s)
    has_next, has_before = t + 1 < T, t > 0
    cut, mate, past = [], [], [[], []]
    past[0].append(push(xw.at[0, s], xw.at[1, s], ahead, has_next))
    for r in range(1, S):
        mate.append(push(xw.at[0, s], xw.at[0, s], (t, strip(-r))))
    for r in range(1, S):
        cut.append(push(slice_out.at[strip(-r)], cw.at[s], (t, strip(-r))))

    odd = lax.rem(t, 2) == 1
    even = lax.rem(t, 2) == 0

    def relay_near(r):
        take(mate[r - 1], xw.at[0, strip(r)])
        past[0].append(push(xw.at[0, strip(r)], xw.at[1, strip(r)], ahead, has_next))

    def relay_far(r, when):
        take(past[0][r], xw.at[1, strip(r)], has_before & when)
        ok = has_next & has_before
        if r < len(past[1]):
            pl.when(ok & when)(sent[past[1][r]][0].start)
        else:
            past[1].append(push(xw.at[1, strip(r)], xw.at[2, strip(r)], ahead, ok, ok & when))

    fx[...] = jnp.zeros_like(fx)
    fg[...] = jnp.zeros_like(fg)
    fbuf[...] = jnp.zeros_like(fbuf)
    if total_rows > 27 * chans:
        acc[27 * chans :, :] = jnp.zeros((total_rows - 27 * chans, ce), F32)

    gain = gain_ref[...]
    bias = bias_ref[...]
    group = chans // GROUPS
    count = rows * width * T * group
    relay_far(0, odd)
    relay_far(0, even)
    sums = take_stats(0)
    grouped = group_sum(sums, group)
    mean2 = grouped[:halves] / count
    inv2 = lax.rsqrt(grouped[halves:] / count - mean2 * mean2 + EPSILON)

    def wide(two):
        return jnp.concatenate([two[i : i + 1] for i in range(halves)], axis=1)

    mean, inv = wide(mean2), wide(inv2)

    def shift_grad(conv, cot, mean, inv, gain, bias):
        normed = (conv.astype(F32) - mean) * inv
        shifted = normed * gain + bias
        sigma = jax.nn.sigmoid(shifted)
        return normed, cot.astype(F32) * sigma * (1.0 + shifted * (1.0 - sigma))

    normed, grad = shift_grad(co_ref[0], ct_ref[0], mean, inv, gain, bias)
    own[0] = normed
    own[1] = grad
    put_stats(
        1,
        jnp.sum(jnp.sum(grad, axis=0), axis=0, keepdims=True),
        jnp.sum(jnp.sum(grad * normed, axis=0), axis=0, keepdims=True),
    )
    send_stats(1)

    def part(v):
        out = v[..., 0:ce]
        for j in range(1, S):
            out = jnp.where(s == j, v[..., j * ce : (j + 1) * ce], out)
        return out

    for r in range(1, S):
        relay_near(r)
    for r in range(1, S):
        relay_far(r, odd)
    for r in range(1, S):
        take(cut[r - 1], cw.at[strip(r)])
    keep.wait()
    firsts = tuple(part(p) for p in (mean, inv, gain, bias))
    for j in range(S):
        normed, grad = shift_grad(cw[j, 0], cw[j, 1], *firsts)
        pre[j, 0] = normed
        pre[j, 1] = grad

    def put_input(k):
        for j in range(S):
            value = xw[k, j].astype(F32)
            if k > 0:
                value = jnp.where(t >= k, value, 0.0)
            fx[0:rows, j * cols : (j + 1) * cols, :] = value
        placed = fx[...].reshape(fx.shape[0] * fx.shape[1], chans)[0:depth]
        xt[k] = jnp.transpose(placed).astype(BF16)

    put_input(0)
    for r in range(1, S):
        relay_far(r, even)
    put_input(1)
    sums = take_stats(1)
    chan_bias, chan_gain = wide(sums[:halves]), wide(sums[halves:])
    gb_ref[...] = chan_bias
    gg_ref[...] = chan_gain
    gain2 = jnp.concatenate([gain[:, i * 128 : (i + 1) * 128] for i in range(halves)], axis=0)
    plain = wide(group_sum(sums[:halves] * gain2, group)) / count
    product = wide(group_sum(sums[halves:] * gain2, group)) / count

    def conv_grad(normed, grad, inv, gain, plain, product):
        return inv * (grad * gain - plain - normed * product)

    g = conv_grad(own[0], own[1], inv, gain, plain, product)
    gs[...] = g.astype(BF16)
    for h in range(rows):
        ge_out[0, h : h + 1, :] = g[h, 0:1, :].astype(BF16)
        ge_out[1, h : h + 1, :] = g[h, cols - 1 : cols, :].astype(BF16)
    later = [
        push(gs, gh.at[0], behind, has_before),
        push(gs, gh.at[1], (frame(-2), s), odd & (t > 1)),
    ]
    rims = []
    for k in range(3):
        back = (frame(-k), strip(1)), (frame(-k), strip(-1))
        rims.append((
            push(ge_out.at[1], ge_in.at[k, 0], back[0], (t >= k) & (s + 1 < S)),
            push(ge_out.at[0], ge_in.at[k, 1], back[1], (t >= k) & (s > 0)),
        ))

    seconds = tuple(part(p) for p in (inv, gain, plain, product))
    for j in range(S):
        fg[1 : rows + 1, j * cols : (j + 1) * cols, :] = conv_grad(pre[j, 0], pre[j, 1], *seconds)
    tall = fg.shape[0] * width
    f = fg[...].reshape(tall, ce)
    column = lax.broadcasted_iota(jnp.int32, fg.shape, 1).reshape(tall, ce)
    moved = (
        jnp.where(column < width - 1, pltpu.roll(f, tall - 1, 0), 0.0),
        f,
        jnp.where(column > 0, pltpu.roll(f, 1, 0), 0.0),
    )
    for c, w in enumerate(moved):
        for b in range(3):
            gw[b, :, c * ce : (c + 1) * ce] = w[(2 - b) * width : (2 - b) * width + depth].astype(BF16)

    bits = T.bit_length() - 1
    streams = len(sizes)
    orders = stage_orders(bits, streams)
    starts = stream_starts(sizes, chans)
    bases = [sum(sizes[:p]) for p in range(streams)]
    offs = [0] * streams
    flying = [None] * streams
    copies = []

    def side(bit):
        return lax.rem(t // (2**bit), 2)

    def partner(bit):
        return (t + (1 - 2 * side(bit)) * 2**bit, s)

    def span(p, off, n):
        return pl.ds(pl.multiple_of(bases[p] + off, 16), n)

    def start_of(p, i):
        return bases[p] + sizes[p] - (sizes[p] >> i)

    def launch(i, p):
        half = sizes[p] >> (i + 1)
        start = start_of(p, i)
        copy = pltpu.make_async_remote_copy(
            src_ref=sbuf.at[start : start + half], dst_ref=rbuf.at[start : start + half],
            send_sem=rs_send.at[0, p, i], recv_sem=rs_recv.at[0, p, i],
            device_id=partner(orders[p][i]), device_id_type=MESH,
        )
        copy.start()
        copies.append(copy)
        flying[p] = copy

    tree = T == 4 * LINE
    z, x, core = t // 4, lax.rem(t // 2, 2), lax.rem(t, 2)
    side_z = z // 2
    inner = (z == 1) | (z == 2)
    outer = (z == 0) | (z == 3)
    toward = jnp.where(inner, z - 1 + 2 * side_z, z + 1 - 2 * side_z)
    mates = {
        "core": (t + 1 - 2 * core, s),
        "x": (t + 2 - 4 * x, s),
        "line": (toward * 4 + lax.rem(t, 4), s),
        "middle": (lax.rem(3 - z + T, T) * 4 + lax.rem(t, 4), s),
    }
    slots = {"c0": 0, "x0": 1, "z0": 2, "z1": 3, "a2b": 3, "a1": 4, "a2a": 4, "x1": 5}

    def tree_push(p, kind, src, dst, device):
        by_role = kind in ("z0", "z1", "a1", "a2a", "a2b")
        pltpu.make_async_remote_copy(
            src_ref=src, dst_ref=dst, send_sem=tree_send.at[int(by_role)],
            recv_sem=tree_send.at[2] if kind == "c1" else tree_recv.at[p, slots[kind]],
            device_id=device, device_id_type=MESH,
        ).start()

    def tree_wait(p, kind, ref):
        pltpu.make_async_copy(ref, ref, tree_recv.at[p, slots[kind]]).wait()

    def places(p):
        half, n, h = sizes[p] // 2, sizes[p] // 4, sizes[p] // 8
        mine = core * half + x * n
        apart = core * half + (1 - x) * n
        return half, n, h, mine, apart

    def rows_of(ref, p, off, n):
        return ref.at[span(p, off, n)]

    def tree_event(p, e):
        half, n, h, mine, apart = places(p)
        base = bases[p]
        near, far = mine + side_z * h, mine + (1 - side_z) * h
        at_x, at_z = half, half + n
        zrow = pl.ds(base // 8, h)

        def taken(ref, off, rows):
            return ref[span(p, off, rows), :]

        def put_half(kind, off, device):
            tree_push(p, kind, rows_of(gk_ref, p, off, h), rows_of(gk_ref, p, off, h), device)

        def put_whole(kind, off):
            tree_push(p, kind, rows_of(gk_ref, p, off, n), rows_of(gk_ref, p, off, n), mates["core"])

        if e == 0:
            tree_wait(p, "c0", rows_of(rbuf, p, 0, half))
            value = taken(acc, apart, n) + taken(rbuf, (1 - x) * n, n).astype(F32)
            sbuf[span(p, at_x, n), :] = value.astype(BF16)
            tree_push(p, "x0", rows_of(sbuf, p, at_x, n), rows_of(rbuf, p, at_x, n), mates["x"])
            acc[span(p, mine, n), :] = taken(acc, mine, n) + taken(rbuf, x * n, n).astype(F32)
        elif e == 1:
            tree_wait(p, "x0", rows_of(rbuf, p, at_x, n))

            @pl.when(outer)
            def _():
                value = taken(acc, mine, n) + taken(rbuf, at_x, n).astype(F32)
                sbuf[span(p, at_z, n), :] = value.astype(BF16)
                tree_push(p, "z0", rows_of(sbuf, p, at_z, n), rows_of(rbuf, p, at_z, n), mates["line"])

            @pl.when(inner)
            def _():
                acc[span(p, mine, n), :] = taken(acc, mine, n) + taken(rbuf, at_x, n).astype(F32)
        elif e == 2:
            @pl.when(inner)
            def _():
                tree_wait(p, "z0", rows_of(rbuf, p, at_z, n))
                value = taken(acc, far, h) + taken(rbuf, at_z + (1 - side_z) * h, h).astype(F32)
                sbuf[span(p, at_z, h), :] = value.astype(BF16)
                tree_push(p, "z1", rows_of(sbuf, p, at_z, h), zbuf.at[zrow], mates["middle"])
                acc[span(p, near, h), :] = taken(acc, near, h) + taken(rbuf, at_z + side_z * h, h).astype(F32)
        elif e == 3:
            @pl.when(inner)
            def _():
                tree_wait(p, "z1", zbuf.at[zrow])
                gk_ref[span(p, near, h), :] = (taken(acc, near, h) + zbuf[zrow, :].astype(F32)).astype(BF16)
                put_half("x1", near, mates["x"])
                put_half("a1", near, mates["middle"])
                put_half("a2a", near, mates["line"])
        elif e == 4:
            @pl.when(inner)
            def _():
                tree_wait(p, "a1", rows_of(gk_ref, p, far, h))
                put_half("x1", far, mates["x"])
                put_half("a2b", far, mates["line"])
                put_whole("c1", mine)

            @pl.when(outer)
            def _():
                tree_wait(p, "a2a", rows_of(gk_ref, p, near, h))
                put_half("x1", near, mates["x"])
        elif e == 5:
            @pl.when(outer)
            def _():
                tree_wait(p, "a2b", rows_of(gk_ref, p, far, h))
                put_half("x1", far, mates["x"])
                put_whole("c1", mine)
        else:
            tree_wait(p, "x1", rows_of(gk_ref, p, apart, n))
            put_whole("c1", apart)

    def tree_end():
        for ref, i in ((gk_ref.at[0 : total_rows // 2], 2), (acc.at[0 : total_rows * 3 // 4], 0)):
            pltpu.make_async_copy(ref, ref, tree_send.at[i]).wait()

        @pl.when(outer)
        def _():
            pltpu.make_async_copy(sbuf.at[0 : total_rows // 4], sbuf.at[0 : total_rows // 4], tree_send.at[1]).wait()

        @pl.when(inner)
        def _():
            pltpu.make_async_copy(sbuf.at[0 : total_rows // 2], sbuf.at[0 : total_rows // 2], tree_send.at[1]).wait()

    def begin(p):
        half = sizes[p] >> 1
        mine = side(orders[p][0])
        start = start_of(p, 0)
        sbuf[start : start + half, :] = acc[span(p, (1 - mine) * half, half), :].astype(BF16)
        if tree:
            tree_push(p, "c0", sbuf.at[start : start + half], rbuf.at[start : start + half], mates["core"])
            return
        launch(0, p)
        offs[p] = mine * half

    def sum_at(p, i, off, n):
        at = span(p, offs[p] + off, n)
        seen = pl.ds(pl.multiple_of(start_of(p, i) + off, 16), n)
        return at, acc[at, :] + rbuf[seen, :].astype(F32)

    def spread(i, p):
        n = sizes[p] >> (i + 1)
        bit = orders[p][i]
        at = span(p, offs[p], n)
        copy = pltpu.make_async_remote_copy(
            src_ref=gk_ref.at[at], dst_ref=gk_ref.at[at],
            send_sem=rs_send.at[1, p, i], recv_sem=rs_recv.at[1, p, i],
            device_id=partner(bit), device_id_type=MESH,
        )
        copy.start()
        copies.append(copy)
        offs[p] = offs[p] - side(bit) * n
        flying[p] = copy

    def arrive(p, step):
        flying[p].wait_recv()
        if step < bits - 1:
            half = sizes[p] >> (step + 2)
            mine = side(orders[p][step + 1])
            start = start_of(p, step + 1)
            _, value = sum_at(p, step, (1 - mine) * half, half)
            sbuf[start : start + half, :] = value.astype(BF16)
            launch(step + 1, p)
            at, value = sum_at(p, step, mine * half, half)
            acc[at, :] = value
            offs[p] = offs[p] + mine * half
        elif step == bits - 1:
            at, value = sum_at(p, step, 0, sizes[p] >> bits)
            gk_ref[at, :] = value.astype(BF16)
            spread(bits - 1, p)
        elif step + 1 < 2 * bits:
            spread(2 * bits - 2 - step, p)

    def taps(a, b, ready):
        if a == TAPS_A[-1] and b == 0:
            for r in range(S):
                take(past[1][r], xw.at[2, strip(r)], t > 1)
            put_input(2)
        res = jnp.dot(xt[2 - a], gw[b], preferred_element_type=F32)
        for c in range(3):
            at = ((a * 3 + b) * 3 + c) * chans
            acc[at : at + chans, :] = res[:, c * ce : (c + 1) * ce]
        for p in ready:
            begin(p)

    def put_gown(k):
        live = t + k < T
        if k == 0:
            value = gs[...].astype(F32)
        else:
            if k == 1:
                take(later[0], gh.at[0], live)
                later.append(push(gh.at[0], gh.at[1], behind, live & odd))
            else:
                take(later[1], gh.at[1], live & odd)
                take(later[2], gh.at[1], live & (lax.rem(t, 2) == 0))
            value = jnp.where(live, gh[k - 1].astype(F32), 0.0)
        fbuf[1 : rows + 1, 0:cols, :] = value
        take(rims[k][0], ge_in.at[k, 0], live & (s > 0))
        take(rims[k][1], ge_in.at[k, 1], live & (s + 1 < S))
        left = jnp.where(live & (s > 0), ge_in[k, 0].astype(F32), 0.0)
        right = jnp.where(live & (s < S - 1), ge_in[k, 1].astype(F32), 0.0)
        for h in range(rows):
            fbuf[h, pitch - 1 : pitch, :] = left[h : h + 1]
            fbuf[h + 1, cols : cols + 1, :] = right[h : h + 1]
        f = fbuf[...].reshape(flat_all, chans)
        for c, w in enumerate((pltpu.roll(f, flat_all - 1, 0), f, pltpu.roll(f, 1, 0))):
            gown[k, :, c * chans : (c + 1) * chans] = w.astype(BF16)

    counted = [0]

    def input_grad(a, b):
        if counted[0] == 0:
            load.wait()
        total = None if counted[0] == 0 else tot[...]
        for c in range(3):
            term = lax.dot_general(
                gown[2 - a, (2 - b) * pitch : (2 - b) * pitch + flat, c * chans : (c + 1) * chans],
                wbuf[a, b, c], (((1,), (1,)), ((), ())), preferred_element_type=F32,
            )
            total = term if total is None else total + term
        counted[0] += 1
        if counted[0] < 9:
            tot[...] = total
        else:
            gi_ref[0] = total.reshape(rows, pitch, chans)[:, 0:cols, :].astype(BF16)

    tasks = tree_plan(starts, streams) if tree else plan(bits, sizes, orders, starts, ce * 2)
    for task in tasks:
        if task[0] == "taps":
            taps(*task[1:])
        elif task[0] == "arrive":
            arrive(*task[1:])
        elif task[0] == "tree":
            tree_event(*task[1:])
        elif task[0] == "gown":
            put_gown(task[1])
        else:
            input_grad(*task[1:])
    if tree:
        tree_end()

    for copy in copies:
        copy.wait_send()
    for copy, ok in sent:
        if ok is None:
            copy.wait_send()
        else:
            pl.when(ok)(copy.wait_send)
    for which in range(2):
        pltpu.make_async_copy(st_in.at[which], st_in.at[which], st_send.at[which]).wait()


def solution(mesh):
    T, S = mesh.shape["tm"], mesh.shape["space"]

    def shards(conv_input, conv_out, kernel, gain, bias, cotangent):
        _, rows, cols, chans = conv_out.shape
        width = cols * S
        ce = chans // S
        bits = T.bit_length() - 1
        groups = round_up(27 * chans, T * 16) // (T * 16)
        streams = min(STREAMS, groups)
        sizes = [(groups // streams + (p < groups % streams)) * T * 16 for p in range(streams)]
        total_rows = sum(sizes)
        pitch = round_up(cols + 2, 16)
        depth = round_up(rows * width, 128)
        fx_rows = (depth + width - 1) // width
        fg_rows = max(rows + 2, (2 * width + depth + width - 1) // width)
        n_bulk = (S - 1) * 2 + 2 * S + 3 + 6
        tree = T == 4 * LINE
        halving, line = ((1, 1, 1), (streams, 6)) if tree else ((2, streams, bits), (1, 1))
        vmem = pl.BlockSpec(memory_space=pltpu.VMEM)
        whole = pl.BlockSpec(memory_space=pl.ANY)
        gi, gk, gg, gb = pl.pallas_call(
            functools.partial(body, T, S, sizes),
            out_shape=(
                jax.ShapeDtypeStruct(conv_input.shape, BF16),
                jax.ShapeDtypeStruct((total_rows, ce), BF16),
                jax.ShapeDtypeStruct((1, chans), F32),
                jax.ShapeDtypeStruct((1, chans), F32),
            ),
            in_specs=[whole, whole, whole, vmem, vmem, whole],
            out_specs=(vmem, vmem, vmem, vmem),
            scratch_shapes=[
                pltpu.VMEM((3, S, rows, cols, chans), BF16),
                pltpu.VMEM(conv_out.shape, BF16),
                pltpu.VMEM(cotangent.shape, BF16),
                pltpu.VMEM((S, 2, rows, cols, ce), BF16),
                pltpu.VMEM((S, 2, rows, cols, ce), BF16),
                pltpu.VMEM((2, 2 * chans // 128, 128), F32),
                pltpu.VMEM((2, T * S - 1, 2 * chans // 128, 128), F32),
                pltpu.VMEM((2, rows, cols, chans), F32),
                pltpu.VMEM((S, 2, rows, cols, ce), F32),
                pltpu.VMEM((fx_rows, width, chans), F32),
                pltpu.VMEM((fg_rows, width, ce), F32),
                pltpu.VMEM((rows + 2, pitch, chans), F32),
                pltpu.VMEM((rows, cols, chans), BF16),
                pltpu.VMEM((2, rows, cols, chans), BF16),
                pltpu.VMEM((2, rows, chans), BF16),
                pltpu.VMEM((3, 2, rows, chans), BF16),
                pltpu.VMEM((3, (rows + 2) * pitch, 3 * chans), BF16),
                pltpu.VMEM((3, depth, 3 * ce), BF16),
                pltpu.VMEM((3, chans, depth), BF16),
                pltpu.VMEM((3, 3, 3, chans, chans), BF16),
                pltpu.VMEM((rows * pitch, chans), F32),
                pltpu.VMEM((total_rows, ce), F32),
                pltpu.VMEM((total_rows, ce), BF16),
                pltpu.VMEM((total_rows, ce), BF16),
                pltpu.VMEM((total_rows // 8, ce), BF16),
                pltpu.SemaphoreType.DMA((4,)),
                pltpu.SemaphoreType.DMA,
                pltpu.SemaphoreType.DMA((2,)),
                pltpu.SemaphoreType.DMA((2,)),
                pltpu.SemaphoreType.DMA((n_bulk,)),
                pltpu.SemaphoreType.DMA((n_bulk,)),
                pltpu.SemaphoreType.DMA(halving),
                pltpu.SemaphoreType.DMA(halving),
                pltpu.SemaphoreType.DMA((3,)),
                pltpu.SemaphoreType.DMA(line),
            ],
            compiler_params=pltpu.CompilerParams(
                collective_id=0, has_side_effects=True, vmem_limit_bytes=60 * 1024 * 1024
            ),
        )(conv_input, conv_out, kernel, gain.reshape(1, chans), bias.reshape(1, chans), cotangent)
        part_rows = 27 * chans // PARTS
        gi, gk, gg, gb = pl.pallas_call(
            hand_out,
            grid=(PARTS,),
            out_shape=(
                jax.ShapeDtypeStruct(gi.shape, BF16),
                jax.ShapeDtypeStruct((27 * chans, ce), F32),
                jax.ShapeDtypeStruct((1, chans), F32),
                jax.ShapeDtypeStruct((1, chans), F32),
            ),
            in_specs=[
                pl.BlockSpec(gi.shape, lambda i: (0, 0, 0, 0)),
                pl.BlockSpec((part_rows, ce), lambda i: (i, 0)),
                pl.BlockSpec((1, chans), lambda i: (0, 0)),
                pl.BlockSpec((1, chans), lambda i: (0, 0)),
            ],
            out_specs=(
                pl.BlockSpec(gi.shape, lambda i: (0, 0, 0, 0)),
                pl.BlockSpec((part_rows, ce), lambda i: (i, 0)),
                pl.BlockSpec((1, chans), lambda i: (0, 0)),
                pl.BlockSpec((1, chans), lambda i: (0, 0)),
            ),
        )(gi, gk, gg, gb)
        return gi, gk.reshape(3, 3, 3, chans, ce), gg.reshape(chans), gb.reshape(chans)

    strip = P("tm", None, "space", None)
    return jax.shard_map(
        shards,
        mesh=mesh,
        in_specs=(strip, strip, P(), P(), P(), strip),
        out_specs=(strip, P(None, None, None, None, "space"), P(), P()),
        check_vma=False,
    )
```

```python
import functools
import heapq

import jax
import jax.numpy as jnp
from jax import lax
from jax.experimental import pallas as pl
from jax.experimental.pallas import tpu as pltpu
from jax.sharding import PartitionSpec as P

GROUPS = 32
STREAMS = 13
PARTS = 3
EPSILON = 1e-06
MESH = pl.DeviceIdType.MESH
F32 = jnp.float32
BF16 = jnp.bfloat16


def round_up(value, unit):
    return (value + unit - 1) // unit * unit


def group_sum(x, width):
    lanes = x.shape[1]
    lane = lax.broadcasted_iota(jnp.int32, x.shape, 1)
    step = 1
    while step < width:
        up = pltpu.roll(x, lanes - step, 1)
        down = pltpu.roll(x, step, 1)
        x = x + jnp.where((lane // step) % 2 == 0, up, down)
        step *= 2
    return x


def hand_out(gi_in, gk_in, gg_in, gb_in, gi_out, gk_out, gg_out, gb_out, wide, sems):
    rows = gk_out.shape[0] // PARTS
    copies = [pltpu.make_async_copy(gi_in, gi_out, sems.at[PARTS])]
    copies[0].start()
    for i in range(PARTS):
        at = slice(i * rows, (i + 1) * rows)
        wide[at, :] = gk_in[at, :].astype(F32)
        copies.append(pltpu.make_async_copy(wide.at[at], gk_out.at[at], sems.at[i]))
        copies[-1].start()
    gg_out[...] = gg_in[...]
    gb_out[...] = gb_in[...]
    for copy in copies:
        copy.wait()


TAPS_A = (2, 1, 0)
MATMUL = 0.36
FILLER = 0.36
ON_CHIP = (1.1, 200e3)
ON_LINK = (1.7, 46e3)
FAR = 0.75


def stage_orders(bits, streams):
    straight = list(range(bits))
    swapped = list(range(bits))
    if bits > 2:
        swapped[1], swapped[2] = swapped[2], swapped[1]
    return [swapped if p % 2 else straight for p in range(streams)]


def stream_starts(sizes, chans):
    done, begun, starts = set(), set(), []
    edges = [sum(sizes[:p]) for p in range(len(sizes) + 1)]
    for a in TAPS_A:
        for b in range(3):
            done.add(a * 3 + b)
            ready = []
            for p in range(len(sizes)):
                first, last = edges[p] // (3 * chans), (min(edges[p + 1], 27 * chans) - 1) // (3 * chans)
                if p not in begun and all(g in done for g in range(first, last + 1)):
                    begun.add(p)
                    ready.append(p)
            starts.append(((a, b), ready))
    return starts


def plan(bits, sizes, orders, starts, row_bytes):
    free = {}
    heap = []
    steps = 2 * bits

    def send(now, p, step):
        level = step if step < bits else steps - 1 - step
        rows = sizes[p] >> (level + 1)
        bit = orders[p][level]
        latency, rate = ON_CHIP if bit == 0 else ON_LINK
        time = rows * row_bytes / rate
        if bit > 2:
            latency, time = latency + FAR, 2 * time
        link = min(bit, 2)
        begin = max(now, free.get(link, 0.0))
        free[link] = begin + time
        heapq.heappush(heap, (begin + time + latency, step, p))

    matmuls = list(starts)
    fillers = [(0.0, ("gown", 0))] + [(0.0, ("input", 2, b)) for b in range(3)]
    fillers += [(7.0, ("gown", 1))] + [(0.0, ("input", 1, b)) for b in range(3)]
    fillers += [(11.0, ("gown", 2))] + [(0.0, ("input", 0, b)) for b in range(3)]
    tasks, now = [], 0.0
    while heap or matmuls or fillers:
        if heap and heap[0][0] <= now:
            _, step, p = heapq.heappop(heap)
            tasks.append(("arrive", p, step))
            now += 0.03 + 1.5e-4 * (sizes[p] >> (step + 1) if step < bits else 0)
            if step + 1 < steps:
                send(now, p, step + 1)
        elif matmuls:
            (a, b), ready = matmuls.pop(0)
            tasks.append(("taps", a, b, ready))
            now += MATMUL
            for p in ready:
                send(now, p, 0)
        elif fillers and fillers[0][0] <= now and (not heap or heap[0][0] - now >= 0.8 * FILLER):
            tasks.append(fillers.pop(0)[1])
            now += FILLER
        else:
            now = heap[0][0] if heap else fillers[0][0]
    return tasks


EVENTS = ((1.06, 0.31), (3.7, 0.72), (5.7, 0.73), (7.69, 0.73), (9.53, 0.71), (11.68, 0.76), (13.94, 1.05))
FILL_AT = (4.45, 12.45, 17.5)
FILL_STEP = 1.09
LINE = 4


def tree_plan(starts, streams):
    tasks, number = [], 0
    for i, ((a, b), ready) in enumerate(starts):
        tasks.append((i * MATMUL, ("taps", a, b, ready)))
        for p in ready:
            last = i * MATMUL
            for e, (first, step) in enumerate(EVENTS):
                last = max(last + 1e-3, first + step * number * 13 / streams)
                tasks.append((last, ("tree", p, e)))
            number += 1
    for k, a in enumerate(TAPS_A):
        tasks.append((FILL_AT[k], ("gown", k)))
        for b in range(3):
            tasks.append((FILL_AT[k] + (b + 1) * FILL_STEP, ("input", a, b)))
    return [task for _, task in sorted(tasks, key=lambda item: item[0])]


def body(
    T, S, sizes,
    x_hbm, co_hbm, k_hbm, gain_ref, bias_ref, ct_hbm,
    gi_ref, gk_ref, gg_ref, gb_ref,
    xw, co_ref, ct_ref, slice_out, cw, st_out, st_in, own, pre, fx, fg, fbuf,
    gflat, gs, gr, gh, ge_out, ge_in, gown, gw, xt, wbuf, tot, acc, sbuf, rbuf, zbuf,
    in_sem, w_sem, st_send, st_recv, bulk_send, bulk_recv, rs_send, rs_recv, tree_send, tree_recv,
):
    N = T * S
    total_rows = sum(sizes)
    _, rows, cols, chans = co_ref.shape
    width = cols * S
    ce = chans // S
    depth = xt.shape[2]
    pitch = fbuf.shape[1]
    flat = rows * pitch
    flat_all = (rows + 2) * pitch
    halves = chans // 128
    t = lax.axis_index("tm")
    s = lax.axis_index("space")
    me = t * S + s

    loads = [
        pltpu.make_async_copy(src, dst, in_sem.at[i])
        for i, (src, dst) in enumerate(((co_hbm, co_ref), (ct_hbm, ct_ref), (x_hbm.at[0], xw.at[0, s])))
    ]
    for copy in loads:
        copy.start()
    load = pltpu.make_async_copy(k_hbm, wbuf, w_sem)
    load.start()

    barrier = pltpu.get_barrier_semaphore()

    def greet(r, carry):
        d = lax.rem(me + r, N)
        pl.semaphore_signal(barrier, inc=1, device_id=(d // S, lax.rem(d, S)), device_id_type=MESH)
        return carry

    lax.fori_loop(1, N, greet, 0)

    loads[0].wait()
    conv = co_ref[0].astype(F32)
    first = jnp.sum(jnp.sum(conv, axis=0), axis=0, keepdims=True)
    second = jnp.sum(jnp.sum(conv * conv, axis=0), axis=0, keepdims=True)

    def put_stats(which, one, two):
        for i in range(halves):
            st_out[which, i : i + 1, :] = one[:, i * 128 : (i + 1) * 128]
            st_out[which, halves + i : halves + i + 1, :] = two[:, i * 128 : (i + 1) * 128]

    def send_stats(which):
        def send(r, carry):
            r = 1 + lax.rem(r + N // 2 - 1, N - 1)
            d = lax.rem(me + r, N)
            pltpu.make_async_remote_copy(
                src_ref=st_out.at[which], dst_ref=st_in.at[which, r - 1],
                send_sem=st_send.at[which], recv_sem=st_recv.at[which],
                device_id=(d // S, lax.rem(d, S)), device_id_type=MESH,
            ).start()
            return carry

        lax.fori_loop(1, N, send, 0)

    def take_stats(which):
        pltpu.make_async_copy(st_in.at[which], st_in.at[which], st_recv.at[which]).wait()
        return jnp.sum(st_in[which], axis=0) + st_out[which]

    put_stats(0, first, second)
    loads[1].wait()
    loads[2].wait()
    for arr, ref in ((0, co_ref), (1, ct_ref)):
        whole = ref[0]
        for j in range(S):
            slice_out[j, arr] = whole[:, :, j * ce : (j + 1) * ce]
    keep = pltpu.make_async_copy(slice_out.at[s], cw.at[s], in_sem.at[3])
    keep.start()
    pl.semaphore_wait(barrier, N - 1)
    send_stats(0)

    sent = []

    def push(src, dst, device, ok=None, now=None):
        i = len(sent)
        copy = pltpu.make_async_remote_copy(
            src_ref=src, dst_ref=dst, send_sem=bulk_send.at[i], recv_sem=bulk_recv.at[i],
            device_id=device, device_id_type=MESH,
        )
        if ok is None:
            copy.start()
        else:
            pl.when(ok if now is None else now)(copy.start)
        sent.append((copy, ok))
        return i

    def take(i, dst, ok=None):
        copy = pltpu.make_async_copy(dst, dst, bulk_recv.at[i])
        if ok is None:
            copy.wait()
        else:
            pl.when(ok)(copy.wait)

    def frame(n):
        return lax.rem(t + T + n, T)

    def strip(n):
        return lax.rem(s + S + n, S)

    ahead = (frame(1), s)
    behind = (frame(-1), s)
    has_next, has_before = t + 1 < T, t > 0
    cut, mate, past = [], [], [[], []]
    past[0].append(push(xw.at[0, s], xw.at[1, s], ahead, has_next))
    for r in range(1, S):
        mate.append(push(xw.at[0, s], xw.at[0, s], (t, strip(-r))))
    for r in range(1, S):
        cut.append(push(slice_out.at[strip(-r)], cw.at[s], (t, strip(-r))))

    odd = lax.rem(t, 2) == 1
    even = lax.rem(t, 2) == 0

    def relay_near(r):
        take(mate[r - 1], xw.at[0, strip(r)])
        past[0].append(push(xw.at[0, strip(r)], xw.at[1, strip(r)], ahead, has_next))

    def relay_far(r, when):
        take(past[0][r], xw.at[1, strip(r)], has_before & when)
        ok = has_next & has_before
        if r < len(past[1]):
            pl.when(ok & when)(sent[past[1][r]][0].start)
        else:
            past[1].append(push(xw.at[1, strip(r)], xw.at[2, strip(r)], ahead, ok, ok & when))

    fx[...] = jnp.zeros_like(fx)
    fg[...] = jnp.zeros_like(fg)
    fbuf[...] = jnp.zeros_like(fbuf)
    if total_rows > 27 * chans:
        acc[27 * chans :, :] = jnp.zeros((total_rows - 27 * chans, ce), F32)

    gain = gain_ref[...]
    bias = bias_ref[...]
    group = chans // GROUPS
    count = rows * width * T * group
    relay_far(0, odd)
    relay_far(0, even)
    sums = take_stats(0)
    grouped = group_sum(sums, group)
    mean2 = grouped[:halves] / count
    inv2 = lax.rsqrt(grouped[halves:] / count - mean2 * mean2 + EPSILON)

    def wide(two):
        return jnp.concatenate([two[i : i + 1] for i in range(halves)], axis=1)

    mean, inv = wide(mean2), wide(inv2)

    def shift_grad(conv, cot, mean, inv, gain, bias):
        normed = (conv.astype(F32) - mean) * inv
        shifted = normed * gain + bias
        sigma = jax.nn.sigmoid(shifted)
        return normed, cot.astype(F32) * sigma * (1.0 + shifted * (1.0 - sigma))

    normed, grad = shift_grad(co_ref[0], ct_ref[0], mean, inv, gain, bias)
    own[0] = normed
    own[1] = grad
    put_stats(
        1,
        jnp.sum(jnp.sum(grad, axis=0), axis=0, keepdims=True),
        jnp.sum(jnp.sum(grad * normed, axis=0), axis=0, keepdims=True),
    )
    send_stats(1)

    def part(v):
        out = v[..., 0:ce]
        for j in range(1, S):
            out = jnp.where(s == j, v[..., j * ce : (j + 1) * ce], out)
        return out

    for r in range(1, S):
        relay_near(r)
    for r in range(1, S):
        relay_far(r, odd)
    for r in range(1, S):
        take(cut[r - 1], cw.at[strip(r)])
    keep.wait()
    firsts = tuple(part(p) for p in (mean, inv, gain, bias))
    for j in range(S):
        normed, grad = shift_grad(cw[j, 0], cw[j, 1], *firsts)
        pre[j, 0] = normed
        pre[j, 1] = grad

    def put_input(k):
        for j in range(S):
            value = xw[k, j].astype(F32)
            if k > 0:
                value = jnp.where(t >= k, value, 0.0)
            fx[0:rows, j * cols : (j + 1) * cols, :] = value
        placed = fx[...].reshape(fx.shape[0] * fx.shape[1], chans)[0:depth]
        xt[k] = jnp.transpose(placed).astype(BF16)

    put_input(0)
    for r in range(1, S):
        relay_far(r, even)
    put_input(1)
    sums = take_stats(1)
    chan_bias, chan_gain = wide(sums[:halves]), wide(sums[halves:])
    gb_ref[...] = chan_bias
    gg_ref[...] = chan_gain
    gain2 = jnp.concatenate([gain[:, i * 128 : (i + 1) * 128] for i in range(halves)], axis=0)
    plain = wide(group_sum(sums[:halves] * gain2, group)) / count
    product = wide(group_sum(sums[halves:] * gain2, group)) / count

    def conv_grad(normed, grad, inv, gain, plain, product):
        return inv * (grad * gain - plain - normed * product)

    g = conv_grad(own[0], own[1], inv, gain, plain, product)
    for h in range(rows):
        gflat[h * cols : (h + 1) * cols, :] = g[h]
    gs[...] = gflat[...].astype(BF16)
    for h in range(rows):
        ge_out[0, h : h + 1, :] = g[h, 0:1, :].astype(BF16)
        ge_out[1, h : h + 1, :] = g[h, cols - 1 : cols, :].astype(BF16)
    second = (frame(-2), s)
    later = {
        "pair": push(gs, gr, ahead, even),
        "near": push(gs, gh.at[0], behind, odd),
        "far": push(gs, gh.at[1], second, odd & (t > 1)),
    }
    rims = []
    for k in range(3):
        back = (frame(-k), strip(1)), (frame(-k), strip(-1))
        rims.append((
            push(ge_out.at[1], ge_in.at[k, 0], back[0], (t >= k) & (s + 1 < S)),
            push(ge_out.at[0], ge_in.at[k, 1], back[1], (t >= k) & (s > 0)),
        ))

    seconds = tuple(part(p) for p in (inv, gain, plain, product))
    for j in range(S):
        fg[1 : rows + 1, j * cols : (j + 1) * cols, :] = conv_grad(pre[j, 0], pre[j, 1], *seconds)
    tall = fg.shape[0] * width
    f = fg[...].reshape(tall, ce)
    column = lax.broadcasted_iota(jnp.int32, fg.shape, 1).reshape(tall, ce)
    moved = (
        jnp.where(column < width - 1, pltpu.roll(f, tall - 1, 0), 0.0),
        f,
        jnp.where(column > 0, pltpu.roll(f, 1, 0), 0.0),
    )
    for c, w in enumerate(moved):
        for b in range(3):
            gw[b, :, c * ce : (c + 1) * ce] = w[(2 - b) * width : (2 - b) * width + depth].astype(BF16)

    bits = T.bit_length() - 1
    streams = len(sizes)
    orders = stage_orders(bits, streams)
    starts = stream_starts(sizes, chans)
    bases = [sum(sizes[:p]) for p in range(streams)]
    offs = [0] * streams
    flying = [None] * streams
    copies = []

    def side(bit):
        return lax.rem(t // (2**bit), 2)

    def partner(bit):
        return (t + (1 - 2 * side(bit)) * 2**bit, s)

    def span(p, off, n):
        return pl.ds(pl.multiple_of(bases[p] + off, 16), n)

    def start_of(p, i):
        return bases[p] + sizes[p] - (sizes[p] >> i)

    def launch(i, p):
        half = sizes[p] >> (i + 1)
        start = start_of(p, i)
        copy = pltpu.make_async_remote_copy(
            src_ref=sbuf.at[start : start + half], dst_ref=rbuf.at[start : start + half],
            send_sem=rs_send.at[0, p, i], recv_sem=rs_recv.at[0, p, i],
            device_id=partner(orders[p][i]), device_id_type=MESH,
        )
        copy.start()
        copies.append(copy)
        flying[p] = copy

    tree = T == 4 * LINE
    z, x, core = t // 4, lax.rem(t // 2, 2), lax.rem(t, 2)
    side_z = z // 2
    inner = (z == 1) | (z == 2)
    outer = (z == 0) | (z == 3)
    toward = jnp.where(inner, z - 1 + 2 * side_z, z + 1 - 2 * side_z)
    mates = {
        "core": (t + 1 - 2 * core, s),
        "x": (t + 2 - 4 * x, s),
        "line": (toward * 4 + lax.rem(t, 4), s),
        "middle": (lax.rem(3 - z + T, T) * 4 + lax.rem(t, 4), s),
    }
    slots = {"c0": 0, "x0": 1, "z0": 2, "z1": 3, "a2b": 3, "a1": 4, "a2a": 4, "x1": 5}

    def tree_push(p, kind, src, dst, device):
        by_role = kind in ("z0", "z1", "a1", "a2a", "a2b")
        pltpu.make_async_remote_copy(
            src_ref=src, dst_ref=dst, send_sem=tree_send.at[int(by_role)],
            recv_sem=tree_send.at[2] if kind == "c1" else tree_recv.at[p, slots[kind]],
            device_id=device, device_id_type=MESH,
        ).start()

    def tree_wait(p, kind, ref):
        pltpu.make_async_copy(ref, ref, tree_recv.at[p, slots[kind]]).wait()

    def places(p):
        half, n, h = sizes[p] // 2, sizes[p] // 4, sizes[p] // 8
        mine = core * half + x * n
        apart = core * half + (1 - x) * n
        return half, n, h, mine, apart

    def rows_of(ref, p, off, n):
        return ref.at[span(p, off, n)]

    def tree_event(p, e):
        half, n, h, mine, apart = places(p)
        base = bases[p]
        near, far = mine + side_z * h, mine + (1 - side_z) * h
        at_x, at_z = half, half + n
        zrow = pl.ds(base // 8, h)

        def taken(ref, off, rows):
            return ref[span(p, off, rows), :]

        def put_half(kind, off, device):
            tree_push(p, kind, rows_of(gk_ref, p, off, h), rows_of(gk_ref, p, off, h), device)

        def put_whole(kind, off):
            tree_push(p, kind, rows_of(gk_ref, p, off, n), rows_of(gk_ref, p, off, n), mates["core"])

        if e == 0:
            tree_wait(p, "c0", rows_of(rbuf, p, 0, half))
            value = taken(acc, apart, n) + taken(rbuf, (1 - x) * n, n).astype(F32)
            sbuf[span(p, at_x, n), :] = value.astype(BF16)
            tree_push(p, "x0", rows_of(sbuf, p, at_x, n), rows_of(rbuf, p, at_x, n), mates["x"])
            acc[span(p, mine, n), :] = taken(acc, mine, n) + taken(rbuf, x * n, n).astype(F32)
        elif e == 1:
            tree_wait(p, "x0", rows_of(rbuf, p, at_x, n))

            @pl.when(outer)
            def _():
                value = taken(acc, mine, n) + taken(rbuf, at_x, n).astype(F32)
                sbuf[span(p, at_z, n), :] = value.astype(BF16)
                tree_push(p, "z0", rows_of(sbuf, p, at_z, n), rows_of(rbuf, p, at_z, n), mates["line"])

            @pl.when(inner)
            def _():
                acc[span(p, mine, n), :] = taken(acc, mine, n) + taken(rbuf, at_x, n).astype(F32)
        elif e == 2:
            @pl.when(inner)
            def _():
                tree_wait(p, "z0", rows_of(rbuf, p, at_z, n))
                value = taken(acc, far, h) + taken(rbuf, at_z + (1 - side_z) * h, h).astype(F32)
                sbuf[span(p, at_z, h), :] = value.astype(BF16)
                tree_push(p, "z1", rows_of(sbuf, p, at_z, h), zbuf.at[zrow], mates["middle"])
                acc[span(p, near, h), :] = taken(acc, near, h) + taken(rbuf, at_z + side_z * h, h).astype(F32)
        elif e == 3:
            @pl.when(inner)
            def _():
                tree_wait(p, "z1", zbuf.at[zrow])
                gk_ref[span(p, near, h), :] = (taken(acc, near, h) + zbuf[zrow, :].astype(F32)).astype(BF16)
                put_half("x1", near, mates["x"])
                put_half("a1", near, mates["middle"])
                put_half("a2a", near, mates["line"])
        elif e == 4:
            @pl.when(inner)
            def _():
                tree_wait(p, "a1", rows_of(gk_ref, p, far, h))
                put_half("x1", far, mates["x"])
                put_half("a2b", far, mates["line"])
                put_whole("c1", mine)

            @pl.when(outer)
            def _():
                tree_wait(p, "a2a", rows_of(gk_ref, p, near, h))
                put_half("x1", near, mates["x"])
        elif e == 5:
            @pl.when(outer)
            def _():
                tree_wait(p, "a2b", rows_of(gk_ref, p, far, h))
                put_half("x1", far, mates["x"])
                put_whole("c1", mine)
        else:
            tree_wait(p, "x1", rows_of(gk_ref, p, apart, n))
            put_whole("c1", apart)

    def tree_end():
        for ref, i in ((gk_ref.at[0 : total_rows // 2], 2), (acc.at[0 : total_rows * 3 // 4], 0)):
            pltpu.make_async_copy(ref, ref, tree_send.at[i]).wait()

        @pl.when(outer)
        def _():
            pltpu.make_async_copy(sbuf.at[0 : total_rows // 4], sbuf.at[0 : total_rows // 4], tree_send.at[1]).wait()

        @pl.when(inner)
        def _():
            pltpu.make_async_copy(sbuf.at[0 : total_rows // 2], sbuf.at[0 : total_rows // 2], tree_send.at[1]).wait()

    def begin(p):
        half = sizes[p] >> 1
        mine = side(orders[p][0])
        start = start_of(p, 0)
        sbuf[start : start + half, :] = acc[span(p, (1 - mine) * half, half), :].astype(BF16)
        if tree:
            tree_push(p, "c0", sbuf.at[start : start + half], rbuf.at[start : start + half], mates["core"])
            return
        launch(0, p)
        offs[p] = mine * half

    def sum_at(p, i, off, n):
        at = span(p, offs[p] + off, n)
        seen = pl.ds(pl.multiple_of(start_of(p, i) + off, 16), n)
        return at, acc[at, :] + rbuf[seen, :].astype(F32)

    def spread(i, p):
        n = sizes[p] >> (i + 1)
        bit = orders[p][i]
        at = span(p, offs[p], n)
        copy = pltpu.make_async_remote_copy(
            src_ref=gk_ref.at[at], dst_ref=gk_ref.at[at],
            send_sem=rs_send.at[1, p, i], recv_sem=rs_recv.at[1, p, i],
            device_id=partner(bit), device_id_type=MESH,
        )
        copy.start()
        copies.append(copy)
        offs[p] = offs[p] - side(bit) * n
        flying[p] = copy

    def arrive(p, step):
        flying[p].wait_recv()
        if step < bits - 1:
            half = sizes[p] >> (step + 2)
            mine = side(orders[p][step + 1])
            start = start_of(p, step + 1)
            _, value = sum_at(p, step, (1 - mine) * half, half)
            sbuf[start : start + half, :] = value.astype(BF16)
            launch(step + 1, p)
            at, value = sum_at(p, step, mine * half, half)
            acc[at, :] = value
            offs[p] = offs[p] + mine * half
        elif step == bits - 1:
            at, value = sum_at(p, step, 0, sizes[p] >> bits)
            gk_ref[at, :] = value.astype(BF16)
            spread(bits - 1, p)
        elif step + 1 < 2 * bits:
            spread(2 * bits - 2 - step, p)

    def taps(a, b, ready):
        if a == TAPS_A[-1] and b == 0:
            for r in range(S):
                take(past[1][r], xw.at[2, strip(r)], t > 1)
            put_input(2)
        res = jnp.dot(xt[2 - a], gw[b], preferred_element_type=F32)
        for c in range(3):
            at = ((a * 3 + b) * 3 + c) * chans
            acc[at : at + chans, :] = res[:, c * ce : (c + 1) * ce]
        for p in ready:
            begin(p)
        if (a, b) == (TAPS_A[0], 2):
            take(later["pair"], gr, odd)
            later["next"] = push(gr, gh.at[0], second, odd & (t > 1))

    def put_gown(k):
        live = t + k < T
        if k == 0:
            value = gs[...].astype(F32)
        else:
            if k == 1:
                take(later["near"], gh.at[0], live & even)
                take(later["next"], gh.at[0], live & odd)
                later["last"] = push(gh.at[0], gh.at[1], behind, live & odd)
            else:
                take(later["far"], gh.at[1], live & odd)
                take(later["last"], gh.at[1], live & even)
            value = jnp.where(live, gh[k - 1].astype(F32), 0.0)
        for h in range(rows):
            fbuf[h + 1, 0:cols, :] = value[h * cols : (h + 1) * cols]
        take(rims[k][0], ge_in.at[k, 0], live & (s > 0))
        take(rims[k][1], ge_in.at[k, 1], live & (s + 1 < S))
        left = jnp.where(live & (s > 0), ge_in[k, 0].astype(F32), 0.0)
        right = jnp.where(live & (s < S - 1), ge_in[k, 1].astype(F32), 0.0)
        for h in range(rows):
            fbuf[h, pitch - 1 : pitch, :] = left[h : h + 1]
            fbuf[h + 1, cols : cols + 1, :] = right[h : h + 1]
        f = fbuf[...].reshape(flat_all, chans)
        for c, w in enumerate((pltpu.roll(f, flat_all - 1, 0), f, pltpu.roll(f, 1, 0))):
            gown[k, :, c * chans : (c + 1) * chans] = w.astype(BF16)

    counted = [0]

    def input_grad(a, b):
        if counted[0] == 0:
            load.wait()
        total = None if counted[0] == 0 else tot[...]
        for c in range(3):
            term = lax.dot_general(
                gown[2 - a, (2 - b) * pitch : (2 - b) * pitch + flat, c * chans : (c + 1) * chans],
                wbuf[a, b, c], (((1,), (1,)), ((), ())), preferred_element_type=F32,
            )
            total = term if total is None else total + term
        counted[0] += 1
        if counted[0] < 9:
            tot[...] = total
        else:
            gi_ref[0] = total.reshape(rows, pitch, chans)[:, 0:cols, :].astype(BF16)

    tasks = tree_plan(starts, streams) if tree else plan(bits, sizes, orders, starts, ce * 2)
    for task in tasks:
        if task[0] == "taps":
            taps(*task[1:])
        elif task[0] == "arrive":
            arrive(*task[1:])
        elif task[0] == "tree":
            tree_event(*task[1:])
        elif task[0] == "gown":
            put_gown(task[1])
        else:
            input_grad(*task[1:])
    if tree:
        tree_end()

    for copy in copies:
        copy.wait_send()
    for copy, ok in sent:
        if ok is None:
            copy.wait_send()
        else:
            pl.when(ok)(copy.wait_send)
    for which in range(2):
        pltpu.make_async_copy(st_in.at[which], st_in.at[which], st_send.at[which]).wait()


def solution(mesh):
    T, S = mesh.shape["tm"], mesh.shape["space"]

    def shards(conv_input, conv_out, kernel, gain, bias, cotangent):
        _, rows, cols, chans = conv_out.shape
        width = cols * S
        ce = chans // S
        bits = T.bit_length() - 1
        groups = round_up(27 * chans, T * 16) // (T * 16)
        streams = min(STREAMS, groups)
        sizes = [(groups // streams + (p < groups % streams)) * T * 16 for p in range(streams)]
        total_rows = sum(sizes)
        pitch = round_up(cols + 2, 16)
        depth = round_up(rows * width, 128)
        fx_rows = (depth + width - 1) // width
        fg_rows = max(rows + 2, (2 * width + depth + width - 1) // width)
        n_bulk = (S - 1) * 2 + 2 * S + 5 + 6
        tree = T == 4 * LINE
        halving, line = ((1, 1, 1), (streams, 6)) if tree else ((2, streams, bits), (1, 1))
        vmem = pl.BlockSpec(memory_space=pltpu.VMEM)
        hbm = pl.BlockSpec(memory_space=pltpu.HBM)
        gi, gk, gg, gb = pl.pallas_call(
            functools.partial(body, T, S, sizes),
            out_shape=(
                pltpu.VMEM(conv_input.shape, BF16),
                pltpu.VMEM((total_rows, ce), BF16),
                pltpu.VMEM((1, chans), F32),
                pltpu.VMEM((1, chans), F32),
            ),
            in_specs=[hbm, hbm, hbm, vmem, vmem, hbm],
            out_specs=(vmem, vmem, vmem, vmem),
            scratch_shapes=[
                pltpu.VMEM((3, S, rows, cols, chans), BF16),
                pltpu.VMEM(conv_out.shape, BF16),
                pltpu.VMEM(cotangent.shape, BF16),
                pltpu.VMEM((S, 2, rows, cols, ce), BF16),
                pltpu.VMEM((S, 2, rows, cols, ce), BF16),
                pltpu.VMEM((2, 2 * chans // 128, 128), F32),
                pltpu.VMEM((2, T * S - 1, 2 * chans // 128, 128), F32),
                pltpu.VMEM((2, rows, cols, chans), F32),
                pltpu.VMEM((S, 2, rows, cols, ce), F32),
                pltpu.VMEM((fx_rows, width, chans), F32),
                pltpu.VMEM((fg_rows, width, ce), F32),
                pltpu.VMEM((rows + 2, pitch, chans), F32),
                pltpu.VMEM((rows * cols, chans), F32),
                pltpu.VMEM((rows * cols, chans), BF16),
                pltpu.VMEM((rows * cols, chans), BF16),
                pltpu.VMEM((2, rows * cols, chans), BF16),
                pltpu.VMEM((2, rows, chans), BF16),
                pltpu.VMEM((3, 2, rows, chans), BF16),
                pltpu.VMEM((3, (rows + 2) * pitch, 3 * chans), BF16),
                pltpu.VMEM((3, depth, 3 * ce), BF16),
                pltpu.VMEM((3, chans, depth), BF16),
                pltpu.VMEM((3, 3, 3, chans, chans), BF16),
                pltpu.VMEM((rows * pitch, chans), F32),
                pltpu.VMEM((total_rows, ce), F32),
                pltpu.VMEM((total_rows, ce), BF16),
                pltpu.VMEM((total_rows, ce), BF16),
                pltpu.VMEM((total_rows // 8, ce), BF16),
                pltpu.SemaphoreType.DMA((4,)),
                pltpu.SemaphoreType.DMA,
                pltpu.SemaphoreType.DMA((2,)),
                pltpu.SemaphoreType.DMA((2,)),
                pltpu.SemaphoreType.DMA((n_bulk,)),
                pltpu.SemaphoreType.DMA((n_bulk,)),
                pltpu.SemaphoreType.DMA(halving),
                pltpu.SemaphoreType.DMA(halving),
                pltpu.SemaphoreType.DMA((3,)),
                pltpu.SemaphoreType.DMA(line),
            ],
            compiler_params=pltpu.CompilerParams(
                collective_id=0, has_side_effects=True, vmem_limit_bytes=60 * 1024 * 1024
            ),
        )(conv_input, conv_out, kernel, gain.reshape(1, chans), bias.reshape(1, chans), cotangent)
        gi, gk, gg, gb = pl.pallas_call(
            hand_out,
            out_shape=(
                jax.ShapeDtypeStruct(gi.shape, BF16),
                jax.ShapeDtypeStruct((27 * chans, ce), F32),
                jax.ShapeDtypeStruct((1, chans), F32),
                jax.ShapeDtypeStruct((1, chans), F32),
            ),
            in_specs=[vmem, vmem, vmem, vmem],
            out_specs=(hbm, hbm, vmem, vmem),
            scratch_shapes=[pltpu.VMEM((27 * chans, ce), F32), pltpu.SemaphoreType.DMA((PARTS + 1,))],
            compiler_params=pltpu.CompilerParams(vmem_limit_bytes=16 * 1024 * 1024),
        )(gi, gk, gg, gb)
        return gi, gk.reshape(3, 3, 3, chans, ce), gg.reshape(chans), gb.reshape(chans)

    strip = P("tm", None, "space", None)
    return jax.shard_map(
        shards,
        mesh=mesh,
        in_specs=(strip, strip, P(), P(), P(), strip),
        out_specs=(strip, P(None, None, None, None, "space"), P(), P()),
        check_vma=False,
    )
```

```python
import functools
import heapq

import jax
import jax.numpy as jnp
from jax import lax
from jax.experimental import pallas as pl
from jax.experimental.pallas import tpu as pltpu
from jax.sharding import PartitionSpec as P

GROUPS = 32
STREAMS = 13
PARTS = 3
EPSILON = 1e-06
MESH = pl.DeviceIdType.MESH
F32 = jnp.float32
BF16 = jnp.bfloat16


def round_up(value, unit):
    return (value + unit - 1) // unit * unit


def group_sum(x, width):
    lanes = x.shape[1]
    lane = lax.broadcasted_iota(jnp.int32, x.shape, 1)
    step = 1
    while step < width:
        up = pltpu.roll(x, lanes - step, 1)
        down = pltpu.roll(x, step, 1)
        x = x + jnp.where((lane // step) % 2 == 0, up, down)
        step *= 2
    return x


def hand_out(gi_in, gk_in, gg_in, gb_in, gi_out, gk_out, gg_out, gb_out, wide, sems):
    rows = gk_out.shape[0] // PARTS
    copies = [pltpu.make_async_copy(gi_in, gi_out, sems.at[PARTS])]
    copies[0].start()
    for i in range(PARTS):
        at = slice(i * rows, (i + 1) * rows)
        wide[at, :] = gk_in[at, :].astype(F32)
        copies.append(pltpu.make_async_copy(wide.at[at], gk_out.at[at], sems.at[i]))
        copies[-1].start()
    gg_out[...] = gg_in[...]
    gb_out[...] = gb_in[...]
    for copy in copies:
        copy.wait()


TAPS_A = (2, 1, 0)
MATMUL = 0.36
FILLER = 0.36
ON_CHIP = (1.1, 200e3)
ON_LINK = (1.7, 46e3)
FAR = 0.75


def stage_orders(bits, streams):
    straight = list(range(bits))
    swapped = list(range(bits))
    if bits > 2:
        swapped[1], swapped[2] = swapped[2], swapped[1]
    return [swapped if p % 2 else straight for p in range(streams)]


def stream_starts(sizes, chans):
    done, begun, starts = set(), set(), []
    edges = [sum(sizes[:p]) for p in range(len(sizes) + 1)]
    for a in TAPS_A:
        for b in range(3):
            done.add(a * 3 + b)
            ready = []
            for p in range(len(sizes)):
                first, last = edges[p] // (3 * chans), (min(edges[p + 1], 27 * chans) - 1) // (3 * chans)
                if p not in begun and all(g in done for g in range(first, last + 1)):
                    begun.add(p)
                    ready.append(p)
            starts.append(((a, b), ready))
    return starts


def plan(bits, sizes, orders, starts, row_bytes):
    free = {}
    heap = []
    steps = 2 * bits

    def send(now, p, step):
        level = step if step < bits else steps - 1 - step
        rows = sizes[p] >> (level + 1)
        bit = orders[p][level]
        latency, rate = ON_CHIP if bit == 0 else ON_LINK
        time = rows * row_bytes / rate
        if bit > 2:
            latency, time = latency + FAR, 2 * time
        link = min(bit, 2)
        begin = max(now, free.get(link, 0.0))
        free[link] = begin + time
        heapq.heappush(heap, (begin + time + latency, step, p))

    matmuls = list(starts)
    fillers = [(0.0, ("gown", 0))] + [(0.0, ("input", 2, b)) for b in range(3)]
    fillers += [(7.0, ("gown", 1))] + [(0.0, ("input", 1, b)) for b in range(3)]
    fillers += [(11.0, ("gown", 2))] + [(0.0, ("input", 0, b)) for b in range(3)]
    tasks, now = [], 0.0
    while heap or matmuls or fillers:
        if heap and heap[0][0] <= now:
            _, step, p = heapq.heappop(heap)
            tasks.append(("arrive", p, step))
            now += 0.03 + 1.5e-4 * (sizes[p] >> (step + 1) if step < bits else 0)
            if step + 1 < steps:
                send(now, p, step + 1)
        elif matmuls:
            (a, b), ready = matmuls.pop(0)
            tasks.append(("taps", a, b, ready))
            now += MATMUL
            for p in ready:
                send(now, p, 0)
        elif fillers and fillers[0][0] <= now and (not heap or heap[0][0] - now >= 0.8 * FILLER):
            tasks.append(fillers.pop(0)[1])
            now += FILLER
        else:
            now = heap[0][0] if heap else fillers[0][0]
    return tasks


EVENTS = ((1.54, 0.310), (2.88, 0.710), (4.98, 0.730), (7.79, 0.730), (10.14, 0.800), (12.84, 0.840), (18.50, 0.950))
FILL_AT = (4.45, 12.45, 17.46)
FILL_STEP = 1.06
LINE = 4


def tree_plan(starts, streams):
    tasks, number = [], 0
    for i, ((a, b), ready) in enumerate(starts):
        tasks.append((i * MATMUL, ("taps", a, b, ready)))
        for p in ready:
            last = i * MATMUL
            for e, (first, step) in enumerate(EVENTS):
                last = max(last + 1e-3, first + step * number * 13 / streams)
                tasks.append((last, ("tree", p, e)))
            number += 1
    for k, a in enumerate(TAPS_A):
        tasks.append((FILL_AT[k], ("gown", k)))
        for b in range(3):
            tasks.append((FILL_AT[k] + (b + 1) * FILL_STEP, ("input", a, b)))
    return [task for _, task in sorted(tasks, key=lambda item: item[0])]


def body(
    T, S, sizes,
    x_hbm, co_hbm, k_hbm, gain_ref, bias_ref, ct_hbm,
    gi_ref, gk_ref, gg_ref, gb_ref,
    x_ref, xw, co_ref, ct_ref, slice_out, cw, st_out, st_in, own, pre, fx, fg, fbuf,
    gflat, gs, gr, gh, ge_out, ge_in, gown, gw, xt, wbuf, tot, acc, sbuf, rbuf, zbuf,
    in_sem, w_sem, st_send, st_recv, bulk_send, bulk_recv, rs_send, rs_recv, tree_send, tree_recv,
):
    N = T * S
    total_rows = sum(sizes)
    _, rows, cols, chans = co_ref.shape
    width = cols * S
    ce = chans // S
    depth = xt.shape[2]
    pitch = fbuf.shape[1]
    flat = rows * pitch
    flat_all = (rows + 2) * pitch
    halves = chans // 128
    t = lax.axis_index("tm")
    s = lax.axis_index("space")
    me = t * S + s

    loads = [
        pltpu.make_async_copy(src, dst, in_sem.at[i])
        for i, (src, dst) in enumerate(((co_hbm, co_ref), (ct_hbm, ct_ref), (x_hbm, x_ref)))
    ]
    for copy in loads:
        copy.start()

    barrier = pltpu.get_barrier_semaphore()

    strips = S.bit_length() - 1
    spans = N.bit_length() - 1 - strips
    flip_s = [(1 - 2 * lax.rem(s // 2**k, 2)) * 2**k for k in range(strips)]
    flip_t = [(1 - 2 * lax.rem(t // 2**k, 2)) * 2**k for k in range(spans)]

    def others():
        for r in range(N - 1, 0, -1):
            to_s = sum((flip for k, flip in enumerate(flip_s) if r >> k & 1), s)
            to_t = sum((flip for k, flip in enumerate(flip_t) if r >> (k + strips) & 1), t)
            yield r, (to_t, to_s)

    def each_other(act):
        if N <= 64:
            for r, to in others():
                act(r, to)
        else:
            def step(r, carry):
                r = N - r
                to_s = sum((lax.rem(r // 2**k, 2) * flip for k, flip in enumerate(flip_s)), s)
                to_t = sum((lax.rem(r // 2 ** (k + strips), 2) * flip for k, flip in enumerate(flip_t)), t)
                act(r, (to_t, to_s))
                return carry

            lax.fori_loop(1, N, step, 0)

    each_other(lambda r, to: pl.semaphore_signal(barrier, inc=1, device_id=to, device_id_type=MESH))

    loads[0].wait()
    load = pltpu.make_async_copy(k_hbm, wbuf, w_sem)
    load.start()
    conv = co_ref[0].astype(F32)
    first = jnp.sum(jnp.sum(conv, axis=0), axis=0, keepdims=True)
    second = jnp.sum(jnp.sum(conv * conv, axis=0), axis=0, keepdims=True)

    def put_stats(which, one, two):
        for i in range(halves):
            st_out[which, i : i + 1, :] = one[:, i * 128 : (i + 1) * 128]
            st_out[which, halves + i : halves + i + 1, :] = two[:, i * 128 : (i + 1) * 128]

    def send_stats(which):
        each_other(lambda r, to: pltpu.make_async_remote_copy(
            src_ref=st_out.at[which], dst_ref=st_in.at[which, r - 1],
            send_sem=st_send.at[which], recv_sem=st_recv.at[which],
            device_id=to, device_id_type=MESH,
        ).start())

    def take_stats(which):
        pltpu.make_async_copy(st_in.at[which], st_in.at[which], st_recv.at[which]).wait()
        return jnp.sum(st_in[which], axis=0) + st_out[which]

    put_stats(0, first, second)
    pl.semaphore_wait(barrier, N - 1)
    send_stats(0)
    loads[1].wait()
    loads[2].wait()

    sent = []

    def push(src, dst, device, ok=None, now=None):
        i = len(sent)
        copy = pltpu.make_async_remote_copy(
            src_ref=src, dst_ref=dst, send_sem=bulk_send.at[i], recv_sem=bulk_recv.at[i],
            device_id=device, device_id_type=MESH,
        )
        if ok is None:
            copy.start()
        else:
            pl.when(ok if now is None else now)(copy.start)
        sent.append((copy, ok))
        return i

    def take(i, dst, ok=None):
        copy = pltpu.make_async_copy(dst, dst, bulk_recv.at[i])
        if ok is None:
            copy.wait()
        else:
            pl.when(ok)(copy.wait)

    def frame(n):
        return lax.rem(t + T + n, T)

    def strip(n):
        return lax.rem(s + S + n, S)

    ahead = (frame(1), s)
    behind = (frame(-1), s)
    has_next, has_before = t + 1 < T, t > 0
    cut, mate, past = [], [], [[], []]
    def pack(ref):
        for h in range(rows):
            gflat[h * cols : (h + 1) * cols, :] = ref[0, h].astype(F32)
        return gflat[...].astype(BF16)

    xw[0, s] = pack(x_ref)
    past[0].append(push(xw.at[0, s], xw.at[1, s], ahead, has_next))
    for r in range(1, S):
        mate.append(push(xw.at[0, s], xw.at[0, s], (t, strip(-r))))
    for arr, ref in ((0, co_ref), (1, ct_ref)):
        whole = pack(ref)
        for j in range(S):
            slice_out[j, arr] = whole[:, j * ce : (j + 1) * ce]
    keep = pltpu.make_async_copy(slice_out.at[s], cw.at[s], in_sem.at[3])
    keep.start()
    for r in range(1, S):
        cut.append(push(slice_out.at[strip(-r)], cw.at[s], (t, strip(-r))))

    odd = lax.rem(t, 2) == 1
    even = lax.rem(t, 2) == 0

    def relay_near(r):
        take(mate[r - 1], xw.at[0, strip(r)])
        past[0].append(push(xw.at[0, strip(r)], xw.at[1, strip(r)], ahead, has_next))

    def relay_far(r, when):
        take(past[0][r], xw.at[1, strip(r)], has_before & when)
        ok = has_next & has_before
        if r < len(past[1]):
            pl.when(ok & when)(sent[past[1][r]][0].start)
        else:
            past[1].append(push(xw.at[1, strip(r)], xw.at[2, strip(r)], ahead, ok, ok & when))

    fx[...] = jnp.zeros_like(fx)
    fg[...] = jnp.zeros_like(fg)
    fbuf[...] = jnp.zeros_like(fbuf)
    if total_rows > 27 * chans:
        acc[27 * chans :, :] = jnp.zeros((total_rows - 27 * chans, ce), F32)

    gain = gain_ref[...]
    bias = bias_ref[...]
    group = chans // GROUPS
    count = rows * width * T * group
    relay_far(0, odd)
    relay_far(0, even)
    sums = take_stats(0)
    grouped = group_sum(sums, group)
    mean2 = grouped[:halves] / count
    inv2 = lax.rsqrt(grouped[halves:] / count - mean2 * mean2 + EPSILON)

    def wide(two):
        return jnp.concatenate([two[i : i + 1] for i in range(halves)], axis=1)

    mean, inv = wide(mean2), wide(inv2)

    def shift_grad(conv, cot, mean, inv, gain, bias):
        normed = (conv.astype(F32) - mean) * inv
        shifted = normed * gain + bias
        sigma = jax.nn.sigmoid(shifted)
        return normed, cot.astype(F32) * sigma * (1.0 + shifted * (1.0 - sigma))

    normed, grad = shift_grad(co_ref[0], ct_ref[0], mean, inv, gain, bias)
    own[0] = normed
    own[1] = grad
    put_stats(
        1,
        jnp.sum(jnp.sum(grad, axis=0), axis=0, keepdims=True),
        jnp.sum(jnp.sum(grad * normed, axis=0), axis=0, keepdims=True),
    )
    send_stats(1)

    def part(v):
        out = v[..., 0:ce]
        for j in range(1, S):
            out = jnp.where(s == j, v[..., j * ce : (j + 1) * ce], out)
        return out

    for r in range(1, S):
        relay_near(r)
    for r in range(1, S):
        relay_far(r, odd)
    for r in range(1, S):
        take(cut[r - 1], cw.at[strip(r)])
    keep.wait()
    firsts = tuple(part(p) for p in (mean, inv, gain, bias))
    for j in range(S):
        normed, grad = shift_grad(cw[j, 0], cw[j, 1], *firsts)
        pre[j, 0] = normed
        pre[j, 1] = grad

    def put_input(k):
        for j in range(S):
            value = xw[k, j].astype(F32)
            if k > 0:
                value = jnp.where(t >= k, value, 0.0)
            for h in range(rows):
                fx[h, j * cols : (j + 1) * cols, :] = value[h * cols : (h + 1) * cols]
        placed = fx[...].reshape(fx.shape[0] * fx.shape[1], chans)[0:depth]
        xt[k] = jnp.transpose(placed).astype(BF16)

    put_input(0)
    for r in range(1, S):
        relay_far(r, even)
    put_input(1)
    sums = take_stats(1)
    chan_bias, chan_gain = wide(sums[:halves]), wide(sums[halves:])
    gb_ref[...] = chan_bias
    gg_ref[...] = chan_gain
    gain2 = jnp.concatenate([gain[:, i * 128 : (i + 1) * 128] for i in range(halves)], axis=0)
    plain = wide(group_sum(sums[:halves] * gain2, group)) / count
    product = wide(group_sum(sums[halves:] * gain2, group)) / count

    def conv_grad(normed, grad, inv, gain, plain, product):
        return inv * (grad * gain - plain - normed * product)

    g = conv_grad(own[0], own[1], inv, gain, plain, product)
    for h in range(rows):
        gflat[h * cols : (h + 1) * cols, :] = g[h]
    gs[...] = gflat[...].astype(BF16)
    for h in range(rows):
        ge_out[0, h : h + 1, :] = g[h, 0:1, :].astype(BF16)
        ge_out[1, h : h + 1, :] = g[h, cols - 1 : cols, :].astype(BF16)
    second = (frame(-2), s)
    later = {
        "pair": push(gs, gr, ahead, even),
        "near": push(gs, gh.at[0], behind, odd),
        "far": push(gs, gh.at[1], second, odd & (t > 1)),
    }
    rims = []
    for k in range(3):
        back = (frame(-k), strip(1)), (frame(-k), strip(-1))
        rims.append((
            push(ge_out.at[1], ge_in.at[k, 0], back[0], (t >= k) & (s + 1 < S)),
            push(ge_out.at[0], ge_in.at[k, 1], back[1], (t >= k) & (s > 0)),
        ))

    seconds = tuple(part(p) for p in (inv, gain, plain, product))
    for j in range(S):
        value = conv_grad(pre[j, 0], pre[j, 1], *seconds)
        for h in range(rows):
            fg[h + 1, j * cols : (j + 1) * cols, :] = value[h * cols : (h + 1) * cols]
    tall = fg.shape[0] * width
    f = fg[...].reshape(tall, ce)
    column = lax.broadcasted_iota(jnp.int32, fg.shape, 1).reshape(tall, ce)
    moved = (
        jnp.where(column < width - 1, pltpu.roll(f, tall - 1, 0), 0.0),
        f,
        jnp.where(column > 0, pltpu.roll(f, 1, 0), 0.0),
    )
    for c, w in enumerate(moved):
        for b in range(3):
            gw[b, :, c * ce : (c + 1) * ce] = w[(2 - b) * width : (2 - b) * width + depth].astype(BF16)

    bits = T.bit_length() - 1
    streams = len(sizes)
    orders = stage_orders(bits, streams)
    starts = stream_starts(sizes, chans)
    bases = [sum(sizes[:p]) for p in range(streams)]
    offs = [0] * streams
    flying = [None] * streams
    copies = []

    def side(bit):
        return lax.rem(t // (2**bit), 2)

    def partner(bit):
        return (t + (1 - 2 * side(bit)) * 2**bit, s)

    def span(p, off, n):
        return pl.ds(pl.multiple_of(bases[p] + off, 16), n)

    def start_of(p, i):
        return bases[p] + sizes[p] - (sizes[p] >> i)

    def launch(i, p):
        half = sizes[p] >> (i + 1)
        start = start_of(p, i)
        copy = pltpu.make_async_remote_copy(
            src_ref=sbuf.at[start : start + half], dst_ref=rbuf.at[start : start + half],
            send_sem=rs_send.at[0, p, i], recv_sem=rs_recv.at[0, p, i],
            device_id=partner(orders[p][i]), device_id_type=MESH,
        )
        copy.start()
        copies.append(copy)
        flying[p] = copy

    tree = T == 4 * LINE
    z, x, core = t // 4, lax.rem(t // 2, 2), lax.rem(t, 2)
    side_z = z // 2
    inner = (z == 1) | (z == 2)
    outer = (z == 0) | (z == 3)
    toward = jnp.where(inner, z - 1 + 2 * side_z, z + 1 - 2 * side_z)
    mates = {
        "core": (t + 1 - 2 * core, s),
        "x": (t + 2 - 4 * x, s),
        "line": (toward * 4 + lax.rem(t, 4), s),
        "middle": (lax.rem(3 - z + T, T) * 4 + lax.rem(t, 4), s),
    }
    slots = {"c0": 0, "x0": 1, "z0": 2, "z1": 3, "a2b": 3, "a1": 4, "a2a": 4, "x1": 5}

    def tree_push(p, kind, src, dst, device):
        by_role = kind in ("z0", "z1", "a1", "a2a", "a2b")
        pltpu.make_async_remote_copy(
            src_ref=src, dst_ref=dst, send_sem=tree_send.at[int(by_role)],
            recv_sem=tree_send.at[2] if kind == "c1" else tree_recv.at[p, slots[kind]],
            device_id=device, device_id_type=MESH,
        ).start()

    def tree_wait(p, kind, ref):
        pltpu.make_async_copy(ref, ref, tree_recv.at[p, slots[kind]]).wait()

    def places(p):
        half, n, h = sizes[p] // 2, sizes[p] // 4, sizes[p] // 8
        mine = core * half + x * n
        apart = core * half + (1 - x) * n
        return half, n, h, mine, apart

    def rows_of(ref, p, off, n):
        return ref.at[span(p, off, n)]

    def tree_event(p, e):
        half, n, h, mine, apart = places(p)
        base = bases[p]
        near, far = mine + side_z * h, mine + (1 - side_z) * h
        at_x, at_z = half, half + n
        zrow = pl.ds(base // 8, h)

        def taken(ref, off, rows):
            return ref[span(p, off, rows), :]

        def put_half(kind, off, device):
            tree_push(p, kind, rows_of(gk_ref, p, off, h), rows_of(gk_ref, p, off, h), device)

        def put_whole(kind, off):
            tree_push(p, kind, rows_of(gk_ref, p, off, n), rows_of(gk_ref, p, off, n), mates["core"])

        if e == 0:
            tree_wait(p, "c0", rows_of(rbuf, p, 0, half))
            value = taken(acc, apart, n) + taken(rbuf, (1 - x) * n, n).astype(F32)
            sbuf[span(p, at_x, n), :] = value.astype(BF16)
            tree_push(p, "x0", rows_of(sbuf, p, at_x, n), rows_of(rbuf, p, at_x, n), mates["x"])
            acc[span(p, mine, n), :] = taken(acc, mine, n) + taken(rbuf, x * n, n).astype(F32)
        elif e == 1:
            tree_wait(p, "x0", rows_of(rbuf, p, at_x, n))

            @pl.when(outer)
            def _():
                value = taken(acc, mine, n) + taken(rbuf, at_x, n).astype(F32)
                sbuf[span(p, at_z, n), :] = value.astype(BF16)
                tree_push(p, "z0", rows_of(sbuf, p, at_z, n), rows_of(rbuf, p, at_z, n), mates["line"])

            @pl.when(inner)
            def _():
                acc[span(p, mine, n), :] = taken(acc, mine, n) + taken(rbuf, at_x, n).astype(F32)
        elif e == 2:
            @pl.when(inner)
            def _():
                tree_wait(p, "z0", rows_of(rbuf, p, at_z, n))
                value = taken(acc, far, h) + taken(rbuf, at_z + (1 - side_z) * h, h).astype(F32)
                sbuf[span(p, at_z, h), :] = value.astype(BF16)
                tree_push(p, "z1", rows_of(sbuf, p, at_z, h), zbuf.at[zrow], mates["middle"])
                acc[span(p, near, h), :] = taken(acc, near, h) + taken(rbuf, at_z + side_z * h, h).astype(F32)
        elif e == 3:
            @pl.when(inner)
            def _():
                tree_wait(p, "z1", zbuf.at[zrow])
                gk_ref[span(p, near, h), :] = (taken(acc, near, h) + zbuf[zrow, :].astype(F32)).astype(BF16)
                put_half("x1", near, mates["x"])
                put_half("a1", near, mates["middle"])
                put_half("a2a", near, mates["line"])
        elif e == 4:
            @pl.when(inner)
            def _():
                tree_wait(p, "a1", rows_of(gk_ref, p, far, h))
                put_half("x1", far, mates["x"])
                put_half("a2b", far, mates["line"])
                put_whole("c1", mine)

            @pl.when(outer)
            def _():
                tree_wait(p, "a2a", rows_of(gk_ref, p, near, h))
                put_half("x1", near, mates["x"])
        elif e == 5:
            @pl.when(outer)
            def _():
                tree_wait(p, "a2b", rows_of(gk_ref, p, far, h))
                put_half("x1", far, mates["x"])
                put_whole("c1", mine)
        else:
            tree_wait(p, "x1", rows_of(gk_ref, p, apart, n))
            put_whole("c1", apart)

    def tree_end():
        for ref, i in ((gk_ref.at[0 : total_rows // 2], 2), (acc.at[0 : total_rows * 3 // 4], 0)):
            pltpu.make_async_copy(ref, ref, tree_send.at[i]).wait()

        @pl.when(outer)
        def _():
            pltpu.make_async_copy(sbuf.at[0 : total_rows // 4], sbuf.at[0 : total_rows // 4], tree_send.at[1]).wait()

        @pl.when(inner)
        def _():
            pltpu.make_async_copy(sbuf.at[0 : total_rows // 2], sbuf.at[0 : total_rows // 2], tree_send.at[1]).wait()

    def begin(p):
        half = sizes[p] >> 1
        mine = side(orders[p][0])
        start = start_of(p, 0)
        sbuf[start : start + half, :] = acc[span(p, (1 - mine) * half, half), :].astype(BF16)
        if tree:
            tree_push(p, "c0", sbuf.at[start : start + half], rbuf.at[start : start + half], mates["core"])
            return
        launch(0, p)
        offs[p] = mine * half

    def sum_at(p, i, off, n):
        at = span(p, offs[p] + off, n)
        seen = pl.ds(pl.multiple_of(start_of(p, i) + off, 16), n)
        return at, acc[at, :] + rbuf[seen, :].astype(F32)

    def spread(i, p):
        n = sizes[p] >> (i + 1)
        bit = orders[p][i]
        at = span(p, offs[p], n)
        copy = pltpu.make_async_remote_copy(
            src_ref=gk_ref.at[at], dst_ref=gk_ref.at[at],
            send_sem=rs_send.at[1, p, i], recv_sem=rs_recv.at[1, p, i],
            device_id=partner(bit), device_id_type=MESH,
        )
        copy.start()
        copies.append(copy)
        offs[p] = offs[p] - side(bit) * n
        flying[p] = copy

    def arrive(p, step):
        flying[p].wait_recv()
        if step < bits - 1:
            half = sizes[p] >> (step + 2)
            mine = side(orders[p][step + 1])
            start = start_of(p, step + 1)
            _, value = sum_at(p, step, (1 - mine) * half, half)
            sbuf[start : start + half, :] = value.astype(BF16)
            launch(step + 1, p)
            at, value = sum_at(p, step, mine * half, half)
            acc[at, :] = value
            offs[p] = offs[p] + mine * half
        elif step == bits - 1:
            at, value = sum_at(p, step, 0, sizes[p] >> bits)
            gk_ref[at, :] = value.astype(BF16)
            spread(bits - 1, p)
        elif step + 1 < 2 * bits:
            spread(2 * bits - 2 - step, p)

    def taps(a, b, ready):
        if a == TAPS_A[-1] and b == 0:
            for r in range(S):
                take(past[1][r], xw.at[2, strip(r)], t > 1)
            put_input(2)
        res = jnp.dot(xt[2 - a], gw[b], preferred_element_type=F32)
        for c in range(3):
            at = ((a * 3 + b) * 3 + c) * chans
            acc[at : at + chans, :] = res[:, c * ce : (c + 1) * ce]
        for p in ready:
            begin(p)
        if (a, b) == (TAPS_A[0], 2):
            take(later["pair"], gr, odd)
            later["next"] = push(gr, gh.at[0], second, odd & (t > 1))

    def put_gown(k):
        live = t + k < T
        if k == 0:
            value = gs[...].astype(F32)
        else:
            if k == 1:
                take(later["near"], gh.at[0], live & even)
                take(later["next"], gh.at[0], live & odd)
                later["last"] = push(gh.at[0], gh.at[1], behind, live & odd)
            else:
                take(later["far"], gh.at[1], live & odd)
                take(later["last"], gh.at[1], live & even)
            value = jnp.where(live, gh[k - 1].astype(F32), 0.0)
        for h in range(rows):
            fbuf[h + 1, 0:cols, :] = value[h * cols : (h + 1) * cols]
        take(rims[k][0], ge_in.at[k, 0], live & (s > 0))
        take(rims[k][1], ge_in.at[k, 1], live & (s + 1 < S))
        left = jnp.where(live & (s > 0), ge_in[k, 0].astype(F32), 0.0)
        right = jnp.where(live & (s < S - 1), ge_in[k, 1].astype(F32), 0.0)
        for h in range(rows):
            fbuf[h, pitch - 1 : pitch, :] = left[h : h + 1]
            fbuf[h + 1, cols : cols + 1, :] = right[h : h + 1]
        f = fbuf[...].reshape(flat_all, chans)
        for c, w in enumerate((pltpu.roll(f, flat_all - 1, 0), f, pltpu.roll(f, 1, 0))):
            gown[k, :, c * chans : (c + 1) * chans] = w.astype(BF16)

    counted = [0]

    def input_grad(a, b):
        if counted[0] == 0:
            load.wait()
        total = None if counted[0] == 0 else tot[...]
        for c in range(3):
            term = lax.dot_general(
                gown[2 - a, (2 - b) * pitch : (2 - b) * pitch + flat, c * chans : (c + 1) * chans],
                wbuf[a, b, c], (((1,), (1,)), ((), ())), preferred_element_type=F32,
            )
            total = term if total is None else total + term
        counted[0] += 1
        if counted[0] < 9:
            tot[...] = total
        else:
            gi_ref[0] = total.reshape(rows, pitch, chans)[:, 0:cols, :].astype(BF16)

    tasks = tree_plan(starts, streams) if tree else plan(bits, sizes, orders, starts, ce * 2)
    for task in tasks:
        if task[0] == "taps":
            taps(*task[1:])
        elif task[0] == "arrive":
            arrive(*task[1:])
        elif task[0] == "tree":
            tree_event(*task[1:])
        elif task[0] == "gown":
            put_gown(task[1])
        else:
            input_grad(*task[1:])
    if tree:
        tree_end()

    for copy in copies:
        copy.wait_send()
    for copy, ok in sent:
        if ok is None:
            copy.wait_send()
        else:
            pl.when(ok)(copy.wait_send)
    for which in range(2):
        pltpu.make_async_copy(st_in.at[which], st_in.at[which], st_send.at[which]).wait()


def solution(mesh):
    T, S = mesh.shape["tm"], mesh.shape["space"]

    def shards(conv_input, conv_out, kernel, gain, bias, cotangent):
        _, rows, cols, chans = conv_out.shape
        width = cols * S
        ce = chans // S
        bits = T.bit_length() - 1
        groups = round_up(27 * chans, T * 16) // (T * 16)
        streams = min(STREAMS, groups)
        sizes = [(groups // streams + (p < groups % streams)) * T * 16 for p in range(streams)]
        total_rows = sum(sizes)
        pitch = round_up(cols + 2, 16)
        depth = round_up(rows * width, 128)
        fx_rows = (depth + width - 1) // width
        fg_rows = max(rows + 2, (2 * width + depth + width - 1) // width)
        n_bulk = (S - 1) * 2 + 2 * S + 5 + 6
        tree = T == 4 * LINE
        halving, line = ((1, 1, 1), (streams, 6)) if tree else ((2, streams, bits), (1, 1))
        vmem = pl.BlockSpec(memory_space=pltpu.VMEM)
        hbm = pl.BlockSpec(memory_space=pltpu.HBM)
        gi, gk, gg, gb = pl.pallas_call(
            functools.partial(body, T, S, sizes),
            out_shape=(
                pltpu.VMEM(conv_input.shape, BF16),
                pltpu.VMEM((total_rows, ce), BF16),
                pltpu.VMEM((1, chans), F32),
                pltpu.VMEM((1, chans), F32),
            ),
            in_specs=[hbm, hbm, hbm, vmem, vmem, hbm],
            out_specs=(vmem, vmem, vmem, vmem),
            scratch_shapes=[
                pltpu.VMEM(conv_input.shape, BF16),
                pltpu.VMEM((3, S, rows * cols, chans), BF16),
                pltpu.VMEM(conv_out.shape, BF16),
                pltpu.VMEM(cotangent.shape, BF16),
                pltpu.VMEM((S, 2, rows * cols, ce), BF16),
                pltpu.VMEM((S, 2, rows * cols, ce), BF16),
                pltpu.VMEM((2, 2 * chans // 128, 128), F32),
                pltpu.VMEM((2, T * S - 1, 2 * chans // 128, 128), F32),
                pltpu.VMEM((2, rows, cols, chans), F32),
                pltpu.VMEM((S, 2, rows * cols, ce), F32),
                pltpu.VMEM((fx_rows, width, chans), F32),
                pltpu.VMEM((fg_rows, width, ce), F32),
                pltpu.VMEM((rows + 2, pitch, chans), F32),
                pltpu.VMEM((rows * cols, chans), F32),
                pltpu.VMEM((rows * cols, chans), BF16),
                pltpu.VMEM((rows * cols, chans), BF16),
                pltpu.VMEM((2, rows * cols, chans), BF16),
                pltpu.VMEM((2, rows, chans), BF16),
                pltpu.VMEM((3, 2, rows, chans), BF16),
                pltpu.VMEM((3, (rows + 2) * pitch, 3 * chans), BF16),
                pltpu.VMEM((3, depth, 3 * ce), BF16),
                pltpu.VMEM((3, chans, depth), BF16),
                pltpu.VMEM((3, 3, 3, chans, chans), BF16),
                pltpu.VMEM((rows * pitch, chans), F32),
                pltpu.VMEM((total_rows, ce), F32),
                pltpu.VMEM((total_rows, ce), BF16),
                pltpu.VMEM((total_rows, ce), BF16),
                pltpu.VMEM((total_rows // 8, ce), BF16),
                pltpu.SemaphoreType.DMA((4,)),
                pltpu.SemaphoreType.DMA,
                pltpu.SemaphoreType.DMA((2,)),
                pltpu.SemaphoreType.DMA((2,)),
                pltpu.SemaphoreType.DMA((n_bulk,)),
                pltpu.SemaphoreType.DMA((n_bulk,)),
                pltpu.SemaphoreType.DMA(halving),
                pltpu.SemaphoreType.DMA(halving),
                pltpu.SemaphoreType.DMA((3,)),
                pltpu.SemaphoreType.DMA(line),
            ],
            compiler_params=pltpu.CompilerParams(
                collective_id=0, has_side_effects=True, vmem_limit_bytes=60 * 1024 * 1024
            ),
        )(conv_input, conv_out, kernel, gain.reshape(1, chans), bias.reshape(1, chans), cotangent)
        gi, gk, gg, gb = pl.pallas_call(
            hand_out,
            out_shape=(
                jax.ShapeDtypeStruct(gi.shape, BF16),
                jax.ShapeDtypeStruct((27 * chans, ce), F32),
                jax.ShapeDtypeStruct((1, chans), F32),
                jax.ShapeDtypeStruct((1, chans), F32),
            ),
            in_specs=[vmem, vmem, vmem, vmem],
            out_specs=(hbm, hbm, vmem, vmem),
            scratch_shapes=[pltpu.VMEM((27 * chans, ce), F32), pltpu.SemaphoreType.DMA((PARTS + 1,))],
            compiler_params=pltpu.CompilerParams(vmem_limit_bytes=16 * 1024 * 1024),
        )(gi, gk, gg, gb)
        return gi, gk.reshape(3, 3, 3, chans, ce), gg.reshape(chans), gb.reshape(chans)

    strip = P("tm", None, "space", None)
    return jax.shard_map(
        shards,
        mesh=mesh,
        in_specs=(strip, strip, P(), P(), P(), strip),
        out_specs=(strip, P(None, None, None, None, "space"), P(), P()),
        check_vma=False,
    )
```

```python
import functools
import heapq

import jax
import jax.numpy as jnp
from jax import lax
from jax.experimental import pallas as pl
from jax.experimental.pallas import tpu as pltpu
from jax.sharding import PartitionSpec as P

GROUPS = 32
STREAMS = 13
EPSILON = 1e-06
MESH = pl.DeviceIdType.MESH
F32 = jnp.float32
BF16 = jnp.bfloat16


def round_up(value, unit):
    return (value + unit - 1) // unit * unit


def group_sum(x, width):
    lanes = x.shape[1]
    lane = lax.broadcasted_iota(jnp.int32, x.shape, 1)
    step = 1
    while step < width:
        up = pltpu.roll(x, lanes - step, 1)
        down = pltpu.roll(x, step, 1)
        x = x + jnp.where((lane // step) % 2 == 0, up, down)
        step *= 2
    return x


PARTS = 1


def hand_out(gi_in, gk_in, gg_in, gb_in, gi_out, gk_out, gg_out, gb_out, sems):
    rows = gk_out.shape[0] // PARTS
    pairs = [(gk_in.at[i * rows : (i + 1) * rows], gk_out.at[i * rows : (i + 1) * rows]) for i in range(PARTS)]
    pairs += [(gi_in, gi_out), (gg_in, gg_out), (gb_in, gb_out)]
    copies = [pltpu.make_async_copy(src, dst, sems.at[i]) for i, (src, dst) in enumerate(pairs)]
    for copy in copies:
        copy.start()
    for copy in copies:
        copy.wait()


TAPS_A = (2, 1, 0)
MATMUL = 0.36
FILLER = 0.36
ON_CHIP = (1.1, 200e3)
ON_LINK = (1.7, 46e3)
FAR = 0.75


def stage_orders(bits, streams):
    straight = list(range(bits))
    swapped = list(range(bits))
    if bits > 2:
        swapped[1], swapped[2] = swapped[2], swapped[1]
    return [swapped if p % 2 else straight for p in range(streams)]


def stream_starts(sizes, chans):
    done, begun, starts = set(), set(), []
    edges = [sum(sizes[:p]) for p in range(len(sizes) + 1)]
    for a in TAPS_A:
        for b in range(3):
            done.add(a * 3 + b)
            ready = []
            for p in range(len(sizes)):
                first, last = edges[p] // (3 * chans), (min(edges[p + 1], 27 * chans) - 1) // (3 * chans)
                if p not in begun and all(g in done for g in range(first, last + 1)):
                    begun.add(p)
                    ready.append(p)
            starts.append(((a, b), ready))
    return starts


def plan(bits, sizes, orders, starts, row_bytes):
    free = {}
    heap = []
    steps = 2 * bits

    def send(now, p, step):
        level = step if step < bits else steps - 1 - step
        rows = sizes[p] >> (level + 1)
        bit = orders[p][level]
        latency, rate = ON_CHIP if bit == 0 else ON_LINK
        time = rows * row_bytes / rate
        if bit > 2:
            latency, time = latency + FAR, 2 * time
        link = min(bit, 2)
        begin = max(now, free.get(link, 0.0))
        free[link] = begin + time
        heapq.heappush(heap, (begin + time + latency, step, p))

    matmuls = list(starts)
    fillers = [(0.0, ("gown", 0))] + [(0.0, ("input", 2, b)) for b in range(3)]
    fillers += [(7.0, ("gown", 1))] + [(0.0, ("input", 1, b)) for b in range(3)]
    fillers += [(11.0, ("gown", 2))] + [(0.0, ("input", 0, b)) for b in range(3)]
    tasks, now = [], 0.0
    while heap or matmuls or fillers:
        if heap and heap[0][0] <= now:
            _, step, p = heapq.heappop(heap)
            tasks.append(("arrive", p, step))
            now += 0.03 + 1.5e-4 * (sizes[p] >> (step + 1) if step < bits else 0)
            if step + 1 < steps:
                send(now, p, step + 1)
        elif matmuls:
            (a, b), ready = matmuls.pop(0)
            tasks.append(("taps", a, b, ready))
            now += MATMUL
            for p in ready:
                send(now, p, 0)
        elif fillers and fillers[0][0] <= now and (not heap or heap[0][0] - now >= 0.8 * FILLER):
            tasks.append(fillers.pop(0)[1])
            now += FILLER
        else:
            now = heap[0][0] if heap else fillers[0][0]
    return tasks


EVENTS = ((1.54, 0.310), (2.88, 0.710), (4.98, 0.730), (7.79, 0.730), (10.14, 0.800), (12.84, 0.840), (18.50, 0.950))
FILL_AT = (4.45, 12.45, 17.46)
FILL_STEP = 1.06
LINE = 4


def tree_plan(starts, streams):
    tasks, number = [], 0
    for i, ((a, b), ready) in enumerate(starts):
        tasks.append((i * MATMUL, ("taps", a, b, ready)))
        for p in ready:
            last = i * MATMUL
            for e, (first, step) in enumerate(EVENTS):
                last = max(last + 1e-3, first + step * number * 13 / streams)
                tasks.append((last, ("tree", p, e)))
            number += 1
    for k, a in enumerate(TAPS_A):
        tasks.append((FILL_AT[k], ("gown", k)))
        for b in range(3):
            tasks.append((FILL_AT[k] + (b + 1) * FILL_STEP, ("input", a, b)))
    return [task for _, task in sorted(tasks, key=lambda item: item[0])]


def body(
    T, S, sizes,
    x_hbm, co_hbm, k_hbm, gain_ref, bias_ref, ct_hbm,
    gi_ref, gk_out, gg_ref, gb_ref,
    gk_ref, x_ref, xw, co_ref, ct_ref, slice_out, cw, st_out, st_in, own, pre, fx, fg, fbuf,
    gflat, gs, gr, gh, ge_out, ge_in, gown, gw, xt, wbuf, tot, acc, sbuf, rbuf, zbuf,
    in_sem, w_sem, st_send, st_recv, bulk_send, bulk_recv, rs_send, rs_recv, tree_send, tree_recv,
):
    N = T * S
    total_rows = sum(sizes)
    _, rows, cols, chans = co_ref.shape
    width = cols * S
    ce = chans // S
    depth = xt.shape[2]
    pitch = fbuf.shape[1]
    flat = rows * pitch
    flat_all = (rows + 2) * pitch
    halves = chans // 128
    t = lax.axis_index("tm")
    s = lax.axis_index("space")
    me = t * S + s

    loads = [
        pltpu.make_async_copy(src, dst, in_sem.at[i])
        for i, (src, dst) in enumerate(((co_hbm, co_ref), (ct_hbm, ct_ref), (x_hbm, x_ref)))
    ]
    for copy in loads:
        copy.start()

    barrier = pltpu.get_barrier_semaphore()

    strips = S.bit_length() - 1
    spans = N.bit_length() - 1 - strips
    flip_s = [(1 - 2 * lax.rem(s // 2**k, 2)) * 2**k for k in range(strips)]
    flip_t = [(1 - 2 * lax.rem(t // 2**k, 2)) * 2**k for k in range(spans)]

    def others():
        for r in range(N - 1, 0, -1):
            to_s = sum((flip for k, flip in enumerate(flip_s) if r >> k & 1), s)
            to_t = sum((flip for k, flip in enumerate(flip_t) if r >> (k + strips) & 1), t)
            yield r, (to_t, to_s)

    def each_other(act):
        if N <= 64:
            for r, to in others():
                act(r, to)
        else:
            def step(r, carry):
                r = N - r
                to_s = sum((lax.rem(r // 2**k, 2) * flip for k, flip in enumerate(flip_s)), s)
                to_t = sum((lax.rem(r // 2 ** (k + strips), 2) * flip for k, flip in enumerate(flip_t)), t)
                act(r, (to_t, to_s))
                return carry

            lax.fori_loop(1, N, step, 0)

    each_other(lambda r, to: pl.semaphore_signal(barrier, inc=1, device_id=to, device_id_type=MESH))

    loads[0].wait()
    load = pltpu.make_async_copy(k_hbm, wbuf, w_sem)
    load.start()
    conv = co_ref[0].astype(F32)
    first = jnp.sum(jnp.sum(conv, axis=0), axis=0, keepdims=True)
    second = jnp.sum(jnp.sum(conv * conv, axis=0), axis=0, keepdims=True)

    def put_stats(which, one, two):
        for i in range(halves):
            st_out[which, i : i + 1, :] = one[:, i * 128 : (i + 1) * 128]
            st_out[which, halves + i : halves + i + 1, :] = two[:, i * 128 : (i + 1) * 128]

    def send_stats(which):
        each_other(lambda r, to: pltpu.make_async_remote_copy(
            src_ref=st_out.at[which], dst_ref=st_in.at[which, r - 1],
            send_sem=st_send.at[which], recv_sem=st_recv.at[which],
            device_id=to, device_id_type=MESH,
        ).start())

    def take_stats(which):
        pltpu.make_async_copy(st_in.at[which], st_in.at[which], st_recv.at[which]).wait()
        return jnp.sum(st_in[which], axis=0) + st_out[which]

    put_stats(0, first, second)
    pl.semaphore_wait(barrier, N - 1)
    send_stats(0)
    loads[1].wait()
    loads[2].wait()

    sent = []

    def push(src, dst, device, ok=None, now=None):
        i = len(sent)
        copy = pltpu.make_async_remote_copy(
            src_ref=src, dst_ref=dst, send_sem=bulk_send.at[i], recv_sem=bulk_recv.at[i],
            device_id=device, device_id_type=MESH,
        )
        if ok is None:
            copy.start()
        else:
            pl.when(ok if now is None else now)(copy.start)
        sent.append((copy, ok))
        return i

    def take(i, dst, ok=None):
        copy = pltpu.make_async_copy(dst, dst, bulk_recv.at[i])
        if ok is None:
            copy.wait()
        else:
            pl.when(ok)(copy.wait)

    def frame(n):
        return lax.rem(t + T + n, T)

    def strip(n):
        return lax.rem(s + S + n, S)

    ahead = (frame(1), s)
    behind = (frame(-1), s)
    has_next, has_before = t + 1 < T, t > 0
    cut, mate, past = [], [], [[], []]
    def pack(ref):
        for h in range(rows):
            gflat[h * cols : (h + 1) * cols, :] = ref[0, h].astype(F32)
        return gflat[...].astype(BF16)

    xw[0, s] = pack(x_ref)
    past[0].append(push(xw.at[0, s], xw.at[1, s], ahead, has_next))
    for r in range(1, S):
        mate.append(push(xw.at[0, s], xw.at[0, s], (t, strip(-r))))
    for arr, ref in ((0, co_ref), (1, ct_ref)):
        whole = pack(ref)
        for j in range(S):
            slice_out[j, arr] = whole[:, j * ce : (j + 1) * ce]
    keep = pltpu.make_async_copy(slice_out.at[s], cw.at[s], in_sem.at[3])
    keep.start()
    for r in range(1, S):
        cut.append(push(slice_out.at[strip(-r)], cw.at[s], (t, strip(-r))))

    odd = lax.rem(t, 2) == 1
    even = lax.rem(t, 2) == 0

    def relay_near(r):
        take(mate[r - 1], xw.at[0, strip(r)])
        past[0].append(push(xw.at[0, strip(r)], xw.at[1, strip(r)], ahead, has_next))

    def relay_far(r, when):
        take(past[0][r], xw.at[1, strip(r)], has_before & when)
        ok = has_next & has_before
        if r < len(past[1]):
            pl.when(ok & when)(sent[past[1][r]][0].start)
        else:
            past[1].append(push(xw.at[1, strip(r)], xw.at[2, strip(r)], ahead, ok, ok & when))

    fx[...] = jnp.zeros_like(fx)
    fg[...] = jnp.zeros_like(fg)
    fbuf[...] = jnp.zeros_like(fbuf)
    if total_rows > 27 * chans:
        acc[27 * chans :, :] = jnp.zeros((total_rows - 27 * chans, ce), F32)

    gain = gain_ref[...]
    bias = bias_ref[...]
    group = chans // GROUPS
    count = rows * width * T * group
    relay_far(0, odd)
    relay_far(0, even)
    sums = take_stats(0)
    grouped = group_sum(sums, group)
    mean2 = grouped[:halves] / count
    inv2 = lax.rsqrt(grouped[halves:] / count - mean2 * mean2 + EPSILON)

    def wide(two):
        return jnp.concatenate([two[i : i + 1] for i in range(halves)], axis=1)

    mean, inv = wide(mean2), wide(inv2)

    def shift_grad(conv, cot, mean, inv, gain, bias):
        normed = (conv.astype(F32) - mean) * inv
        shifted = normed * gain + bias
        sigma = jax.nn.sigmoid(shifted)
        return normed, cot.astype(F32) * sigma * (1.0 + shifted * (1.0 - sigma))

    normed, grad = shift_grad(co_ref[0], ct_ref[0], mean, inv, gain, bias)
    own[0] = normed
    own[1] = grad
    put_stats(
        1,
        jnp.sum(jnp.sum(grad, axis=0), axis=0, keepdims=True),
        jnp.sum(jnp.sum(grad * normed, axis=0), axis=0, keepdims=True),
    )
    send_stats(1)

    def part(v):
        out = v[..., 0:ce]
        for j in range(1, S):
            out = jnp.where(s == j, v[..., j * ce : (j + 1) * ce], out)
        return out

    for r in range(1, S):
        relay_near(r)
    for r in range(1, S):
        relay_far(r, odd)
    for r in range(1, S):
        take(cut[r - 1], cw.at[strip(r)])
    keep.wait()
    firsts = tuple(part(p) for p in (mean, inv, gain, bias))
    for j in range(S):
        normed, grad = shift_grad(cw[j, 0], cw[j, 1], *firsts)
        pre[j, 0] = normed
        pre[j, 1] = grad

    def put_input(k):
        for j in range(S):
            value = xw[k, j].astype(F32)
            if k > 0:
                value = jnp.where(t >= k, value, 0.0)
            for h in range(rows):
                fx[h, j * cols : (j + 1) * cols, :] = value[h * cols : (h + 1) * cols]
        placed = fx[...].reshape(fx.shape[0] * fx.shape[1], chans)[0:depth]
        xt[k] = jnp.transpose(placed).astype(BF16)

    put_input(0)
    for r in range(1, S):
        relay_far(r, even)
    put_input(1)
    sums = take_stats(1)
    chan_bias, chan_gain = wide(sums[:halves]), wide(sums[halves:])
    gb_ref[...] = chan_bias
    gg_ref[...] = chan_gain
    gain2 = jnp.concatenate([gain[:, i * 128 : (i + 1) * 128] for i in range(halves)], axis=0)
    plain = wide(group_sum(sums[:halves] * gain2, group)) / count
    product = wide(group_sum(sums[halves:] * gain2, group)) / count

    def conv_grad(normed, grad, inv, gain, plain, product):
        return inv * (grad * gain - plain - normed * product)

    g = conv_grad(own[0], own[1], inv, gain, plain, product)
    for h in range(rows):
        gflat[h * cols : (h + 1) * cols, :] = g[h]
    gs[...] = gflat[...].astype(BF16)
    for h in range(rows):
        ge_out[0, h : h + 1, :] = g[h, 0:1, :].astype(BF16)
        ge_out[1, h : h + 1, :] = g[h, cols - 1 : cols, :].astype(BF16)
    second = (frame(-2), s)
    later = {
        "pair": push(gs, gr, ahead, even),
        "near": push(gs, gh.at[0], behind, odd),
        "far": push(gs, gh.at[1], second, odd & (t > 1)),
    }
    rims = []
    for k in range(3):
        back = (frame(-k), strip(1)), (frame(-k), strip(-1))
        rims.append((
            push(ge_out.at[1], ge_in.at[k, 0], back[0], (t >= k) & (s + 1 < S)),
            push(ge_out.at[0], ge_in.at[k, 1], back[1], (t >= k) & (s > 0)),
        ))

    seconds = tuple(part(p) for p in (inv, gain, plain, product))
    for j in range(S):
        value = conv_grad(pre[j, 0], pre[j, 1], *seconds)
        for h in range(rows):
            fg[h + 1, j * cols : (j + 1) * cols, :] = value[h * cols : (h + 1) * cols]
    tall = fg.shape[0] * width
    f = fg[...].reshape(tall, ce)
    column = lax.broadcasted_iota(jnp.int32, fg.shape, 1).reshape(tall, ce)
    moved = (
        jnp.where(column < width - 1, pltpu.roll(f, tall - 1, 0), 0.0),
        f,
        jnp.where(column > 0, pltpu.roll(f, 1, 0), 0.0),
    )
    for c, w in enumerate(moved):
        for b in range(3):
            gw[b, :, c * ce : (c + 1) * ce] = w[(2 - b) * width : (2 - b) * width + depth].astype(BF16)

    bits = T.bit_length() - 1
    streams = len(sizes)
    orders = stage_orders(bits, streams)
    starts = stream_starts(sizes, chans)
    bases = [sum(sizes[:p]) for p in range(streams)]
    offs = [0] * streams
    flying = [None] * streams
    copies = []

    def side(bit):
        return lax.rem(t // (2**bit), 2)

    def partner(bit):
        return (t + (1 - 2 * side(bit)) * 2**bit, s)

    def span(p, off, n):
        return pl.ds(pl.multiple_of(bases[p] + off, 16), n)

    def start_of(p, i):
        return bases[p] + sizes[p] - (sizes[p] >> i)

    def launch(i, p):
        half = sizes[p] >> (i + 1)
        start = start_of(p, i)
        copy = pltpu.make_async_remote_copy(
            src_ref=sbuf.at[start : start + half], dst_ref=rbuf.at[start : start + half],
            send_sem=rs_send.at[0, p, i], recv_sem=rs_recv.at[0, p, i],
            device_id=partner(orders[p][i]), device_id_type=MESH,
        )
        copy.start()
        copies.append(copy)
        flying[p] = copy

    tree = T == 4 * LINE
    z, x, core = t // 4, lax.rem(t // 2, 2), lax.rem(t, 2)
    side_z = z // 2
    inner = (z == 1) | (z == 2)
    outer = (z == 0) | (z == 3)
    toward = jnp.where(inner, z - 1 + 2 * side_z, z + 1 - 2 * side_z)
    mates = {
        "core": (t + 1 - 2 * core, s),
        "x": (t + 2 - 4 * x, s),
        "line": (toward * 4 + lax.rem(t, 4), s),
        "middle": (lax.rem(3 - z + T, T) * 4 + lax.rem(t, 4), s),
    }
    slots = {"c0": 0, "x1": 0, "x0": 1, "a1": 1, "a2a": 1, "z0": 2, "z1": 3, "a2b": 3}

    def tree_push(p, kind, src, dst, device):
        by_role = kind in ("z0", "z1", "a1", "a2a", "a2b")
        pltpu.make_async_remote_copy(
            src_ref=src, dst_ref=dst, send_sem=tree_send.at[int(by_role)],
            recv_sem=tree_send.at[2] if kind == "c1" else tree_recv.at[p, slots[kind]],
            device_id=device, device_id_type=MESH,
        ).start()

    def tree_wait(p, kind, ref):
        pltpu.make_async_copy(ref, ref, tree_recv.at[p, slots[kind]]).wait()

    def places(p):
        half, n, h = sizes[p] // 2, sizes[p] // 4, sizes[p] // 8
        mine = core * half + x * n
        apart = core * half + (1 - x) * n
        return half, n, h, mine, apart

    def rows_of(ref, p, off, n):
        return ref.at[span(p, off, n)]

    def widen(p, off, n):
        at = span(p, off, n)
        gk_out[at, :] = gk_ref[at, :].astype(F32)

    def tree_event(p, e):
        half, n, h, mine, apart = places(p)
        base = bases[p]
        near, far = mine + side_z * h, mine + (1 - side_z) * h
        at_x, at_z = half, half + n
        zrow = pl.ds(base // 8, h)

        def taken(ref, off, rows):
            return ref[span(p, off, rows), :]

        def put_half(kind, off, device):
            tree_push(p, kind, rows_of(gk_ref, p, off, h), rows_of(gk_ref, p, off, h), device)

        def put_whole(kind, off):
            tree_push(p, kind, rows_of(gk_ref, p, off, n), rows_of(gk_ref, p, off, n), mates["core"])

        if e == 0:
            tree_wait(p, "c0", rows_of(rbuf, p, 0, half))
            value = taken(acc, apart, n) + taken(rbuf, (1 - x) * n, n).astype(F32)
            sbuf[span(p, at_x, n), :] = value.astype(BF16)
            tree_push(p, "x0", rows_of(sbuf, p, at_x, n), rows_of(rbuf, p, at_x, n), mates["x"])
            acc[span(p, mine, n), :] = taken(acc, mine, n) + taken(rbuf, x * n, n).astype(F32)
        elif e == 1:
            tree_wait(p, "x0", rows_of(rbuf, p, at_x, n))

            @pl.when(outer)
            def _():
                value = taken(acc, mine, n) + taken(rbuf, at_x, n).astype(F32)
                sbuf[span(p, at_z, n), :] = value.astype(BF16)
                tree_push(p, "z0", rows_of(sbuf, p, at_z, n), rows_of(rbuf, p, at_z, n), mates["line"])

            @pl.when(inner)
            def _():
                acc[span(p, mine, n), :] = taken(acc, mine, n) + taken(rbuf, at_x, n).astype(F32)
        elif e == 2:
            @pl.when(inner)
            def _():
                tree_wait(p, "z0", rows_of(rbuf, p, at_z, n))
                value = taken(acc, far, h) + taken(rbuf, at_z + (1 - side_z) * h, h).astype(F32)
                sbuf[span(p, at_z, h), :] = value.astype(BF16)
                tree_push(p, "z1", rows_of(sbuf, p, at_z, h), zbuf.at[zrow], mates["middle"])
                acc[span(p, near, h), :] = taken(acc, near, h) + taken(rbuf, at_z + side_z * h, h).astype(F32)
        elif e == 3:
            @pl.when(inner)
            def _():
                tree_wait(p, "z1", zbuf.at[zrow])
                gk_ref[span(p, near, h), :] = (taken(acc, near, h) + zbuf[zrow, :].astype(F32)).astype(BF16)
                put_half("x1", near, mates["x"])
                put_half("a1", near, mates["middle"])
                put_half("a2a", near, mates["line"])
        elif e == 4:
            @pl.when(inner)
            def _():
                tree_wait(p, "a1", rows_of(gk_ref, p, far, h))
                put_half("x1", far, mates["x"])
                put_half("a2b", far, mates["line"])
                put_whole("c1", mine)

            @pl.when(outer)
            def _():
                tree_wait(p, "a2a", rows_of(gk_ref, p, near, h))
                put_half("x1", near, mates["x"])
        elif e == 5:
            @pl.when(outer)
            def _():
                tree_wait(p, "a2b", rows_of(gk_ref, p, far, h))
                put_half("x1", far, mates["x"])
                put_whole("c1", mine)
        else:
            tree_wait(p, "x1", rows_of(gk_ref, p, apart, n))
            put_whole("c1", apart)
            widen(p, core * half, half)

    def tree_end():
        for ref, i in ((gk_ref.at[0 : total_rows // 2], 2), (acc.at[0 : total_rows * 3 // 4], 0)):
            pltpu.make_async_copy(ref, ref, tree_send.at[i]).wait()
        for p in range(streams):
            widen(p, (1 - core) * (sizes[p] // 2), sizes[p] // 2)

        @pl.when(outer)
        def _():
            pltpu.make_async_copy(sbuf.at[0 : total_rows // 4], sbuf.at[0 : total_rows // 4], tree_send.at[1]).wait()

        @pl.when(inner)
        def _():
            pltpu.make_async_copy(sbuf.at[0 : total_rows // 2], sbuf.at[0 : total_rows // 2], tree_send.at[1]).wait()

    def begin(p):
        half = sizes[p] >> 1
        mine = side(orders[p][0])
        start = start_of(p, 0)
        sbuf[start : start + half, :] = acc[span(p, (1 - mine) * half, half), :].astype(BF16)
        if tree:
            tree_push(p, "c0", sbuf.at[start : start + half], rbuf.at[start : start + half], mates["core"])
            return
        launch(0, p)
        offs[p] = mine * half

    def sum_at(p, i, off, n):
        at = span(p, offs[p] + off, n)
        seen = pl.ds(pl.multiple_of(start_of(p, i) + off, 16), n)
        return at, acc[at, :] + rbuf[seen, :].astype(F32)

    def spread(i, p):
        n = sizes[p] >> (i + 1)
        bit = orders[p][i]
        at = span(p, offs[p], n)
        copy = pltpu.make_async_remote_copy(
            src_ref=gk_ref.at[at], dst_ref=gk_ref.at[at],
            send_sem=rs_send.at[1, p, i], recv_sem=rs_recv.at[1, p, i],
            device_id=partner(bit), device_id_type=MESH,
        )
        copy.start()
        copies.append(copy)
        offs[p] = offs[p] - side(bit) * n
        flying[p] = copy

    def arrive(p, step):
        flying[p].wait_recv()
        if step < bits - 1:
            half = sizes[p] >> (step + 2)
            mine = side(orders[p][step + 1])
            start = start_of(p, step + 1)
            _, value = sum_at(p, step, (1 - mine) * half, half)
            sbuf[start : start + half, :] = value.astype(BF16)
            launch(step + 1, p)
            at, value = sum_at(p, step, mine * half, half)
            acc[at, :] = value
            offs[p] = offs[p] + mine * half
        elif step == bits - 1:
            at, value = sum_at(p, step, 0, sizes[p] >> bits)
            gk_ref[at, :] = value.astype(BF16)
            spread(bits - 1, p)
        elif step + 1 < 2 * bits:
            spread(2 * bits - 2 - step, p)

    def taps(a, b, ready):
        if a == TAPS_A[-1] and b == 0:
            for r in range(S):
                take(past[1][r], xw.at[2, strip(r)], t > 1)
            put_input(2)
        res = jnp.dot(xt[2 - a], gw[b], preferred_element_type=F32)
        for c in range(3):
            at = ((a * 3 + b) * 3 + c) * chans
            acc[at : at + chans, :] = res[:, c * ce : (c + 1) * ce]
        for p in ready:
            begin(p)
        if (a, b) == (TAPS_A[0], 2):
            take(later["pair"], gr, odd)
            later["next"] = push(gr, gh.at[0], second, odd & (t > 1))

    def put_gown(k):
        live = t + k < T
        if k == 0:
            value = gs[...].astype(F32)
        else:
            if k == 1:
                take(later["near"], gh.at[0], live & even)
                take(later["next"], gh.at[0], live & odd)
                later["last"] = push(gh.at[0], gh.at[1], behind, live & odd)
            else:
                take(later["far"], gh.at[1], live & odd)
                take(later["last"], gh.at[1], live & even)
            value = jnp.where(live, gh[k - 1].astype(F32), 0.0)
        for h in range(rows):
            fbuf[h + 1, 0:cols, :] = value[h * cols : (h + 1) * cols]
        take(rims[k][0], ge_in.at[k, 0], live & (s > 0))
        take(rims[k][1], ge_in.at[k, 1], live & (s + 1 < S))
        left = jnp.where(live & (s > 0), ge_in[k, 0].astype(F32), 0.0)
        right = jnp.where(live & (s < S - 1), ge_in[k, 1].astype(F32), 0.0)
        for h in range(rows):
            fbuf[h, pitch - 1 : pitch, :] = left[h : h + 1]
            fbuf[h + 1, cols : cols + 1, :] = right[h : h + 1]
        f = fbuf[...].reshape(flat_all, chans)
        for c, w in enumerate((pltpu.roll(f, flat_all - 1, 0), f, pltpu.roll(f, 1, 0))):
            gown[k, :, c * chans : (c + 1) * chans] = w.astype(BF16)

    counted = [0]

    def input_grad(a, b):
        if counted[0] == 0:
            load.wait()
        total = None if counted[0] == 0 else tot[...]
        for c in range(3):
            term = lax.dot_general(
                gown[2 - a, (2 - b) * pitch : (2 - b) * pitch + flat, c * chans : (c + 1) * chans],
                wbuf[a, b, c], (((1,), (1,)), ((), ())), preferred_element_type=F32,
            )
            total = term if total is None else total + term
        counted[0] += 1
        if counted[0] < 9:
            tot[...] = total
        else:
            gi_ref[0] = total.reshape(rows, pitch, chans)[:, 0:cols, :].astype(BF16)

    tasks = tree_plan(starts, streams) if tree else plan(bits, sizes, orders, starts, ce * 2)
    for task in tasks:
        if task[0] == "taps":
            taps(*task[1:])
        elif task[0] == "arrive":
            arrive(*task[1:])
        elif task[0] == "tree":
            tree_event(*task[1:])
        elif task[0] == "gown":
            put_gown(task[1])
        else:
            input_grad(*task[1:])
    if tree:
        tree_end()
    else:
        gk_out[...] = gk_ref[...].astype(F32)

    for copy in copies:
        copy.wait_send()
    for copy, ok in sent:
        if ok is None:
            copy.wait_send()
        else:
            pl.when(ok)(copy.wait_send)
    for which in range(2):
        pltpu.make_async_copy(st_in.at[which], st_in.at[which], st_send.at[which]).wait()


def solution(mesh):
    T, S = mesh.shape["tm"], mesh.shape["space"]

    def shards(conv_input, conv_out, kernel, gain, bias, cotangent):
        _, rows, cols, chans = conv_out.shape
        width = cols * S
        ce = chans // S
        bits = T.bit_length() - 1
        groups = round_up(27 * chans, T * 16) // (T * 16)
        streams = min(STREAMS, groups)
        sizes = [(groups // streams + (p < groups % streams)) * T * 16 for p in range(streams)]
        total_rows = sum(sizes)
        pitch = round_up(cols + 2, 16)
        depth = round_up(rows * width, 128)
        fx_rows = (depth + width - 1) // width
        fg_rows = max(rows + 2, (2 * width + depth + width - 1) // width)
        n_bulk = (S - 1) * 2 + 2 * S + 5 + 6
        tree = T == 4 * LINE
        halving, line = ((1, 1, 1), (streams, 4)) if tree else ((2, streams, bits), (1, 1))
        vmem = pl.BlockSpec(memory_space=pltpu.VMEM)
        hbm = pl.BlockSpec(memory_space=pltpu.HBM)
        gi, gk, gg, gb = pl.pallas_call(
            functools.partial(body, T, S, sizes),
            out_shape=(
                pltpu.VMEM(conv_input.shape, BF16),
                pltpu.VMEM((total_rows, ce), F32),
                pltpu.VMEM((1, chans), F32),
                pltpu.VMEM((1, chans), F32),
            ),
            in_specs=[hbm, hbm, hbm, vmem, vmem, hbm],
            out_specs=(vmem, vmem, vmem, vmem),
            scratch_shapes=[
                pltpu.VMEM((total_rows, ce), BF16),
                pltpu.VMEM(conv_input.shape, BF16),
                pltpu.VMEM((3, S, rows * cols, chans), BF16),
                pltpu.VMEM(conv_out.shape, BF16),
                pltpu.VMEM(cotangent.shape, BF16),
                pltpu.VMEM((S, 2, rows * cols, ce), BF16),
                pltpu.VMEM((S, 2, rows * cols, ce), BF16),
                pltpu.VMEM((2, 2 * chans // 128, 128), F32),
                pltpu.VMEM((2, T * S - 1, 2 * chans // 128, 128), F32),
                pltpu.VMEM((2, rows, cols, chans), F32),
                pltpu.VMEM((S, 2, rows * cols, ce), F32),
                pltpu.VMEM((fx_rows, width, chans), F32),
                pltpu.VMEM((fg_rows, width, ce), F32),
                pltpu.VMEM((rows + 2, pitch, chans), F32),
                pltpu.VMEM((rows * cols, chans), F32),
                pltpu.VMEM((rows * cols, chans), BF16),
                pltpu.VMEM((rows * cols, chans), BF16),
                pltpu.VMEM((2, rows * cols, chans), BF16),
                pltpu.VMEM((2, rows, chans), BF16),
                pltpu.VMEM((3, 2, rows, chans), BF16),
                pltpu.VMEM((3, (rows + 2) * pitch, 3 * chans), BF16),
                pltpu.VMEM((3, depth, 3 * ce), BF16),
                pltpu.VMEM((3, chans, depth), BF16),
                pltpu.VMEM((3, 3, 3, chans, chans), BF16),
                pltpu.VMEM((rows * pitch, chans), F32),
                pltpu.VMEM((total_rows, ce), F32),
                pltpu.VMEM((total_rows, ce), BF16),
                pltpu.VMEM((total_rows, ce), BF16),
                pltpu.VMEM((total_rows // 8, ce), BF16),
                pltpu.SemaphoreType.DMA((4,)),
                pltpu.SemaphoreType.DMA,
                pltpu.SemaphoreType.DMA((2,)),
                pltpu.SemaphoreType.DMA((2,)),
                pltpu.SemaphoreType.DMA((n_bulk,)),
                pltpu.SemaphoreType.DMA((n_bulk,)),
                pltpu.SemaphoreType.DMA(halving),
                pltpu.SemaphoreType.DMA(halving),
                pltpu.SemaphoreType.DMA((3,)),
                pltpu.SemaphoreType.DMA(line),
            ],
            compiler_params=pltpu.CompilerParams(
                collective_id=0, has_side_effects=True, vmem_limit_bytes=60 * 1024 * 1024
            ),
        )(conv_input, conv_out, kernel, gain.reshape(1, chans), bias.reshape(1, chans), cotangent)
        gi, gk, gg, gb = pl.pallas_call(
            hand_out,
            out_shape=(
                jax.ShapeDtypeStruct(gi.shape, BF16),
                jax.ShapeDtypeStruct((27 * chans, ce), F32),
                jax.ShapeDtypeStruct((1, chans), F32),
                jax.ShapeDtypeStruct((1, chans), F32),
            ),
            in_specs=[vmem, vmem, vmem, vmem],
            out_specs=(hbm, hbm, hbm, hbm),
            scratch_shapes=[pltpu.SemaphoreType.DMA((PARTS + 3,))],
            compiler_params=pltpu.CompilerParams(vmem_limit_bytes=16 * 1024 * 1024),
        )(gi, gk, gg, gb)
        return gi, gk.reshape(3, 3, 3, chans, ce), gg.reshape(chans), gb.reshape(chans)

    strip = P("tm", None, "space", None)
    return jax.shard_map(
        shards,
        mesh=mesh,
        in_specs=(strip, strip, P(), P(), P(), strip),
        out_specs=(strip, P(None, None, None, None, "space"), P(), P()),
        check_vma=False,
    )
```

```python
import functools
import heapq

import jax
import jax.numpy as jnp
from jax import lax
from jax.experimental import pallas as pl
from jax.experimental.pallas import tpu as pltpu
from jax.sharding import PartitionSpec as P

GROUPS = 32
STREAMS = 13
EPSILON = 1e-06
MESH = pl.DeviceIdType.MESH
F32 = jnp.float32
BF16 = jnp.bfloat16


def round_up(value, unit):
    return (value + unit - 1) // unit * unit


def group_sum(x, width):
    lanes = x.shape[1]
    lane = lax.broadcasted_iota(jnp.int32, x.shape, 1)
    step = 1
    while step < width:
        up = pltpu.roll(x, lanes - step, 1)
        down = pltpu.roll(x, step, 1)
        x = x + jnp.where((lane // step) % 2 == 0, up, down)
        step *= 2
    return x


PARTS = 1


def hand_out(gi_in, gk_in, gg_in, gb_in, gi_out, gk_out, gg_out, gb_out, sems):
    rows = gk_out.shape[0] // PARTS
    pairs = [(gk_in.at[i * rows : (i + 1) * rows], gk_out.at[i * rows : (i + 1) * rows]) for i in range(PARTS)]
    pairs += [(gi_in, gi_out), (gg_in, gg_out), (gb_in, gb_out)]
    copies = [pltpu.make_async_copy(src, dst, sems.at[i]) for i, (src, dst) in enumerate(pairs)]
    for copy in copies:
        copy.start()
    for copy in copies:
        copy.wait()


TAPS_A = (2, 1, 0)
MATMUL = 0.36
FILLER = 0.36
ON_CHIP = (1.1, 200e3)
ON_LINK = (1.7, 46e3)
FAR = 0.75


def stage_orders(bits, streams):
    straight = list(range(bits))
    swapped = list(range(bits))
    if bits > 2:
        swapped[1], swapped[2] = swapped[2], swapped[1]
    return [swapped if p % 2 else straight for p in range(streams)]


def stream_starts(sizes, chans):
    done, begun, starts = set(), set(), []
    edges = [sum(sizes[:p]) for p in range(len(sizes) + 1)]
    for a in TAPS_A:
        for b in range(3):
            done.add(a * 3 + b)
            ready = []
            for p in range(len(sizes)):
                first, last = edges[p] // (3 * chans), (min(edges[p + 1], 27 * chans) - 1) // (3 * chans)
                if p not in begun and all(g in done for g in range(first, last + 1)):
                    begun.add(p)
                    ready.append(p)
            starts.append(((a, b), ready))
    return starts


def plan(bits, sizes, orders, starts, row_bytes):
    free = {}
    heap = []
    steps = 2 * bits

    def send(now, p, step):
        level = step if step < bits else steps - 1 - step
        rows = sizes[p] >> (level + 1)
        bit = orders[p][level]
        latency, rate = ON_CHIP if bit == 0 else ON_LINK
        time = rows * row_bytes / rate
        if bit > 2:
            latency, time = latency + FAR, 2 * time
        link = min(bit, 2)
        begin = max(now, free.get(link, 0.0))
        free[link] = begin + time
        heapq.heappush(heap, (begin + time + latency, step, p))

    matmuls = list(starts)
    fillers = [(0.0, ("gown", 0))] + [(0.0, ("input", 2, b)) for b in range(3)]
    fillers += [(7.0, ("gown", 1))] + [(0.0, ("input", 1, b)) for b in range(3)]
    fillers += [(11.0, ("gown", 2))] + [(0.0, ("input", 0, b)) for b in range(3)]
    tasks, now = [], 0.0
    while heap or matmuls or fillers:
        if heap and heap[0][0] <= now:
            _, step, p = heapq.heappop(heap)
            tasks.append(("arrive", p, step))
            now += 0.03 + 1.5e-4 * (sizes[p] >> (step + 1) if step < bits else 0)
            if step + 1 < steps:
                send(now, p, step + 1)
        elif matmuls:
            (a, b), ready = matmuls.pop(0)
            tasks.append(("taps", a, b, ready))
            now += MATMUL
            for p in ready:
                send(now, p, 0)
        elif fillers and fillers[0][0] <= now and (not heap or heap[0][0] - now >= 0.8 * FILLER):
            tasks.append(fillers.pop(0)[1])
            now += FILLER
        else:
            now = heap[0][0] if heap else fillers[0][0]
    return tasks


EVENTS = ((1.54, 0.310), (2.88, 0.710), (4.98, 0.730), (7.79, 0.730), (10.14, 0.800), (12.84, 0.840), (18.50, 0.950))
FILL_AT = (4.45, 12.45, 17.46)
FILL_STEP = 1.06
LINE = 4


def tree_plan(starts, streams):
    tasks, number = [], 0
    for i, ((a, b), ready) in enumerate(starts):
        tasks.append((i * MATMUL, ("taps", a, b, ready)))
        for p in ready:
            last = i * MATMUL
            for e, (first, step) in enumerate(EVENTS):
                last = max(last + 1e-3, first + step * number * 13 / streams)
                tasks.append((last, ("tree", p, e)))
            number += 1
    for k, a in enumerate(TAPS_A):
        tasks.append((FILL_AT[k], ("gown", k)))
        for b in range(3):
            tasks.append((FILL_AT[k] + (b + 1) * FILL_STEP, ("input", a, b)))
    return [task for _, task in sorted(tasks, key=lambda item: item[0])]


def body(
    T, S, sizes,
    x_hbm, co_hbm, k_hbm, gain_ref, bias_ref, ct_hbm,
    gi_ref, gk_out, gg_ref, gb_ref,
    gk_ref, x_ref, xw, co_ref, ct_ref, slice_out, cw, st_out, st_in, own, pre, fx, fg, fbuf,
    gflat, gs, gh, ge_out, ge_in, gown, gw, xt, wbuf, tot, acc, sbuf, rbuf, zbuf,
    in_sem, w_sem, st_send, st_recv, bulk_send, bulk_recv, rs_send, rs_recv, tree_send, tree_recv,
):
    N = T * S
    total_rows = sum(sizes)
    _, rows, cols, chans = co_ref.shape
    width = cols * S
    ce = chans // S
    depth = xt.shape[2]
    pitch = fbuf.shape[1]
    flat = rows * pitch
    flat_all = (rows + 2) * pitch
    halves = chans // 128
    t = lax.axis_index("tm")
    s = lax.axis_index("space")
    me = t * S + s

    loads = [
        pltpu.make_async_copy(src, dst, in_sem.at[i])
        for i, (src, dst) in enumerate(((co_hbm, co_ref), (ct_hbm, ct_ref), (x_hbm, x_ref)))
    ]
    for copy in loads:
        copy.start()

    barrier = pltpu.get_barrier_semaphore()

    strips = S.bit_length() - 1
    spans = N.bit_length() - 1 - strips
    flip_s = [(1 - 2 * lax.rem(s // 2**k, 2)) * 2**k for k in range(strips)]
    flip_t = [(1 - 2 * lax.rem(t // 2**k, 2)) * 2**k for k in range(spans)]

    def others():
        for r in range(N - 1, 0, -1):
            to_s = sum((flip for k, flip in enumerate(flip_s) if r >> k & 1), s)
            to_t = sum((flip for k, flip in enumerate(flip_t) if r >> (k + strips) & 1), t)
            yield r, (to_t, to_s)

    def each_other(act):
        if N <= 64:
            for r, to in others():
                act(r, to)
        else:
            def step(r, carry):
                r = N - r
                to_s = sum((lax.rem(r // 2**k, 2) * flip for k, flip in enumerate(flip_s)), s)
                to_t = sum((lax.rem(r // 2 ** (k + strips), 2) * flip for k, flip in enumerate(flip_t)), t)
                act(r, (to_t, to_s))
                return carry

            lax.fori_loop(1, N, step, 0)

    each_other(lambda r, to: pl.semaphore_signal(barrier, inc=1, device_id=to, device_id_type=MESH))

    loads[0].wait()
    load = pltpu.make_async_copy(k_hbm, wbuf, w_sem)
    load.start()
    conv = co_ref[0].astype(F32)
    first = jnp.sum(jnp.sum(conv, axis=0), axis=0, keepdims=True)
    second = jnp.sum(jnp.sum(conv * conv, axis=0), axis=0, keepdims=True)

    def put_stats(which, one, two):
        for i in range(halves):
            st_out[which, i : i + 1, :] = one[:, i * 128 : (i + 1) * 128]
            st_out[which, halves + i : halves + i + 1, :] = two[:, i * 128 : (i + 1) * 128]

    def send_stats(which):
        each_other(lambda r, to: pltpu.make_async_remote_copy(
            src_ref=st_out.at[which], dst_ref=st_in.at[which, r - 1],
            send_sem=st_send.at[which], recv_sem=st_recv.at[which],
            device_id=to, device_id_type=MESH,
        ).start())

    def take_stats(which):
        pltpu.make_async_copy(st_in.at[which], st_in.at[which], st_recv.at[which]).wait()
        return jnp.sum(st_in[which], axis=0) + st_out[which]

    put_stats(0, first, second)
    pl.semaphore_wait(barrier, N - 1)
    send_stats(0)
    loads[1].wait()
    loads[2].wait()

    sent = []

    def push(src, dst, device, ok=None, now=None):
        i = len(sent)
        copy = pltpu.make_async_remote_copy(
            src_ref=src, dst_ref=dst, send_sem=bulk_send.at[i], recv_sem=bulk_recv.at[i],
            device_id=device, device_id_type=MESH,
        )
        if ok is None:
            copy.start()
        else:
            pl.when(ok if now is None else now)(copy.start)
        sent.append((copy, ok))
        return i

    def take(i, dst, ok=None):
        copy = pltpu.make_async_copy(dst, dst, bulk_recv.at[i])
        if ok is None:
            copy.wait()
        else:
            pl.when(ok)(copy.wait)

    def frame(n):
        return lax.rem(t + T + n, T)

    def strip(n):
        return lax.rem(s + S + n, S)

    ahead = (frame(1), s)
    behind = (frame(-1), s)
    has_next, has_before = t + 1 < T, t > 0
    cut, mate, past = [], [], [[], []]
    def pack(ref):
        for h in range(rows):
            gflat[h * cols : (h + 1) * cols, :] = ref[0, h].astype(F32)
        return gflat[...].astype(BF16)

    xw[0, s] = pack(x_ref)
    past[0].append(push(xw.at[0, s], xw.at[1, s], ahead, has_next))
    for r in range(1, S):
        mate.append(push(xw.at[0, s], xw.at[0, s], (t, strip(-r))))
    for arr, ref in ((0, co_ref), (1, ct_ref)):
        whole = pack(ref)
        for j in range(S):
            slice_out[j, arr] = whole[:, j * ce : (j + 1) * ce]
    keep = pltpu.make_async_copy(slice_out.at[s], cw.at[s], in_sem.at[3])
    keep.start()
    for r in range(1, S):
        cut.append(push(slice_out.at[strip(-r)], cw.at[s], (t, strip(-r))))

    odd = lax.rem(t, 2) == 1
    even = lax.rem(t, 2) == 0

    def relay_near(r):
        take(mate[r - 1], xw.at[0, strip(r)])
        past[0].append(push(xw.at[0, strip(r)], xw.at[1, strip(r)], ahead, has_next))

    def relay_far(r, when):
        take(past[0][r], xw.at[1, strip(r)], has_before & when)
        ok = has_next & has_before
        if r < len(past[1]):
            pl.when(ok & when)(sent[past[1][r]][0].start)
        else:
            past[1].append(push(xw.at[1, strip(r)], xw.at[2, strip(r)], ahead, ok, ok & when))

    fx[...] = jnp.zeros_like(fx)
    fg[...] = jnp.zeros_like(fg)
    fbuf[...] = jnp.zeros_like(fbuf)
    if total_rows > 27 * chans:
        acc[27 * chans :, :] = jnp.zeros((total_rows - 27 * chans, ce), F32)

    gain = gain_ref[...]
    bias = bias_ref[...]
    group = chans // GROUPS
    count = rows * width * T * group
    relay_far(0, odd)
    relay_far(0, even)
    sums = take_stats(0)
    grouped = group_sum(sums, group)
    mean2 = grouped[:halves] / count
    inv2 = lax.rsqrt(grouped[halves:] / count - mean2 * mean2 + EPSILON)

    def wide(two):
        return jnp.concatenate([two[i : i + 1] for i in range(halves)], axis=1)

    mean, inv = wide(mean2), wide(inv2)

    def shift_grad(conv, cot, mean, inv, gain, bias):
        normed = (conv.astype(F32) - mean) * inv
        shifted = normed * gain + bias
        sigma = jax.nn.sigmoid(shifted)
        return normed, cot.astype(F32) * sigma * (1.0 + shifted * (1.0 - sigma))

    normed, grad = shift_grad(co_ref[0], ct_ref[0], mean, inv, gain, bias)
    own[0] = normed
    own[1] = grad
    put_stats(
        1,
        jnp.sum(jnp.sum(grad, axis=0), axis=0, keepdims=True),
        jnp.sum(jnp.sum(grad * normed, axis=0), axis=0, keepdims=True),
    )
    send_stats(1)

    def part(v):
        out = v[..., 0:ce]
        for j in range(1, S):
            out = jnp.where(s == j, v[..., j * ce : (j + 1) * ce], out)
        return out

    for r in range(1, S):
        relay_near(r)
    for r in range(1, S):
        relay_far(r, odd)
    for r in range(1, S):
        take(cut[r - 1], cw.at[strip(r)])
    keep.wait()
    firsts = tuple(part(p) for p in (mean, inv, gain, bias))
    for j in range(S):
        normed, grad = shift_grad(cw[j, 0], cw[j, 1], *firsts)
        pre[j, 0] = normed
        pre[j, 1] = grad

    def put_input(k):
        for j in range(S):
            value = xw[k, j].astype(F32)
            if k > 0:
                value = jnp.where(t >= k, value, 0.0)
            for h in range(rows):
                fx[h, j * cols : (j + 1) * cols, :] = value[h * cols : (h + 1) * cols]
        placed = fx[...].reshape(fx.shape[0] * fx.shape[1], chans)[0:depth]
        xt[k] = jnp.transpose(placed).astype(BF16)

    put_input(0)
    for r in range(1, S):
        relay_far(r, even)
    put_input(1)
    sums = take_stats(1)
    chan_bias, chan_gain = wide(sums[:halves]), wide(sums[halves:])
    gb_ref[...] = chan_bias
    gg_ref[...] = chan_gain
    gain2 = jnp.concatenate([gain[:, i * 128 : (i + 1) * 128] for i in range(halves)], axis=0)
    plain = wide(group_sum(sums[:halves] * gain2, group)) / count
    product = wide(group_sum(sums[halves:] * gain2, group)) / count

    def conv_grad(normed, grad, inv, gain, plain, product):
        return inv * (grad * gain - plain - normed * product)

    g = conv_grad(own[0], own[1], inv, gain, plain, product)
    for h in range(rows):
        gflat[h * cols : (h + 1) * cols, :] = g[h]
    gs[...] = gflat[...].astype(BF16)
    for h in range(rows):
        ge_out[0, h : h + 1, :] = g[h, 0:1, :].astype(BF16)
        ge_out[1, h : h + 1, :] = g[h, cols - 1 : cols, :].astype(BF16)
    second = (frame(-2), s)
    later = {
        "near": push(gs, gh.at[0], behind, has_before),
        "far": push(gs, gh.at[1], second, odd & (t > 1)),
    }
    rims = []
    for k in range(3):
        back = (frame(-k), strip(1)), (frame(-k), strip(-1))
        rims.append((
            push(ge_out.at[1], ge_in.at[k, 0], back[0], (t >= k) & (s + 1 < S)),
            push(ge_out.at[0], ge_in.at[k, 1], back[1], (t >= k) & (s > 0)),
        ))

    seconds = tuple(part(p) for p in (inv, gain, plain, product))
    for j in range(S):
        value = conv_grad(pre[j, 0], pre[j, 1], *seconds)
        for h in range(rows):
            fg[h + 1, j * cols : (j + 1) * cols, :] = value[h * cols : (h + 1) * cols]
    tall = fg.shape[0] * width
    f = fg[...].reshape(tall, ce)
    column = lax.broadcasted_iota(jnp.int32, fg.shape, 1).reshape(tall, ce)
    moved = (
        jnp.where(column < width - 1, pltpu.roll(f, tall - 1, 0), 0.0),
        f,
        jnp.where(column > 0, pltpu.roll(f, 1, 0), 0.0),
    )
    for c, w in enumerate(moved):
        for b in range(3):
            gw[b, :, c * ce : (c + 1) * ce] = w[(2 - b) * width : (2 - b) * width + depth].astype(BF16)

    bits = T.bit_length() - 1
    streams = len(sizes)
    orders = stage_orders(bits, streams)
    starts = stream_starts(sizes, chans)
    bases = [sum(sizes[:p]) for p in range(streams)]
    offs = [0] * streams
    flying = [None] * streams
    copies = []

    def side(bit):
        return lax.rem(t // (2**bit), 2)

    def partner(bit):
        return (t + (1 - 2 * side(bit)) * 2**bit, s)

    def span(p, off, n):
        return pl.ds(pl.multiple_of(bases[p] + off, 16), n)

    def start_of(p, i):
        return bases[p] + sizes[p] - (sizes[p] >> i)

    def launch(i, p):
        half = sizes[p] >> (i + 1)
        start = start_of(p, i)
        copy = pltpu.make_async_remote_copy(
            src_ref=sbuf.at[start : start + half], dst_ref=rbuf.at[start : start + half],
            send_sem=rs_send.at[0, p, i], recv_sem=rs_recv.at[0, p, i],
            device_id=partner(orders[p][i]), device_id_type=MESH,
        )
        copy.start()
        copies.append(copy)
        flying[p] = copy

    tree = T == 4 * LINE
    z, x, core = t // 4, lax.rem(t // 2, 2), lax.rem(t, 2)
    side_z = z // 2
    inner = (z == 1) | (z == 2)
    outer = (z == 0) | (z == 3)
    toward = jnp.where(inner, z - 1 + 2 * side_z, z + 1 - 2 * side_z)
    mates = {
        "core": (t + 1 - 2 * core, s),
        "x": (t + 2 - 4 * x, s),
        "line": (toward * 4 + lax.rem(t, 4), s),
        "middle": (lax.rem(3 - z + T, T) * 4 + lax.rem(t, 4), s),
    }
    slots = {"c0": 0, "x1": 0, "x0": 1, "a1": 1, "a2a": 1, "z0": 2, "z1": 3, "a2b": 3}

    def tree_push(p, kind, src, dst, device):
        by_role = kind in ("z0", "z1", "a1", "a2a", "a2b")
        pltpu.make_async_remote_copy(
            src_ref=src, dst_ref=dst, send_sem=tree_send.at[int(by_role)],
            recv_sem=tree_send.at[2] if kind == "c1" else tree_recv.at[p, slots[kind]],
            device_id=device, device_id_type=MESH,
        ).start()

    def tree_wait(p, kind, ref):
        pltpu.make_async_copy(ref, ref, tree_recv.at[p, slots[kind]]).wait()

    def places(p):
        half, n, h = sizes[p] // 2, sizes[p] // 4, sizes[p] // 8
        mine = core * half + x * n
        apart = core * half + (1 - x) * n
        return half, n, h, mine, apart

    def rows_of(ref, p, off, n):
        return ref.at[span(p, off, n)]

    def widen(p, off, n):
        at = span(p, off, n)
        gk_out[at, :] = gk_ref[at, :].astype(F32)

    def tree_event(p, e):
        half, n, h, mine, apart = places(p)
        base = bases[p]
        near, far = mine + side_z * h, mine + (1 - side_z) * h
        at_x, at_z = half, half + n
        zrow = pl.ds(base // 8, h)

        def taken(ref, off, rows):
            return ref[span(p, off, rows), :]

        def put_half(kind, off, device):
            tree_push(p, kind, rows_of(gk_ref, p, off, h), rows_of(gk_ref, p, off, h), device)

        def put_whole(kind, off):
            tree_push(p, kind, rows_of(gk_ref, p, off, n), rows_of(gk_ref, p, off, n), mates["core"])

        if e == 0:
            tree_wait(p, "c0", rows_of(rbuf, p, 0, half))
            value = taken(acc, apart, n) + taken(rbuf, (1 - x) * n, n).astype(F32)
            sbuf[span(p, at_x, n), :] = value.astype(BF16)
            tree_push(p, "x0", rows_of(sbuf, p, at_x, n), rows_of(rbuf, p, at_x, n), mates["x"])
            acc[span(p, mine, n), :] = taken(acc, mine, n) + taken(rbuf, x * n, n).astype(F32)
        elif e == 1:
            tree_wait(p, "x0", rows_of(rbuf, p, at_x, n))

            @pl.when(outer)
            def _():
                value = taken(acc, mine, n) + taken(rbuf, at_x, n).astype(F32)
                sbuf[span(p, at_z, n), :] = value.astype(BF16)
                tree_push(p, "z0", rows_of(sbuf, p, at_z, n), rows_of(rbuf, p, at_z, n), mates["line"])

            @pl.when(inner)
            def _():
                acc[span(p, mine, n), :] = taken(acc, mine, n) + taken(rbuf, at_x, n).astype(F32)
        elif e == 2:
            @pl.when(inner)
            def _():
                tree_wait(p, "z0", rows_of(rbuf, p, at_z, n))
                value = taken(acc, far, h) + taken(rbuf, at_z + (1 - side_z) * h, h).astype(F32)
                sbuf[span(p, at_z, h), :] = value.astype(BF16)
                tree_push(p, "z1", rows_of(sbuf, p, at_z, h), zbuf.at[zrow], mates["middle"])
                acc[span(p, near, h), :] = taken(acc, near, h) + taken(rbuf, at_z + side_z * h, h).astype(F32)
        elif e == 3:
            @pl.when(inner)
            def _():
                tree_wait(p, "z1", zbuf.at[zrow])
                gk_ref[span(p, near, h), :] = (taken(acc, near, h) + zbuf[zrow, :].astype(F32)).astype(BF16)
                put_half("a1", near, mates["middle"])
                put_half("a2a", near, mates["line"])
                put_half("x1", near, mates["x"])
        elif e == 4:
            @pl.when(inner)
            def _():
                tree_wait(p, "a1", rows_of(gk_ref, p, far, h))
                put_half("x1", far, mates["x"])
                put_half("a2b", far, mates["line"])
                put_whole("c1", mine)

            @pl.when(outer)
            def _():
                tree_wait(p, "a2a", rows_of(gk_ref, p, near, h))
                put_half("x1", near, mates["x"])
        elif e == 5:
            @pl.when(outer)
            def _():
                tree_wait(p, "a2b", rows_of(gk_ref, p, far, h))
                put_half("x1", far, mates["x"])
                put_whole("c1", mine)
        else:
            tree_wait(p, "x1", rows_of(gk_ref, p, apart, n))
            put_whole("c1", apart)
            widen(p, core * half, half)

    def tree_end():
        for ref, i in ((gk_ref.at[0 : total_rows // 2], 2), (acc.at[0 : total_rows * 3 // 4], 0)):
            pltpu.make_async_copy(ref, ref, tree_send.at[i]).wait()
        for p in range(streams):
            widen(p, (1 - core) * (sizes[p] // 2), sizes[p] // 2)

        @pl.when(outer)
        def _():
            pltpu.make_async_copy(sbuf.at[0 : total_rows // 4], sbuf.at[0 : total_rows // 4], tree_send.at[1]).wait()

        @pl.when(inner)
        def _():
            pltpu.make_async_copy(sbuf.at[0 : total_rows // 2], sbuf.at[0 : total_rows // 2], tree_send.at[1]).wait()

    def begin(p):
        half = sizes[p] >> 1
        mine = side(orders[p][0])
        start = start_of(p, 0)
        sbuf[start : start + half, :] = acc[span(p, (1 - mine) * half, half), :].astype(BF16)
        if tree:
            tree_push(p, "c0", sbuf.at[start : start + half], rbuf.at[start : start + half], mates["core"])
            return
        launch(0, p)
        offs[p] = mine * half

    def sum_at(p, i, off, n):
        at = span(p, offs[p] + off, n)
        seen = pl.ds(pl.multiple_of(start_of(p, i) + off, 16), n)
        return at, acc[at, :] + rbuf[seen, :].astype(F32)

    def spread(i, p):
        n = sizes[p] >> (i + 1)
        bit = orders[p][i]
        at = span(p, offs[p], n)
        copy = pltpu.make_async_remote_copy(
            src_ref=gk_ref.at[at], dst_ref=gk_ref.at[at],
            send_sem=rs_send.at[1, p, i], recv_sem=rs_recv.at[1, p, i],
            device_id=partner(bit), device_id_type=MESH,
        )
        copy.start()
        copies.append(copy)
        offs[p] = offs[p] - side(bit) * n
        flying[p] = copy

    def arrive(p, step):
        flying[p].wait_recv()
        if step < bits - 1:
            half = sizes[p] >> (step + 2)
            mine = side(orders[p][step + 1])
            start = start_of(p, step + 1)
            _, value = sum_at(p, step, (1 - mine) * half, half)
            sbuf[start : start + half, :] = value.astype(BF16)
            launch(step + 1, p)
            at, value = sum_at(p, step, mine * half, half)
            acc[at, :] = value
            offs[p] = offs[p] + mine * half
        elif step == bits - 1:
            at, value = sum_at(p, step, 0, sizes[p] >> bits)
            gk_ref[at, :] = value.astype(BF16)
            spread(bits - 1, p)
        elif step + 1 < 2 * bits:
            spread(2 * bits - 2 - step, p)

    def taps(a, b, ready):
        if a == TAPS_A[-1] and b == 0:
            for r in range(S):
                take(past[1][r], xw.at[2, strip(r)], t > 1)
            put_input(2)
        res = jnp.dot(xt[2 - a], gw[b], preferred_element_type=F32)
        for c in range(3):
            at = ((a * 3 + b) * 3 + c) * chans
            acc[at : at + chans, :] = res[:, c * ce : (c + 1) * ce]
        for p in ready:
            begin(p)

    def put_gown(k):
        live = t + k < T
        if k == 0:
            value = gs[...].astype(F32)
        else:
            if k == 1:
                take(later["near"], gh.at[0], live)
                later["last"] = push(gh.at[0], gh.at[1], behind, live & odd)
            else:
                take(later["far"], gh.at[1], live & odd)
                take(later["last"], gh.at[1], live & even)
            value = jnp.where(live, gh[k - 1].astype(F32), 0.0)
        for h in range(rows):
            fbuf[h + 1, 0:cols, :] = value[h * cols : (h + 1) * cols]
        take(rims[k][0], ge_in.at[k, 0], live & (s > 0))
        take(rims[k][1], ge_in.at[k, 1], live & (s + 1 < S))
        left = jnp.where(live & (s > 0), ge_in[k, 0].astype(F32), 0.0)
        right = jnp.where(live & (s < S - 1), ge_in[k, 1].astype(F32), 0.0)
        for h in range(rows):
            fbuf[h, pitch - 1 : pitch, :] = left[h : h + 1]
            fbuf[h + 1, cols : cols + 1, :] = right[h : h + 1]
        f = fbuf[...].reshape(flat_all, chans)
        for c, w in enumerate((pltpu.roll(f, flat_all - 1, 0), f, pltpu.roll(f, 1, 0))):
            gown[k, :, c * chans : (c + 1) * chans] = w.astype(BF16)

    counted = [0]

    def input_grad(a, b):
        if counted[0] == 0:
            load.wait()
        total = None if counted[0] == 0 else tot[...]
        for c in range(3):
            term = lax.dot_general(
                gown[2 - a, (2 - b) * pitch : (2 - b) * pitch + flat, c * chans : (c + 1) * chans],
                wbuf[a, b, c], (((1,), (1,)), ((), ())), preferred_element_type=F32,
            )
            total = term if total is None else total + term
        counted[0] += 1
        if counted[0] < 9:
            tot[...] = total
        else:
            gi_ref[0] = total.reshape(rows, pitch, chans)[:, 0:cols, :].astype(BF16)

    tasks = tree_plan(starts, streams) if tree else plan(bits, sizes, orders, starts, ce * 2)
    for task in tasks:
        if task[0] == "taps":
            taps(*task[1:])
        elif task[0] == "arrive":
            arrive(*task[1:])
        elif task[0] == "tree":
            tree_event(*task[1:])
        elif task[0] == "gown":
            put_gown(task[1])
        else:
            input_grad(*task[1:])
    if tree:
        tree_end()
    else:
        gk_out[...] = gk_ref[...].astype(F32)

    for copy in copies:
        copy.wait_send()
    for copy, ok in sent:
        if ok is None:
            copy.wait_send()
        else:
            pl.when(ok)(copy.wait_send)
    for which in range(2):
        pltpu.make_async_copy(st_in.at[which], st_in.at[which], st_send.at[which]).wait()


def solution(mesh):
    T, S = mesh.shape["tm"], mesh.shape["space"]

    def shards(conv_input, conv_out, kernel, gain, bias, cotangent):
        _, rows, cols, chans = conv_out.shape
        width = cols * S
        ce = chans // S
        bits = T.bit_length() - 1
        groups = round_up(27 * chans, T * 16) // (T * 16)
        streams = min(STREAMS, groups)
        sizes = [(groups // streams + (p < groups % streams)) * T * 16 for p in range(streams)]
        total_rows = sum(sizes)
        pitch = round_up(cols + 2, 16)
        depth = round_up(rows * width, 128)
        fx_rows = (depth + width - 1) // width
        fg_rows = max(rows + 2, (2 * width + depth + width - 1) // width)
        n_bulk = (S - 1) * 2 + 2 * S + 3 + 6
        tree = T == 4 * LINE
        halving, line = ((1, 1, 1), (streams, 4)) if tree else ((2, streams, bits), (1, 1))
        vmem = pl.BlockSpec(memory_space=pltpu.VMEM)
        hbm = pl.BlockSpec(memory_space=pltpu.HBM)
        gi, gk, gg, gb = pl.pallas_call(
            functools.partial(body, T, S, sizes),
            out_shape=(
                pltpu.VMEM(conv_input.shape, BF16),
                pltpu.VMEM((total_rows, ce), F32),
                pltpu.VMEM((1, chans), F32),
                pltpu.VMEM((1, chans), F32),
            ),
            in_specs=[hbm, hbm, hbm, vmem, vmem, hbm],
            out_specs=(vmem, vmem, vmem, vmem),
            scratch_shapes=[
                pltpu.VMEM((total_rows, ce), BF16),
                pltpu.VMEM(conv_input.shape, BF16),
                pltpu.VMEM((3, S, rows * cols, chans), BF16),
                pltpu.VMEM(conv_out.shape, BF16),
                pltpu.VMEM(cotangent.shape, BF16),
                pltpu.VMEM((S, 2, rows * cols, ce), BF16),
                pltpu.VMEM((S, 2, rows * cols, ce), BF16),
                pltpu.VMEM((2, 2 * chans // 128, 128), F32),
                pltpu.VMEM((2, T * S - 1, 2 * chans // 128, 128), F32),
                pltpu.VMEM((2, rows, cols, chans), F32),
                pltpu.VMEM((S, 2, rows * cols, ce), F32),
                pltpu.VMEM((fx_rows, width, chans), F32),
                pltpu.VMEM((fg_rows, width, ce), F32),
                pltpu.VMEM((rows + 2, pitch, chans), F32),
                pltpu.VMEM((rows * cols, chans), F32),
                pltpu.VMEM((rows * cols, chans), BF16),
                pltpu.VMEM((2, rows * cols, chans), BF16),
                pltpu.VMEM((2, rows, chans), BF16),
                pltpu.VMEM((3, 2, rows, chans), BF16),
                pltpu.VMEM((3, (rows + 2) * pitch, 3 * chans), BF16),
                pltpu.VMEM((3, depth, 3 * ce), BF16),
                pltpu.VMEM((3, chans, depth), BF16),
                pltpu.VMEM((3, 3, 3, chans, chans), BF16),
                pltpu.VMEM((rows * pitch, chans), F32),
                pltpu.VMEM((total_rows, ce), F32),
                pltpu.VMEM((total_rows, ce), BF16),
                pltpu.VMEM((total_rows, ce), BF16),
                pltpu.VMEM((total_rows // 8, ce), BF16),
                pltpu.SemaphoreType.DMA((4,)),
                pltpu.SemaphoreType.DMA,
                pltpu.SemaphoreType.DMA((2,)),
                pltpu.SemaphoreType.DMA((2,)),
                pltpu.SemaphoreType.DMA((n_bulk,)),
                pltpu.SemaphoreType.DMA((n_bulk,)),
                pltpu.SemaphoreType.DMA(halving),
                pltpu.SemaphoreType.DMA(halving),
                pltpu.SemaphoreType.DMA((3,)),
                pltpu.SemaphoreType.DMA(line),
            ],
            compiler_params=pltpu.CompilerParams(
                collective_id=0, has_side_effects=True, vmem_limit_bytes=60 * 1024 * 1024
            ),
        )(conv_input, conv_out, kernel, gain.reshape(1, chans), bias.reshape(1, chans), cotangent)
        gi, gk, gg, gb = pl.pallas_call(
            hand_out,
            out_shape=(
                jax.ShapeDtypeStruct(gi.shape, BF16),
                jax.ShapeDtypeStruct((27 * chans, ce), F32),
                jax.ShapeDtypeStruct((1, chans), F32),
                jax.ShapeDtypeStruct((1, chans), F32),
            ),
            in_specs=[vmem, vmem, vmem, vmem],
            out_specs=(hbm, hbm, hbm, hbm),
            scratch_shapes=[pltpu.SemaphoreType.DMA((PARTS + 3,))],
            compiler_params=pltpu.CompilerParams(vmem_limit_bytes=16 * 1024 * 1024),
        )(gi, gk, gg, gb)
        return gi, gk.reshape(3, 3, 3, chans, ce), gg.reshape(chans), gb.reshape(chans)

    strip = P("tm", None, "space", None)
    return jax.shard_map(
        shards,
        mesh=mesh,
        in_specs=(strip, strip, P(), P(), P(), strip),
        out_specs=(strip, P(None, None, None, None, "space"), P(), P()),
        check_vma=False,
    )
```
